256 devices in a mesh: star: 64 (over y, z_lo, x, core), gas: 4 (over z_hi).
Axes of the slice: x: 4, y: 4, z: 8 (z_hi: 4, z_lo: 2; z = z_hi * 2 + z_lo), core: 2. Of those that a mesh axis runs over, the one named last changes fastest.
Arguments:
- star_pos: float32 [3, 131072], P(None, ('star', 'gas')), may hold values from 0 to 32
- star_vel: float32 [3, 131072], P(None, ('star', 'gas')), may hold values from -6 to 6
- star_accel: float32 [6, 131072], P(None, ('star', 'gas')), may hold values from -6 to 6
- star_mass: float32 [131072], P(('star', 'gas')), may hold values from 0.1 to 2
- active: int32 [2048], replicated, may hold values from 0 to 131071, as said below
- density: float32 [256, 32, 64], P('star', 'gas'), may hold values from 0.5 to 4
- flow_in: float32 [3, 256, 32, 64], P(None, 'star', 'gas'), may hold values from -2 to 2
- field_in: float32 [3, 256, 32, 64], P(None, 'star', 'gas'), may hold values from -4 to 4
Outputs:
- star_new: float32 [12, 131072], P(None, ('star', 'gas'))
- flow: float32 [3, 256, 32, 64], P(None, 'star', 'gas')
- field_out: float32 [3, 256, 32, 64], P(None, 'star', 'gas')
The draws below stay inside these ranges and needn't reach their ends.
Inputs may be any that keep to these rules, and one draw needn't show every extreme that they name: Distinct and increasing; among the 512 consecutive indices of one device at most 24 are active, and in every draw some device holds exactly 24.
All inputs are finite; a program needn't handle non-finite values.
Results may differ from the reference program's by a relative error of at most 0.0001.
Values sent between devices are 32-bit elements; how exact they have to be, the bound alone decides.
A program may use at most 64 MiB of HBM per device.

```python
import math
import jax
import jax.numpy as jnp
from jax import lax

STAR_DEV = 512
ACT_DEV = 8
STARS = 131072
ACTIVE = 2048
NX = 256
NY = 32
NZ = 64


def draw_active(key, part):
    owners = STARS // STAR_DEV
    groups = owners // 4
    key_a, key_b, key_c, key_d = jax.random.split(jax.random.fold_in(key, 17), 4)
    shift_one = jax.random.randint(key_a, (groups,), 0, ACT_DEV + 1)
    shift_two = jax.random.randint(key_b, (groups,), 0, ACT_DEV // 2 + 1)
    shift_two = jnp.where(jnp.arange(groups) == 0, 0, shift_two)
    pattern = jnp.stack([3 * ACT_DEV - shift_two, shift_one, ACT_DEV - shift_one, shift_two], 1).reshape(-1)
    order = jax.random.permutation(key_c, owners)
    counts_at = pattern[order].astype(jnp.int32)
    owner_keys = jax.random.split(key_d, owners)
    ranks = jax.vmap(lambda one_key: jax.random.permutation(one_key, STAR_DEV))(owner_keys)
    chosen = (ranks < counts_at[:, None]).reshape(-1)
    return jnp.nonzero(chosen, size=ACTIVE, fill_value=0)[0].astype(jnp.int32)


def steps_of(stream_key, dims, cuts, low, top_value):
    factor_of = 1.0
    for axis_at, parts in cuts:
        heights = jax.random.uniform(jax.random.fold_in(jax.random.fold_in(stream_key, 6), axis_at), (parts,), jnp.float32, low / len(cuts), top_value / len(cuts))
        factor_of = factor_of * jnp.repeat(jnp.exp(heights), dims[axis_at] // parts).reshape((-1,) + (1,) * (len(dims) - 1 - axis_at))
    return factor_of


def gaussian(own_key, shape, width, limit, shards=(), held_as=jnp.bfloat16):
    gain = steps_of(own_key, shape, shards, -0.22, 0.18) if shards else 1.0
    entries = jax.random.normal(own_key, shape, jnp.float32) * width * gain
    return jnp.minimum(jnp.maximum(entries, -limit), limit).astype(held_as)


def setup_inputs(seed: int = 0) -> dict:
    key_of = jax.random.split(jax.random.key(seed), 9)
    star_pos = jnp.clip(32.0 * jax.random.uniform(key_of[0], (3, STARS), jnp.float32) ** steps_of(key_of[0], (3, STARS), ((1, 256),), -0.2, 0.2), 0.0, 32.0)
    star_vel = gaussian(key_of[1], (3, STARS), 1.0, 6.0, ((1, 256),), jnp.float32)
    star_accel = gaussian(key_of[2], (6, STARS), 1.0, 6.0, ((1, 256),), jnp.float32)
    star_mass = jnp.clip(jnp.exp(math.log(2.0) - 2.9957323 * jax.random.uniform(key_of[3], (STARS,), jnp.float32) ** steps_of(key_of[3], (STARS,), ((0, 256),), -0.2, 0.2)), 0.1, 2.0)
    active = draw_active(jax.random.fold_in(key_of[8], 71), 0)
    density = jnp.clip(jnp.exp(math.log(4.0) - 2.0794415 * jax.random.uniform(key_of[5], (NX, NY, NZ), jnp.float32) ** steps_of(key_of[5], (NX, NY, NZ), ((0, 64), (1, 4)), -0.2, 0.2)), 0.5, 4.0)
    flow_in = gaussian(key_of[6], (3, NX, NY, NZ), 0.3, 2.0, ((1, 64), (2, 4)), jnp.float32)
    field_in = gaussian(key_of[7], (3, NX, NY, NZ), 0.7, 4.0, ((1, 64), (2, 4)), jnp.float32)
    return {"star_pos": star_pos, "star_vel": star_vel, "star_accel": star_accel, "star_mass": star_mass, "active": active, "density": density, "flow_in": flow_in, "field_in": field_in}


gravity = 0.02
soften = 4.0
time_step = 1.5
field_step = 0.1

def grad_x(values):
    return 0.5 * (values[2:, 1:-1] - values[:-2, 1:-1])

def grad_y(values):
    return 0.5 * (values[1:-1, 2:] - values[1:-1, :-2])

def grad_z(values):
    return 0.5 * (jnp.roll(values, -1, 2) - jnp.roll(values, 1, 2))[1:-1, 1:-1]

def trim_rim(values):
    return values[1:-1, 1:-1]

def curl_of(comp_a, comp_b, comp_c):
    return (grad_y(comp_c) - grad_z(comp_b), grad_z(comp_a) - grad_x(comp_c), grad_x(comp_b) - grad_y(comp_a))

def cross_of(lhs_vec, rhs_vec):
    return (lhs_vec[1] * rhs_vec[2] - lhs_vec[2] * rhs_vec[1], lhs_vec[2] * rhs_vec[0] - lhs_vec[0] * rhs_vec[2], lhs_vec[0] * rhs_vec[1] - lhs_vec[1] * rhs_vec[0])

def field_rate(padded_field, padded_flow, padded_density):
    current = curl_of(padded_field[0], padded_field[1], padded_field[2])
    inner_field = (trim_rim(padded_field[0]), trim_rim(padded_field[1]), trim_rim(padded_field[2]))
    inner_flow = (trim_rim(padded_flow[0]), trim_rim(padded_flow[1]), trim_rim(padded_flow[2]))
    resist = trim_rim(padded_density) ** (-1.5)
    lorentz = cross_of(current, inner_field)
    drift = cross_of(lorentz, inner_field)
    motion = cross_of(inner_flow, inner_field)
    emf_a = motion[0] + resist * drift[0]
    emf_b = motion[1] + resist * drift[1]
    emf_c = motion[2] + resist * drift[2]
    return jnp.stack(curl_of(emf_a, emf_b, emf_c))

def wrap_pad(values):
    widths = ((0, 0),) * (values.ndim - 3) + ((2, 2), (2, 2), (0, 0))
    return jnp.pad(values, widths, mode='wrap')

def star_terms(target, resident):
    star_gap = resident[0:3, None, :] - target[0:3, :, None]
    rel_vel = resident[3:6, None, :] - target[3:6, :, None]
    inv_r = lax.rsqrt(lax.optimization_barrier(jnp.sum(star_gap * star_gap, 0)) + soften)
    weight = gravity * resident[6][None, :] * inv_r * inv_r * inv_r
    star_acc = lax.optimization_barrier(jnp.sum(weight[None] * star_gap, 2))
    approach = lax.optimization_barrier(jnp.sum(star_gap * rel_vel, 0))
    star_jerk = lax.optimization_barrier(jnp.sum(weight[None] * (rel_vel - 3.0 * (approach * inv_r * inv_r)[None] * star_gap), 2))
    return jnp.concatenate([star_acc, star_jerk], 0)

def gas_terms(target, cell_place, cell_mass):
    cell_gap = cell_place[:, None, :] - target[0:3, :, None]
    inv_g = lax.rsqrt(lax.optimization_barrier(jnp.sum(cell_gap * cell_gap, 0)) + soften)
    inv_cube = gravity * inv_g * inv_g * inv_g
    gas_acc = lax.optimization_barrier(jnp.sum((inv_cube * cell_mass[None, :])[None] * cell_gap, 2))
    cell_kick = -lax.optimization_barrier(jnp.sum((inv_cube * target[6][:, None])[None] * cell_gap, 1))
    return (gas_acc, cell_kick)

def reference(star_pos, star_vel, star_accel, star_mass, active, density, flow_in, field_in):
    old_acc = star_accel[0:3]
    old_jerk = star_accel[3:6]
    pred_pos = star_pos + time_step * star_vel + time_step ** 2 / 2.0 * old_acc + time_step ** 3 / 6.0 * old_jerk
    pred_vel = star_vel + time_step * old_acc + time_step ** 2 / 2.0 * old_jerk
    resident = jnp.concatenate([pred_pos, pred_vel, star_mass[None]], 0)
    targets = jnp.take(resident, active, axis=1)
    star_blocks = targets.reshape(7, ACTIVE // 64, 64).transpose(1, 0, 2)
    star_part = lax.map(lambda target_block: star_terms(target_block, resident), star_blocks)
    star_part = star_part.transpose(1, 0, 2).reshape(6, ACTIVE)
    grid_shape = (NX, NY, NZ)
    coord_x = jnp.arange(NX).astype(jnp.float32) + 0.5
    coord_y = jnp.arange(NY).astype(jnp.float32) + 0.5
    coord_z = jnp.arange(NZ).astype(jnp.float32) + 0.5
    cell_place = jnp.stack([jnp.broadcast_to(coord_x[:, None, None], grid_shape), jnp.broadcast_to(coord_y[None, :, None], grid_shape), jnp.broadcast_to(coord_z[None, None, :], grid_shape)]).reshape(3, -1)
    cell_mass = density.reshape(-1)
    gas_blocks = targets.reshape(7, ACTIVE // 16, 16).transpose(1, 0, 2)

    def one_block(running, target_block):
        gas_acc, cell_kick = gas_terms(target_block, cell_place, cell_mass)
        return (running + cell_kick, gas_acc)
    kick_sum, gas_part = lax.scan(one_block, jnp.zeros(cell_place.shape, jnp.float32), gas_blocks)
    gas_part = gas_part.transpose(1, 0, 2).reshape(3, ACTIVE)
    new_acc = star_part[0:3] + gas_part
    new_jerk = star_part[3:6]
    acc_zero = jnp.take(old_acc, active, axis=1)
    jerk_zero = jnp.take(old_jerk, active, axis=1)
    vel_zero = jnp.take(star_vel, active, axis=1)
    pos_zero = jnp.take(star_pos, active, axis=1)
    vel_one = vel_zero + time_step * (acc_zero + new_acc) / 2.0 + time_step ** 2 * (jerk_zero - new_jerk) / 12.0
    pos_one = pos_zero + time_step * (vel_zero + vel_one) / 2.0 + time_step ** 2 * (acc_zero - new_acc) / 12.0
    updated = jnp.concatenate([pos_one, vel_one, new_acc, new_jerk], 0)
    base = jnp.concatenate([star_pos, star_vel, star_accel], 0)
    star_new = base.at[:, active].set(updated)
    flow = flow_in + time_step * kick_sum.reshape(3, NX, NY, NZ)
    padded_flow = wrap_pad(flow)
    padded_density = wrap_pad(density)
    first_section = field_in + field_step * field_rate(wrap_pad(field_in), padded_flow, padded_density)
    field_out = 0.5 * (field_in + first_section + field_step * field_rate(wrap_pad(first_section), padded_flow, padded_density))
    return (star_new, flow, field_out)
```

```python
import functools

import jax
import jax.numpy as jnp
from jax import lax
from jax.experimental import pallas as pl
from jax.experimental.pallas import tpu as pltpu
from jax.sharding import PartitionSpec as P

MESH = pl.DeviceIdType.MESH
gravity = 0.02
soften = 4.0
time_step = 1.5
field_step = 0.1

STARS = 512
ACTIVE = 2048
BLOCKS = ACTIVE // 128
XC, ZL, YN, GAS = 8, 2, 4, 4
TILES = YN * ZL * XC
SLOTS = 32
MOST = 24
NXL, NYL, NZ = 4, 8, 64
COLS = NXL * NYL
f32 = jnp.float32
i32 = jnp.int32


def lanes(shape=(8, 128)):
    return lax.broadcasted_iota(i32, shape, len(shape) - 1)


def take_lanes(values, index):
    return jnp.take_along_axis(values, index, axis=1, mode="promise_in_bounds")


def place():
    star = lax.axis_index("star")
    gas = lax.axis_index("gas")
    xc = lax.rem(star, XC)
    zl = lax.rem(lax.div(star, XC), ZL)
    y = lax.div(star, XC * ZL)
    return star, gas, y, zl, xc


def star_of(y, zl, xc):
    return (y * ZL + zl) * XC + xc


def z_peers(y, zl, xc, gas):
    zi = zl * GAS + gas
    peers = []
    for d in range(1, ZL * GAS):
        other = lax.rem(zi + d, ZL * GAS)
        ozl, ogas = lax.div(other, GAS), lax.rem(other, GAS)
        peers.append((other, ozl, (star_of(y, ozl, xc), ogas)))
    return zi, peers


def y_peers(y, zl, xc, gas):
    peers = []
    for d in range(1, YN):
        other = lax.rem(y + d, YN)
        peers.append((other, (star_of(other, zl, xc), gas)))
    return peers


def xc_peers(y, zl, xc, gas):
    peers = []
    for d in range(1, XC):
        other = lax.rem(xc + d, XC)
        peers.append((other, (star_of(y, zl, other), gas)))
    return peers


def meet(devices):
    barrier = pltpu.get_barrier_semaphore()
    for device in devices:
        pl.semaphore_signal(barrier, inc=1, device_id=device, device_id_type=MESH)
    return lambda: pl.semaphore_wait(barrier, len(devices))


def send(src, dst, send_sem, recv_sem, device):
    copy = pltpu.make_async_remote_copy(
        src_ref=src, dst_ref=dst, send_sem=send_sem, recv_sem=recv_sem,
        device_id=device, device_id_type=MESH,
    )
    copy.start()
    return copy


def own_indices(active_ref, rank, lane0):
    act = active_ref[...]
    base = rank * STARS
    begin = jnp.sum((act < base).astype(f32)).astype(i32)
    slot = lanes() - lane0
    t = begin + slot
    inside = (slot >= 0) & (slot < SLOTS) & (t < ACTIVE)
    t = jnp.where(inside, t, 0)
    block, lane = t >> 7, t & 127
    found = jnp.full((8, 128), -1, i32)
    for b in range(BLOCKS):
        row = jnp.broadcast_to(active_ref[b : b + 1, :], (8, 128))
        found = jnp.where(block == b, take_lanes(row, lane), found)
    local = found - base
    used = inside & (local >= 0) & (local < STARS)
    return jnp.where(used, local, -1), used


def gather_kernel(
    pos, vel, accel, mass, active, tiles, res, begins, zbuf, own, zs, zr, ys, yr, xs, xr
):
    star, gas, y, zl, xc = place()
    zi, zp = z_peers(y, zl, xc, gas)
    yp = y_peers(y, zl, xc, gas)
    xp = xc_peers(y, zl, xc, gas)
    arrived = meet([p[-1] for p in zp] + [p[-1] for p in yp] + [p[-1] for p in xp])
    old_acc, old_jerk = accel[0:3, :], accel[3:6, :]
    v = vel[...]
    res[0:3, :] = (
        pos[...] + time_step * v + time_step**2 / 2.0 * old_acc + time_step**3 / 6.0 * old_jerk
    )
    res[3:6, :] = v + time_step * old_acc + time_step**2 / 2.0 * old_jerk
    res[6:7, :] = mass[...]
    res[7:8, :] = jnp.zeros((1, STARS), f32)
    local, used = own_indices(active, star * GAS + gas, gas * SLOTS)
    block, lane = local >> 7, local & 127
    packed = jnp.zeros((8, 128), f32)
    for b in range(STARS // 128):
        packed = jnp.where(
            used & (block == b), take_lanes(res[:, b * 128 : (b + 1) * 128], lane), packed
        )
    own[...] = packed
    zbuf[zi] = packed
    arrived()
    zc = [
        send(own, zbuf.at[zi], zs.at[d], zr.at[d], device)
        for d, (other, ozl, device) in enumerate(zp)
    ]
    edge0 = (lanes((128, 128)) * STARS).astype(f32)
    edge1 = edge0 + 128.0 * STARS
    count0 = jnp.zeros((8, 128), f32)
    count1 = jnp.zeros((8, 128), f32)
    for b in range(BLOCKS):
        row = jnp.broadcast_to(active[b : b + 1, :].astype(f32), (128, 128))
        col = jnp.transpose(row)
        less0 = jnp.where(col < edge0, 1.0, 0.0).reshape(16, 8, 128)
        less1 = jnp.where(col < edge1, 1.0, 0.0).reshape(16, 8, 128)
        count0 = count0 + jnp.sum(less0, 0)
        count1 = count1 + jnp.sum(less1, 0)
    begins[0:1, :] = jnp.sum(count0, 0, keepdims=True).astype(i32)
    begins[1:2, :] = jnp.sum(count1, 0, keepdims=True).astype(i32)
    for copy in zc:
        copy.wait()
    for z in range(ZL):
        merged = zbuf[z * GAS]
        for g in range(1, GAS):
            merged = merged + zbuf[z * GAS + g]
        tiles[y, z, xc] = merged
    yc = [
        send(tiles.at[y, :, xc], tiles.at[y, :, xc], ys.at[d], yr.at[d], device)
        for d, (other, device) in enumerate(yp)
    ]
    for copy in yc:
        copy.wait()
    xcs = [
        send(tiles.at[:, :, xc], tiles.at[:, :, xc], xs.at[d], xr.at[d], device)
        for d, (other, device) in enumerate(xp)
    ]
    for copy in xcs:
        copy.wait()


def compute_kernel(
    tiles, res, begins, active, density, flow_in, part, flow,
    targ, rb, mb, dz, dz2, mdz, gacc, pt, ks, square
):
    star, gas, y, zl, xc = place()
    lane8 = lanes()
    begin0 = jnp.broadcast_to(begins[0:1, :], (8, 128))
    begin1 = jnp.broadcast_to(begins[1:2, :], (8, 128))

    def compact(b, _):
        act = jnp.broadcast_to(active[pl.ds(b, 1), :], (8, 128))
        owner = act >> 9
        begin = jnp.where(
            owner < 128, take_lanes(begin0, owner & 127), take_lanes(begin1, owner & 127)
        )
        slot = b * 128 + lane8 - begin
        lane = (owner & (GAS - 1)) * SLOTS + slot
        tile = owner >> 2

        def pick(q, found):
            for r in range(8):
                found = jnp.where(tile == q * 8 + r, take_lanes(tiles[q * 8 + r], lane), found)
            return found

        targ[b] = lax.fori_loop(0, TILES // 8, pick, jnp.zeros((8, 128), f32))
        return 0

    lax.fori_loop(0, BLOCKS, compact, 0)

    square[...] = jnp.zeros((128, 128), f32)
    for q in range(STARS // 128):
        square[0:8, :] = res[:, q * 128 : (q + 1) * 128]
        turned = jnp.transpose(square[...])
        for f in range(7):
            column = turned[:, f : f + 1]
            if f == 6:
                column = column * gravity
            rb[f, q * 128 : (q + 1) * 128, :] = jnp.broadcast_to(column, (128, 128))
    for i in range(NXL):
        square[i * NYL : (i + 1) * NYL, 0:NZ] = density[i]
    turned = jnp.transpose(square[...])
    for c in range(COLS):
        mb[c] = jnp.broadcast_to(turned[0:NZ, c : c + 1] * gravity, (NZ, 128)).reshape(8, 8, 128)

    def row(b, f):
        return jnp.broadcast_to(targ[b, f : f + 1, :], (8, 128))

    height = (
        lax.broadcasted_iota(i32, (8, 8, 128), 0) * 8 + lax.broadcasted_iota(i32, (8, 8, 128), 1)
    ).astype(f32) + 0.5

    def stars_on(b, _):
        tx, ty, tz, tu, tv, tw = (row(b, f) for f in range(6))

        def group(g, sums):
            ax, ay, az, jx, jy, jz = sums
            for r in range(4):
                at = pl.ds(pl.multiple_of(g * 32 + r * 8, 8), 8)
                dx, dy, dzz = rb[0, at, :] - tx, rb[1, at, :] - ty, rb[2, at, :] - tz
                ux, uy, uz = rb[3, at, :] - tu, rb[4, at, :] - tv, rb[5, at, :] - tw
                inv = lax.rsqrt(dx * dx + dy * dy + dzz * dzz + soften)
                inv2 = inv * inv
                w = rb[6, at, :] * (inv2 * inv)
                q = 3.0 * (dx * ux + dy * uy + dzz * uz) * inv2
                ax, ay, az = ax + w * dx, ay + w * dy, az + w * dzz
                jx = jx + w * (ux - q * dx)
                jy = jy + w * (uy - q * dy)
                jz = jz + w * (uz - q * dzz)
            return ax, ay, az, jx, jy, jz

        zero = jnp.zeros((8, 128), f32)
        sums = lax.fori_loop(0, STARS // 32, group, (zero,) * 6)
        for f in range(6):
            pt[b, f : f + 1, :] = jnp.sum(sums[f], 0, keepdims=True)
        depth = height - row(b, 2)[None]
        dz[b] = depth
        dz2[b] = depth * depth
        mdz[b] = depth * (row(b, 6) * gravity)[None]
        for f in range(3):
            gacc[f, b] = zero
        return 0

    lax.fori_loop(0, BLOCKS, stars_on, 0)

    for f in range(3):
        ks[f] = jnp.zeros((128, 128), f32)
    x_first = (star * NXL).astype(f32) + 0.5
    y_first = (gas * NYL).astype(f32) + 0.5

    def column(c, _):
        x_here = x_first + lax.div(c, NYL).astype(f32)
        y_here = y_first + lax.rem(c, NYL).astype(f32)
        cell = mb[c]

        def targets_at(b, sums):
            kx, ky, kz = sums
            dx = x_here - row(b, 0)
            dy = y_here - row(b, 1)
            tm = row(b, 6) * gravity
            depth = dz[b]
            inv = lax.rsqrt((dx * dx + dy * dy + soften)[None] + dz2[b])
            w = inv * inv * inv
            u = cell * w
            total = jnp.sum(u, 0)
            gacc[0, b] += total * dx
            gacc[1, b] += total * dy
            gacc[2, b] += jnp.sum(u * depth, 0)
            kx = kx + w * (tm * dx)[None]
            ky = ky + w * (tm * dy)[None]
            kz = kz + w * mdz[b]
            return kx, ky, kz

        zero = jnp.zeros((8, 8, 128), f32)
        sums = lax.fori_loop(0, BLOCKS, targets_at, (zero,) * 3, unroll=2)
        mark = lanes((NZ, 128)) == c
        for f in range(3):
            column_sum = jnp.sum(sums[f].reshape(NZ, 128), 1, keepdims=True)
            ks[f, 0:NZ, :] = jnp.where(mark, column_sum, ks[f, 0:NZ, :])
        return 0

    lax.fori_loop(0, COLS, column, 0)
    for f in range(3):
        turned = jnp.transpose(ks[f])
        for i in range(NXL):
            flow[f, i] = flow_in[f, i] - time_step * turned[i * NYL : (i + 1) * NYL, 0:NZ]

    def close(b, _):
        for f in range(3):
            pt[b, f : f + 1, :] += jnp.sum(gacc[f, b], 0, keepdims=True)
        pt[b, 6:8, :] = jnp.zeros((2, 128), f32)
        return 0

    lax.fori_loop(0, BLOCKS, close, 0)

    def expand(s, _):
        owner = s * GAS + (lane8 >> 5)
        begin = jnp.where(
            owner < 128, take_lanes(begin0, owner & 127), take_lanes(begin1, owner & 127)
        )
        t = jnp.minimum(begin + (lane8 & (SLOTS - 1)), ACTIVE - 1)
        block, lane = t >> 7, t & 127
        found = jnp.zeros((8, 128), f32)
        for b in range(BLOCKS):
            found = jnp.where(block == b, take_lanes(pt[b], lane), found)
        part[s] = found
        return 0

    lax.fori_loop(0, TILES, expand, 0)


def cross_of(lhs, rhs):
    return (
        lhs[1] * rhs[2] - lhs[2] * rhs[1],
        lhs[2] * rhs[0] - lhs[0] * rhs[2],
        lhs[0] * rhs[1] - lhs[1] * rhs[0],
    )


def diff_x(v):
    return 0.5 * (v[2:] - v[:-2])


def diff_y(v):
    n = v.shape[1]
    return (0.5 * (pltpu.roll(v, n - 1, 1) - pltpu.roll(v, 1, 1)))[1:-1]


def diff_z(v):
    n = v.shape[2]
    return (0.5 * (pltpu.roll(v, n - 1, 2) - pltpu.roll(v, 1, 2)))[1:-1]


def curl_of(a, b, c):
    return (diff_y(c) - diff_z(b), diff_z(a) - diff_x(c), diff_x(b) - diff_y(a))


def rate_of(field, flow, resist):
    current = curl_of(*field)
    inner = tuple(v[1:-1] for v in field)
    drift = cross_of(cross_of(current, inner), inner)
    motion = cross_of(flow, inner)
    emf = tuple(m + resist * d for m, d in zip(motion, drift))
    return curl_of(*emf)


def finish_kernel(
    part, field, flow, density, pos, vel, accel, active, star_new, field_out,
    brick, near, r1, q1, r2, t2, r3, big, hs, hr, zs, zr, ys, yr, xs, xr
):
    star, gas, y, zl, xc = place()
    zi, zp = z_peers(y, zl, xc, gas)
    yp = y_peers(y, zl, xc, gas)
    xp = xc_peers(y, zl, xc, gas)
    stars_all = TILES
    sides = []
    for dx in (-1, 0, 1):
        for dy in (-1, 0, 1):
            if dx or dy:
                device = (
                    lax.rem(star + dx + stars_all, stars_all),
                    lax.rem(gas + dy + GAS, GAS),
                )
                sides.append((dx, dy, device))
    arrived = meet(
        [p[-1] for p in zp] + [p[-1] for p in yp] + [p[-1] for p in xp] + [p[-1] for p in sides]
    )
    for f in range(3):
        brick[f] = field[f]
        brick[3 + f] = flow[f]
    brick[6] = density[...]
    arrived()
    xcs = [
        send(part.at[:, :, other], r1.at[xc], xs.at[d], xr.at[d], device)
        for d, (other, device) in enumerate(xp)
    ]
    hcs = [
        send(brick, near.at[1 - dx, 1 - dy], hs.at[d], hr.at[d], device)
        for d, (dx, dy, device) in enumerate(sides)
    ]
    r1[xc] = part[:, :, xc]
    near[1, 1] = brick[...]
    for copy in xcs:
        copy.wait()
    total = r1[0]
    for n in range(1, XC):
        total = total + r1[n]
    q1[...] = total
    ycs = [
        send(q1.at[other], r2.at[y], ys.at[d], yr.at[d], device)
        for d, (other, device) in enumerate(yp)
    ]
    r2[y] = q1[y]
    for copy in ycs:
        copy.wait()
    total = r2[0]
    for n in range(1, YN):
        total = total + r2[n]
    t2[...] = total
    zcs = [
        send(t2.at[ozl], r3.at[zi], zs.at[d], zr.at[d], device)
        for d, (other, ozl, device) in enumerate(zp)
    ]
    r3[zi] = t2[zl]

    for copy in hcs:
        copy.wait()
    for c in range(7):
        for dx in range(3):
            for dy in range(3):
                for i in range(NXL):
                    v = near[dx, dy, c, i]
                    big[c, dx * NXL + i, dy * NYL : (dy + 1) * NYL, :] = jnp.concatenate(
                        [v, v], axis=1
                    )
    mag = tuple(big[c] for c in range(3))
    wind = tuple(big[3 + c] for c in range(3))
    inv = lax.rsqrt(big[6])
    resist = inv * inv * inv
    first = rate_of(mag, tuple(v[1:-1] for v in wind), resist[1:-1])
    one = tuple(m[2:-2] + field_step * r for m, r in zip(mag, first))
    second = rate_of(one, tuple(v[3:-3] for v in wind), resist[3:-3])
    for c in range(3):
        out = 0.5 * (mag[c][4:-4] + one[c][2:-2] + field_step * second[c])
        field_out[c] = out[:, NYL : 2 * NYL, 0:NZ]

    local, used = own_indices(active, star * GAS + gas, 0)
    for copy in zcs:
        copy.wait()
    total = r3[0]
    for n in range(1, ZL * GAS):
        total = total + r3[n]
    mine = pltpu.roll(total, lax.rem(128 - gas * SLOTS, 128), 1)
    index = lanes((8, STARS))
    sums = jnp.zeros((8, STARS), f32)
    hit = jnp.zeros((8, STARS), f32)
    for s in range(MOST):
        here = index == local[:, s : s + 1]
        sums = jnp.where(here, mine[:, s : s + 1], sums)
        hit = jnp.where(here, 1.0, hit)
    is_active = hit[0:3] > 0.5
    new_acc, new_jerk = sums[0:3], sums[3:6]
    p, v = pos[...], vel[...]
    old_acc, old_jerk = accel[0:3, :], accel[3:6, :]
    vel_one = v + time_step * (old_acc + new_acc) / 2.0 + time_step**2 * (old_jerk - new_jerk) / 12.0
    pos_one = p + time_step * (v + vel_one) / 2.0 + time_step**2 * (old_acc - new_acc) / 12.0
    star_new[0:3, :] = jnp.where(is_active, pos_one, p)
    star_new[3:6, :] = jnp.where(is_active, vel_one, v)
    star_new[6:9, :] = jnp.where(is_active, new_acc, old_acc)
    star_new[9:12, :] = jnp.where(is_active, new_jerk, old_jerk)


VM = pl.BlockSpec(memory_space=pltpu.VMEM)
DMA = pltpu.SemaphoreType.DMA


def body(star_pos, star_vel, star_accel, star_mass, active, density, flow_in, field_in):
    act = active.reshape(BLOCKS, 128)
    tiles, res, begins = pl.pallas_call(
        gather_kernel,
        out_shape=(
            jax.ShapeDtypeStruct((YN, ZL, XC, 8, 128), f32),
            jax.ShapeDtypeStruct((8, STARS), f32),
            jax.ShapeDtypeStruct((2, 128), i32),
        ),
        in_specs=[VM] * 5,
        out_specs=(VM,) * 3,
        scratch_shapes=[
            pltpu.VMEM((ZL * GAS, 8, 128), f32),
            pltpu.VMEM((8, 128), f32),
            DMA((ZL * GAS - 1,)), DMA((ZL * GAS - 1,)),
            DMA((YN - 1,)), DMA((YN - 1,)),
            DMA((XC - 1,)), DMA((XC - 1,)),
        ],
        compiler_params=pltpu.CompilerParams(collective_id=0, has_side_effects=True),
        name="gather_targets",
    )(star_pos, star_vel, star_accel, star_mass.reshape(1, STARS), act)
    part, flow = pl.pallas_call(
        compute_kernel,
        out_shape=(
            jax.ShapeDtypeStruct((TILES, 8, 128), f32),
            jax.ShapeDtypeStruct((3, NXL, NYL, NZ), f32),
        ),
        in_specs=[VM] * 6,
        out_specs=(VM,) * 2,
        scratch_shapes=[
            pltpu.VMEM((BLOCKS, 8, 128), f32),
            pltpu.VMEM((7, STARS, 128), f32),
            pltpu.VMEM((COLS, 8, 8, 128), f32),
            pltpu.VMEM((BLOCKS, 8, 8, 128), f32),
            pltpu.VMEM((BLOCKS, 8, 8, 128), f32),
            pltpu.VMEM((BLOCKS, 8, 8, 128), f32),
            pltpu.VMEM((3, BLOCKS, 8, 128), f32),
            pltpu.VMEM((BLOCKS, 8, 128), f32),
            pltpu.VMEM((3, 128, 128), f32),
            pltpu.VMEM((128, 128), f32),
        ],
        compiler_params=pltpu.CompilerParams(vmem_limit_bytes=48 << 20),
        name="pair_sums",
    )(tiles.reshape(TILES, 8, 128), res, begins, act, density, flow_in)
    star_new, field_out = pl.pallas_call(
        finish_kernel,
        out_shape=(
            jax.ShapeDtypeStruct((12, STARS), f32),
            jax.ShapeDtypeStruct((3, NXL, NYL, NZ), f32),
        ),
        in_specs=[VM] * 8,
        out_specs=(VM,) * 2,
        scratch_shapes=[
            pltpu.VMEM((7, NXL, NYL, NZ), f32),
            pltpu.VMEM((3, 3, 7, NXL, NYL, NZ), f32),
            pltpu.VMEM((XC, YN, ZL, 8, 128), f32),
            pltpu.VMEM((YN, ZL, 8, 128), f32),
            pltpu.VMEM((YN, ZL, 8, 128), f32),
            pltpu.VMEM((ZL, 8, 128), f32),
            pltpu.VMEM((ZL * GAS, 8, 128), f32),
            pltpu.VMEM((7, 3 * NXL, 3 * NYL, 128), f32),
            DMA((8,)), DMA((8,)),
            DMA((ZL * GAS - 1,)), DMA((ZL * GAS - 1,)),
            DMA((YN - 1,)), DMA((YN - 1,)),
            DMA((XC - 1,)), DMA((XC - 1,)),
        ],
        compiler_params=pltpu.CompilerParams(collective_id=1, has_side_effects=True),
        name="finish_step",
    )(
        part.reshape(YN, ZL, XC, 8, 128), field_in, flow, density,
        star_pos, star_vel, star_accel, act,
    )
    return (star_new, flow, field_out)


def solution(mesh):
    placed = (
        P(None, ("star", "gas")),
        P(None, ("star", "gas")),
        P(None, ("star", "gas")),
        P(("star", "gas")),
        P(),
        P("star", "gas", None),
        P(None, "star", "gas", None),
        P(None, "star", "gas", None),
    )
    return jax.shard_map(
        body,
        mesh=mesh,
        in_specs=placed,
        out_specs=(
            P(None, ("star", "gas")),
            P(None, "star", "gas", None),
            P(None, "star", "gas", None),
        ),
        check_vma=False,
    )
```

```python
import functools

import jax
import jax.numpy as jnp
from jax import lax
from jax.experimental import pallas as pl
from jax.experimental.pallas import tpu as pltpu
from jax.sharding import PartitionSpec as P

MESH = pl.DeviceIdType.MESH
gravity = 0.02
soften = 4.0
time_step = 1.5
field_step = 0.1

STARS = 512
ACTIVE = 2048
BLOCKS = ACTIVE // 128
XC, ZL, YN, GAS = 8, 2, 4, 4
TILES = YN * ZL * XC
SLOTS = 32
MOST = 24
NXL, NYL, NZ = 4, 8, 64
WIDE = 256
WIDES = ACTIVE // WIDE
CELL_TILES = NXL * NYL * NZ // WIDE
MIDDLE = 16.0
f32 = jnp.float32
bf16 = jnp.bfloat16
i32 = jnp.int32


def lanes(shape=(8, 128)):
    return lax.broadcasted_iota(i32, shape, len(shape) - 1)


def take_lanes(values, index):
    return jnp.take_along_axis(values, index, axis=1, mode="promise_in_bounds")


def place():
    star = lax.axis_index("star")
    gas = lax.axis_index("gas")
    xc = lax.rem(star, XC)
    zl = lax.rem(lax.div(star, XC), ZL)
    y = lax.div(star, XC * ZL)
    return star, gas, y, zl, xc


def star_of(y, zl, xc):
    return (y * ZL + zl) * XC + xc


def z_peers(y, zl, xc, gas):
    zi = zl * GAS + gas
    peers = []
    for d in range(1, ZL * GAS):
        other = lax.rem(zi + d, ZL * GAS)
        ozl, ogas = lax.div(other, GAS), lax.rem(other, GAS)
        peers.append((other, ozl, (star_of(y, ozl, xc), ogas)))
    return zi, peers


def y_peers(y, zl, xc, gas):
    peers = []
    for d in range(1, YN):
        other = lax.rem(y + d, YN)
        peers.append((other, (star_of(other, zl, xc), gas)))
    return peers


def xc_peers(y, zl, xc, gas):
    peers = []
    for d in range(1, XC):
        other = lax.rem(xc + d, XC)
        peers.append((other, (star_of(y, zl, other), gas)))
    return peers


def meet(devices):
    barrier = pltpu.get_barrier_semaphore()
    for device in devices:
        pl.semaphore_signal(barrier, inc=1, device_id=device, device_id_type=MESH)
    return lambda: pl.semaphore_wait(barrier, len(devices))


def send(src, dst, send_sem, recv_sem, device):
    copy = pltpu.make_async_remote_copy(
        src_ref=src, dst_ref=dst, send_sem=send_sem, recv_sem=recv_sem,
        device_id=device, device_id_type=MESH,
    )
    copy.start()
    return copy


def own_indices(active_ref, rank, lane0):
    act = active_ref[...]
    base = rank * STARS
    begin = jnp.sum((act < base).astype(f32)).astype(i32)
    slot = lanes() - lane0
    t = begin + slot
    inside = (slot >= 0) & (slot < SLOTS) & (t < ACTIVE)
    t = jnp.where(inside, t, 0)
    block, lane = t >> 7, t & 127
    found = jnp.full((8, 128), -1, i32)
    for b in range(BLOCKS):
        row = jnp.broadcast_to(active_ref[b : b + 1, :], (8, 128))
        found = jnp.where(block == b, take_lanes(row, lane), found)
    local = found - base
    used = inside & (local >= 0) & (local < STARS)
    return jnp.where(used, local, -1), used


def gather_kernel(
    pos, vel, accel, mass, active, tiles, res, begins, zbuf, own, zs, zr, ys, yr, xs, xr
):
    star, gas, y, zl, xc = place()
    zi, zp = z_peers(y, zl, xc, gas)
    yp = y_peers(y, zl, xc, gas)
    xp = xc_peers(y, zl, xc, gas)
    arrived = meet([p[-1] for p in zp] + [p[-1] for p in yp] + [p[-1] for p in xp])
    old_acc, old_jerk = accel[0:3, :], accel[3:6, :]
    v = vel[...]
    res[0:3, :] = (
        pos[...] + time_step * v + time_step**2 / 2.0 * old_acc + time_step**3 / 6.0 * old_jerk
    )
    res[3:6, :] = v + time_step * old_acc + time_step**2 / 2.0 * old_jerk
    res[6:7, :] = mass[...]
    res[7:8, :] = jnp.zeros((1, STARS), f32)
    local, used = own_indices(active, star * GAS + gas, gas * SLOTS)
    block, lane = local >> 7, local & 127
    packed = jnp.zeros((8, 128), f32)
    for b in range(STARS // 128):
        packed = jnp.where(
            used & (block == b), take_lanes(res[:, b * 128 : (b + 1) * 128], lane), packed
        )
    own[...] = packed
    zbuf[zi] = packed
    arrived()
    zc = [
        send(own, zbuf.at[zi], zs.at[d], zr.at[d], device)
        for d, (other, ozl, device) in enumerate(zp)
    ]
    edge0 = (lanes((128, 128)) * STARS).astype(f32)
    edge1 = edge0 + 128.0 * STARS
    count0 = jnp.zeros((8, 128), f32)
    count1 = jnp.zeros((8, 128), f32)
    for b in range(BLOCKS):
        row = jnp.broadcast_to(active[b : b + 1, :].astype(f32), (128, 128))
        col = jnp.transpose(row)
        less0 = jnp.where(col < edge0, 1.0, 0.0).reshape(16, 8, 128)
        less1 = jnp.where(col < edge1, 1.0, 0.0).reshape(16, 8, 128)
        count0 = count0 + jnp.sum(less0, 0)
        count1 = count1 + jnp.sum(less1, 0)
    begins[0:1, :] = jnp.sum(count0, 0, keepdims=True).astype(i32)
    begins[1:2, :] = jnp.sum(count1, 0, keepdims=True).astype(i32)
    for copy in zc:
        copy.wait()
    for z in range(ZL):
        merged = zbuf[z * GAS]
        for g in range(1, GAS):
            merged = merged + zbuf[z * GAS + g]
        tiles[y, z, xc] = merged
    yc = [
        send(tiles.at[y, :, xc], tiles.at[y, :, xc], ys.at[d], yr.at[d], device)
        for d, (other, device) in enumerate(yp)
    ]
    for copy in yc:
        copy.wait()
    xcs = [
        send(tiles.at[:, :, xc], tiles.at[:, :, xc], xs.at[d], xr.at[d], device)
        for d, (other, device) in enumerate(xp)
    ]
    for copy in xcs:
        copy.wait()


def split(v):
    hi = v.astype(bf16)
    return hi, (v - hi.astype(f32)).astype(bf16)


def twice(v):
    return jnp.concatenate([v, v], axis=1)


def both(v):
    hi = v.astype(bf16).astype(f32)
    return jnp.concatenate([hi, v - hi], axis=0).astype(bf16)


def dot_nn(lhs, rhs):
    return jnp.dot(lhs, rhs, preferred_element_type=f32)


def dot_nt(lhs, rhs):
    return lax.dot_general(lhs, rhs, (((1,), (1,)), ((), ())), preferred_element_type=f32)


def fold(v):
    v = v[0:8] + v[8:16]
    return v[:, 0:WIDE] + v[:, WIDE:] if v.shape[1] > WIDE else v


def compute_kernel(
    tiles, res, begins, active, density, flow_in, begin_of, active_of, part, flow,
    targ, rb, sm, cm, tm, dz2, mom, kacc, pt, rows8, square, wa, wb, pa, pb
):
    star, gas, y, zl, xc = place()
    lane8 = lanes()
    begin0 = jnp.broadcast_to(begins[0:1, :], (8, 128))
    begin1 = jnp.broadcast_to(begins[1:2, :], (8, 128))

    def compact(b, _):
        act = jnp.broadcast_to(active[pl.ds(b, 1), :], (8, 128))
        owner = act >> 9
        begin = jnp.where(
            owner < 128, take_lanes(begin0, owner & 127), take_lanes(begin1, owner & 127)
        )
        slot = b * 128 + lane8 - begin
        lane = (owner & (GAS - 1)) * SLOTS + slot
        tile = owner >> 2
        low, high = active_of[b, 0] >> 11, active_of[b, 127] >> 11

        def pick(q, found):
            for r in range(4):
                at = jnp.minimum(low + q * 4 + r, TILES - 1)
                found = jnp.where(tile == at, take_lanes(tiles[at], lane), found)
            return found

        targ[b] = lax.fori_loop(0, (high - low) // 4 + 1, pick, jnp.zeros((8, 128), f32))
        return 0

    lax.fori_loop(0, BLOCKS, compact, 0)

    square[...] = jnp.zeros((128, 128), f32)
    for q in range(STARS // 128):
        square[0:8, :] = res[:, q * 128 : (q + 1) * 128]
        turned = jnp.transpose(square[...])
        for f in range(6):
            rb[f, q * 128 : (q + 1) * 128, :] = jnp.broadcast_to(turned[:, f : f + 1], (128, 128))
    gm = res[6:7, :] * gravity
    rows8[0:1, :] = gm
    rows8[1:4, :] = gm * (res[0:3, :] - MIDDLE)
    rows8[4:7, :] = gm * res[3:6, :]
    rows8[7:8, :] = jnp.zeros((1, STARS), f32)
    sm[...] = both(rows8[...])

    x_mid = (star * NXL).astype(f32) + 0.5 * NXL
    y_mid = (gas * NYL).astype(f32) + 0.5 * NYL
    z_mid = 0.5 * NZ
    lane1 = lanes((1, 128))
    z_off = (lane1 & (NZ - 1)).astype(f32) + (0.5 - z_mid)
    rows8[4:8, :] = jnp.zeros((4, STARS), f32)
    for i in range(NXL):
        cells = twice(density[i]) * gravity
        for h in range(NYL // 2):
            q, at = i * 2 + h // 2, (h % 2) * 128
            cell = jnp.where(lane1 < NZ, cells[2 * h : 2 * h + 1], cells[2 * h + 1 : 2 * h + 2])
            y_off = jnp.where(lane1 < NZ, 2 * h, 2 * h + 1).astype(f32) + (0.5 - 0.5 * NYL)
            rows8[0:1, at : at + 128] = cell
            rows8[1:2, at : at + 128] = cell * (i + 0.5 - 0.5 * NXL)
            rows8[2:3, at : at + 128] = cell * y_off
            rows8[3:4, at : at + 128] = cell * z_off
            if h % 2:
                cm[q] = both(rows8[:, 0:WIDE])

    def wide(p, f):
        two = jnp.concatenate([targ[2 * p, f : f + 1, :], targ[2 * p + 1, f : f + 1, :]], axis=1)
        return jnp.broadcast_to(two, (8, WIDE))

    height = lax.broadcasted_iota(i32, (NZ, WIDE), 0).astype(f32) + 0.5

    def moments(p, _):
        gm = wide(p, 6)[0:1] * gravity
        rows8[0:1, 0:WIDE] = gm
        rows8[1:2, 0:WIDE] = gm * (wide(p, 0)[0:1] - x_mid)
        rows8[2:3, 0:WIDE] = gm * (wide(p, 1)[0:1] - y_mid)
        rows8[3:4, 0:WIDE] = gm * (wide(p, 2)[0:1] - z_mid)
        tm[p] = twice(both(rows8[:, 0:WIDE]))
        depth = height - jnp.broadcast_to(wide(p, 2)[0:1], (NZ, WIDE))
        dz2[p] = depth * depth
        for f in range(3):
            mom[f, p] = jnp.zeros((8, WIDE), f32)
        return 0

    lax.fori_loop(0, WIDES, moments, 0)
    for buffer in (wa, wb, pa, pb):
        buffer[...] = jnp.zeros((WIDE, 2 * WIDE), bf16)
    for q in range(CELL_TILES):
        kacc[q] = jnp.zeros((8, WIDE), f32)

    def star_weights(p, c, w_buf, p_buf):
        tx, ty, tz, tu, tv, tw = (jnp.concatenate([wide(p, f)] * 2, axis=0) for f in range(6))
        for g in range(WIDE // 16):
            at = pl.ds(c * WIDE + g * 16, 16)
            dx, dy, dz = twice(rb[0, at, :]) - tx, twice(rb[1, at, :]) - ty, twice(rb[2, at, :]) - tz
            ux, uy, uz = twice(rb[3, at, :]) - tu, twice(rb[4, at, :]) - tv, twice(rb[5, at, :]) - tw
            inv = lax.rsqrt(dx * dx + dy * dy + dz * dz + soften)
            inv2 = inv * inv
            w = inv2 * inv
            pull = (dx * ux + dy * uy + dz * uz) * (3.0 * inv2) * w
            here = slice(g * 16, (g + 1) * 16)
            w_buf[here, 0:WIDE], w_buf[here, WIDE:] = split(w)
            p_buf[here, 0:WIDE], p_buf[here, WIDE:] = split(pull)

    def star_sums(p, c, w_buf, p_buf):
        lhs = sm[:, c * WIDE : (c + 1) * WIDE]
        mom[0, p] += fold(dot_nn(lhs, w_buf[...]))
        mom[1, p] += fold(dot_nn(lhs, p_buf[...]))

    def stars_on(p, _):
        star_sums(jnp.maximum(p - 1, 0), 1, wb, pb)
        star_weights(p, 0, wa, pa)
        star_sums(p, 0, wa, pa)
        star_weights(p, 1, wb, pb)
        return 0

    lax.fori_loop(0, WIDES, stars_on, 0)
    star_sums(WIDES - 1, 1, wb, pb)
    wb[...] = jnp.zeros((WIDE, 2 * WIDE), bf16)

    x_first, y_first = x_mid - 0.5 * NXL + 0.5, y_mid - 0.5 * NYL + 0.5

    def gas_weights(step, half, w_buf):
        p, i = lax.div(step, NXL), lax.rem(step, NXL)
        dx = (x_first + i.astype(f32)) - wide(p, 0)
        dx2 = dx * dx + soften
        ty = wide(p, 1)
        for j in range(4):
            dy = (y_first + (half * 4.0 + j)) - ty
            side = dx2 + dy * dy
            side = jnp.concatenate([side, side], axis=0)
            for g in range(NZ // 16):
                inv = lax.rsqrt(side + dz2[p, g * 16 : (g + 1) * 16, :])
                here = slice(j * NZ + g * 16, j * NZ + (g + 1) * 16)
                w_buf[here, 0:WIDE], w_buf[here, WIDE:] = split(inv * inv * inv)

    def gas_sums(step, half, w_buf):
        p, i = lax.div(step, NXL), lax.rem(step, NXL)
        q = i * 2 + half
        w = w_buf[...]
        mom[2, p] += fold(dot_nn(cm[q], w))
        kacc[q] += fold(dot_nt(tm[p], w))

    def gas_on(step, _):
        gas_sums(jnp.maximum(step - 1, 0), 1, wb)
        gas_weights(step, 0, wa)
        gas_sums(step, 0, wa)
        gas_weights(step, 1, wb)
        return 0

    lax.fori_loop(0, WIDES * NXL, gas_on, 0)
    gas_sums(jnp.int32(WIDES * NXL - 1), 1, wb)

    for q in range(CELL_TILES):
        i, half = q // 2, q % 2
        sums = kacc[q]
        for h in range(2):
            at = slice(h * 128, (h + 1) * 128)
            y_off = jnp.where(lane1 < NZ, 0, 1).astype(f32) + (half * 4 + h * 2 + 0.5 - 0.5 * NYL)
            none = sums[0:1, at]
            kick = (
                sums[1:2, at] - (i + 0.5 - 0.5 * NXL) * none,
                sums[2:3, at] - y_off * none,
                sums[3:4, at] - z_off * none,
            )
            for f in range(3):
                row = jnp.broadcast_to(kick[f], (8, 128))
                turned = pltpu.roll(row, NZ, 1)
                j = half * 4 + h * 2
                flow[f, i, j : j + 1, :] = (
                    flow_in[f, i, j : j + 1, :] + time_step * row[0:1, 0:NZ]
                )
                flow[f, i, j + 1 : j + 2, :] = (
                    flow_in[f, i, j + 1 : j + 2, :] + time_step * turned[0:1, 0:NZ]
                )

    def close(p, _):
        w, pull, g = mom[0, p], mom[1, p], mom[2, p]
        mids = (x_mid, y_mid, z_mid)
        for f in range(3):
            at = wide(p, f)[0:1]
            acc = (w[1 + f : 2 + f] - (at - MIDDLE) * w[0:1]) + (
                g[1 + f : 2 + f] - (at - mids[f]) * g[0:1]
            )
            jerk = (w[4 + f : 5 + f] - wide(p, 3 + f)[0:1] * w[0:1]) - (
                pull[1 + f : 2 + f] - (at - MIDDLE) * pull[0:1]
            )
            for h in range(2):
                pt[2 * p + h, f : f + 1, :] = acc[:, h * 128 : (h + 1) * 128]
                pt[2 * p + h, 3 + f : 4 + f, :] = jerk[:, h * 128 : (h + 1) * 128]
        for h in range(2):
            pt[2 * p + h, 6:8, :] = jnp.zeros((2, 128), f32)
        return 0

    lax.fori_loop(0, WIDES, close, 0)

    def expand(s, _):
        owner = s * GAS + (lane8 >> 5)
        begin = jnp.where(s < TILES // 2, take_lanes(begin0, owner & 127), take_lanes(begin1, owner & 127))
        t = jnp.minimum(begin + (lane8 & (SLOTS - 1)), ACTIVE - 1)
        block, lane = t >> 7, t & 127
        first = jnp.minimum(begin_of[s // (TILES // 2), (s * GAS) % 128] >> 7, BLOCKS - 1)
        second = jnp.minimum(first + 1, BLOCKS - 1)
        part[s] = jnp.where(
            block == first, take_lanes(pt[first], lane), take_lanes(pt[second], lane)
        )
        return 0

    lax.fori_loop(0, TILES, expand, 0, unroll=4)


def cross_of(lhs, rhs):
    return (
        lhs[1] * rhs[2] - lhs[2] * rhs[1],
        lhs[2] * rhs[0] - lhs[0] * rhs[2],
        lhs[0] * rhs[1] - lhs[1] * rhs[0],
    )


def diff_x(v):
    return 0.5 * (v[2:] - v[:-2])


def diff_y(v):
    n = v.shape[1]
    return (0.5 * (pltpu.roll(v, n - 1, 1) - pltpu.roll(v, 1, 1)))[1:-1]


def diff_z(v):
    n = v.shape[2]
    return (0.5 * (pltpu.roll(v, n - 1, 2) - pltpu.roll(v, 1, 2)))[1:-1]


def curl_of(a, b, c):
    return (diff_y(c) - diff_z(b), diff_z(a) - diff_x(c), diff_x(b) - diff_y(a))


def rate_of(field, flow, resist):
    current = curl_of(*field)
    inner = tuple(v[1:-1] for v in field)
    drift = cross_of(cross_of(current, inner), inner)
    motion = cross_of(flow, inner)
    emf = tuple(m + resist * d for m, d in zip(motion, drift))
    return curl_of(*emf)


def finish_kernel(
    part, field, flow, density, pos, vel, accel, active, star_new, field_out,
    brick, near, r1, q1, r2, t2, r3, big, hs, hr, zs, zr, ys, yr, xs, xr
):
    star, gas, y, zl, xc = place()
    zi, zp = z_peers(y, zl, xc, gas)
    yp = y_peers(y, zl, xc, gas)
    xp = xc_peers(y, zl, xc, gas)
    stars_all = TILES
    sides = []
    for dx in (-1, 0, 1):
        for dy in (-1, 0, 1):
            if dx or dy:
                device = (
                    lax.rem(star + dx + stars_all, stars_all),
                    lax.rem(gas + dy + GAS, GAS),
                )
                sides.append((dx, dy, device))
    arrived = meet(
        [p[-1] for p in zp] + [p[-1] for p in yp] + [p[-1] for p in xp] + [p[-1] for p in sides]
    )
    for f in range(3):
        brick[f] = field[f]
        brick[3 + f] = flow[f]
    brick[6] = density[...]
    arrived()
    xcs = [
        send(part.at[:, :, other], r1.at[xc], xs.at[d], xr.at[d], device)
        for d, (other, device) in enumerate(xp)
    ]
    hcs = [
        send(brick, near.at[1 - dx, 1 - dy], hs.at[d], hr.at[d], device)
        for d, (dx, dy, device) in enumerate(sides)
    ]
    r1[xc] = part[:, :, xc]
    near[1, 1] = brick[...]
    for copy in xcs:
        copy.wait()
    total = r1[0]
    for n in range(1, XC):
        total = total + r1[n]
    q1[...] = total
    ycs = [
        send(q1.at[other], r2.at[y], ys.at[d], yr.at[d], device)
        for d, (other, device) in enumerate(yp)
    ]
    r2[y] = q1[y]
    for copy in ycs:
        copy.wait()
    total = r2[0]
    for n in range(1, YN):
        total = total + r2[n]
    t2[...] = total
    zcs = [
        send(t2.at[ozl], r3.at[zi], zs.at[d], zr.at[d], device)
        for d, (other, ozl, device) in enumerate(zp)
    ]
    r3[zi] = t2[zl]

    for copy in hcs:
        copy.wait()
    for c in range(7):
        for dx in range(3):
            for dy in range(3):
                for i in range(NXL):
                    v = near[dx, dy, c, i]
                    big[c, dx * NXL + i, dy * NYL : (dy + 1) * NYL, :] = jnp.concatenate(
                        [v, v], axis=1
                    )
    mag = tuple(big[c] for c in range(3))
    wind = tuple(big[3 + c] for c in range(3))
    inv = lax.rsqrt(big[6])
    resist = inv * inv * inv
    first = rate_of(mag, tuple(v[1:-1] for v in wind), resist[1:-1])
    one = tuple(m[2:-2] + field_step * r for m, r in zip(mag, first))
    second = rate_of(one, tuple(v[3:-3] for v in wind), resist[3:-3])
    for c in range(3):
        out = 0.5 * (mag[c][4:-4] + one[c][2:-2] + field_step * second[c])
        field_out[c] = out[:, NYL : 2 * NYL, 0:NZ]

    local, used = own_indices(active, star * GAS + gas, 0)
    for copy in zcs:
        copy.wait()
    total = r3[0]
    for n in range(1, ZL * GAS):
        total = total + r3[n]
    mine = pltpu.roll(total, lax.rem(128 - gas * SLOTS, 128), 1)
    index = lanes((8, STARS))
    sums = jnp.zeros((8, STARS), f32)
    hit = jnp.zeros((8, STARS), f32)
    for s in range(MOST):
        here = index == local[:, s : s + 1]
        sums = jnp.where(here, mine[:, s : s + 1], sums)
        hit = jnp.where(here, 1.0, hit)
    is_active = hit[0:3] > 0.5
    new_acc, new_jerk = sums[0:3], sums[3:6]
    p, v = pos[...], vel[...]
    old_acc, old_jerk = accel[0:3, :], accel[3:6, :]
    vel_one = v + time_step * (old_acc + new_acc) / 2.0 + time_step**2 * (old_jerk - new_jerk) / 12.0
    pos_one = p + time_step * (v + vel_one) / 2.0 + time_step**2 * (old_acc - new_acc) / 12.0
    star_new[0:3, :] = jnp.where(is_active, pos_one, p)
    star_new[3:6, :] = jnp.where(is_active, vel_one, v)
    star_new[6:9, :] = jnp.where(is_active, new_acc, old_acc)
    star_new[9:12, :] = jnp.where(is_active, new_jerk, old_jerk)


VM = pl.BlockSpec(memory_space=pltpu.VMEM)
SM = pl.BlockSpec(memory_space=pltpu.SMEM)
DMA = pltpu.SemaphoreType.DMA


def body(star_pos, star_vel, star_accel, star_mass, active, density, flow_in, field_in):
    act = active.reshape(BLOCKS, 128)
    tiles, res, begins = pl.pallas_call(
        gather_kernel,
        out_shape=(
            jax.ShapeDtypeStruct((YN, ZL, XC, 8, 128), f32),
            jax.ShapeDtypeStruct((8, STARS), f32),
            jax.ShapeDtypeStruct((2, 128), i32),
        ),
        in_specs=[VM] * 5,
        out_specs=(VM,) * 3,
        scratch_shapes=[
            pltpu.VMEM((ZL * GAS, 8, 128), f32),
            pltpu.VMEM((8, 128), f32),
            DMA((ZL * GAS - 1,)), DMA((ZL * GAS - 1,)),
            DMA((YN - 1,)), DMA((YN - 1,)),
            DMA((XC - 1,)), DMA((XC - 1,)),
        ],
        compiler_params=pltpu.CompilerParams(collective_id=0, has_side_effects=True),
        name="gather_targets",
    )(star_pos, star_vel, star_accel, star_mass.reshape(1, STARS), act)
    part, flow = pl.pallas_call(
        compute_kernel,
        out_shape=(
            jax.ShapeDtypeStruct((TILES, 8, 128), f32),
            jax.ShapeDtypeStruct((3, NXL, NYL, NZ), f32),
        ),
        in_specs=[VM] * 6 + [SM] * 2,
        out_specs=(VM,) * 2,
        scratch_shapes=[
            pltpu.VMEM((BLOCKS, 8, 128), f32),
            pltpu.VMEM((6, STARS, 128), f32),
            pltpu.VMEM((16, STARS), bf16),
            pltpu.VMEM((CELL_TILES, 16, WIDE), bf16),
            pltpu.VMEM((WIDES, 16, 2 * WIDE), bf16),
            pltpu.VMEM((WIDES, NZ, WIDE), f32),
            pltpu.VMEM((3, WIDES, 8, WIDE), f32),
            pltpu.VMEM((CELL_TILES, 8, WIDE), f32),
            pltpu.VMEM((BLOCKS, 8, 128), f32),
            pltpu.VMEM((8, STARS), f32),
            pltpu.VMEM((128, 128), f32),
            pltpu.VMEM((WIDE, 2 * WIDE), bf16),
            pltpu.VMEM((WIDE, 2 * WIDE), bf16),
            pltpu.VMEM((WIDE, 2 * WIDE), bf16),
            pltpu.VMEM((WIDE, 2 * WIDE), bf16),
        ],
        compiler_params=pltpu.CompilerParams(vmem_limit_bytes=48 << 20),
        name="pair_sums",
    )(tiles.reshape(TILES, 8, 128), res, begins, act, density, flow_in, begins, act)
    star_new, field_out = pl.pallas_call(
        finish_kernel,
        out_shape=(
            jax.ShapeDtypeStruct((12, STARS), f32),
            jax.ShapeDtypeStruct((3, NXL, NYL, NZ), f32),
        ),
        in_specs=[VM] * 8,
        out_specs=(VM,) * 2,
        scratch_shapes=[
            pltpu.VMEM((7, NXL, NYL, NZ), f32),
            pltpu.VMEM((3, 3, 7, NXL, NYL, NZ), f32),
            pltpu.VMEM((XC, YN, ZL, 8, 128), f32),
            pltpu.VMEM((YN, ZL, 8, 128), f32),
            pltpu.VMEM((YN, ZL, 8, 128), f32),
            pltpu.VMEM((ZL, 8, 128), f32),
            pltpu.VMEM((ZL * GAS, 8, 128), f32),
            pltpu.VMEM((7, 3 * NXL, 3 * NYL, 128), f32),
            DMA((8,)), DMA((8,)),
            DMA((ZL * GAS - 1,)), DMA((ZL * GAS - 1,)),
            DMA((YN - 1,)), DMA((YN - 1,)),
            DMA((XC - 1,)), DMA((XC - 1,)),
        ],
        compiler_params=pltpu.CompilerParams(collective_id=1, has_side_effects=True),
        name="finish_step",
    )(
        part.reshape(YN, ZL, XC, 8, 128), field_in, flow, density,
        star_pos, star_vel, star_accel, act,
    )
    return (star_new, flow, field_out)


def solution(mesh):
    placed = (
        P(None, ("star", "gas")),
        P(None, ("star", "gas")),
        P(None, ("star", "gas")),
        P(("star", "gas")),
        P(),
        P("star", "gas", None),
        P(None, "star", "gas", None),
        P(None, "star", "gas", None),
    )
    return jax.shard_map(
        body,
        mesh=mesh,
        in_specs=placed,
        out_specs=(
            P(None, ("star", "gas")),
            P(None, "star", "gas", None),
            P(None, "star", "gas", None),
        ),
        check_vma=False,
    )
```

```python
import functools

import jax
import jax.numpy as jnp
from jax import lax
from jax.experimental import pallas as pl
from jax.experimental.pallas import tpu as pltpu
from jax.sharding import PartitionSpec as P

MESH = pl.DeviceIdType.MESH
gravity = 0.02
soften = 4.0
time_step = 1.5
field_step = 0.1

STARS = 512
ACTIVE = 2048
BLOCKS = ACTIVE // 128
XC, ZL, YN, GAS = 8, 2, 4, 4
TILES = YN * ZL * XC
PATH = TILES + BLOCKS
SLOTS = 32
MOST = 24
NXL, NYL, NZ = 4, 8, 64
WIDE = 256
WIDES = ACTIVE // WIDE
CELL_TILES = NXL * NYL * NZ // WIDE
MIDDLE = 16.0
f32 = jnp.float32
bf16 = jnp.bfloat16
i32 = jnp.int32


def lanes(shape=(8, 128)):
    return lax.broadcasted_iota(i32, shape, len(shape) - 1)


def take_lanes(values, index):
    return jnp.take_along_axis(values, index, axis=1, mode="promise_in_bounds")


def place():
    star = lax.axis_index("star")
    gas = lax.axis_index("gas")
    xc = lax.rem(star, XC)
    zl = lax.rem(lax.div(star, XC), ZL)
    y = lax.div(star, XC * ZL)
    return star, gas, y, zl, xc


def tile_at(tile):
    return tile >> 4, (tile >> 3) & 1, tile & 7


def star_of(y, zl, xc):
    return (y * ZL + zl) * XC + xc


def z_peers(y, zl, xc, gas):
    zi = zl * GAS + gas
    peers = []
    for d in range(1, ZL * GAS):
        other = lax.rem(zi + d, ZL * GAS)
        ozl, ogas = lax.div(other, GAS), lax.rem(other, GAS)
        peers.append((other, ozl, (star_of(y, ozl, xc), ogas)))
    return zi, peers


def y_peers(y, zl, xc, gas):
    peers = []
    for d in range(1, YN):
        other = lax.rem(y + d, YN)
        peers.append((other, (star_of(other, zl, xc), gas)))
    return peers


def xc_peers(y, zl, xc, gas):
    peers = []
    for d in range(1, XC):
        other = lax.rem(xc + d, XC)
        peers.append((other, (star_of(y, zl, other), gas)))
    return peers


def meet(devices):
    barrier = pltpu.get_barrier_semaphore()
    for device in devices:
        pl.semaphore_signal(barrier, inc=1, device_id=device, device_id_type=MESH)
    return lambda: pl.semaphore_wait(barrier, len(devices))


def send(src, dst, send_sem, recv_sem, device):
    copy = pltpu.make_async_remote_copy(
        src_ref=src, dst_ref=dst, send_sem=send_sem, recv_sem=recv_sem,
        device_id=device, device_id_type=MESH,
    )
    copy.start()
    return copy


def own_indices(active_ref, rank, lane0):
    act = active_ref[...]
    base = rank * STARS
    begin = jnp.sum((act < base).astype(f32)).astype(i32)
    slot = lanes() - lane0
    t = begin + slot
    inside = (slot >= 0) & (slot < SLOTS) & (t < ACTIVE)
    t = jnp.where(inside, t, 0)
    block, lane = t >> 7, t & 127
    found = jnp.full((8, 128), -1, i32)
    for b in range(BLOCKS):
        row = jnp.broadcast_to(active_ref[b : b + 1, :], (8, 128))
        found = jnp.where(block == b, take_lanes(row, lane), found)
    local = found - base
    used = inside & (local >= 0) & (local < STARS)
    return jnp.where(used, local, -1), used


def split(v):
    hi = v.astype(bf16)
    return hi, (v - hi.astype(f32)).astype(bf16)


def twice(v):
    return jnp.concatenate([v, v], axis=1)


def both(v):
    hi = v.astype(bf16).astype(f32)
    return jnp.concatenate([hi, v - hi], axis=0).astype(bf16)


def dot_nn(lhs, rhs):
    return jnp.dot(lhs, rhs, preferred_element_type=f32)


def dot_nt(lhs, rhs):
    return lax.dot_general(lhs, rhs, (((1,), (1,)), ((), ())), preferred_element_type=f32)


def fold(v):
    v = v[0:8] + v[8:16]
    return v[:, 0:WIDE] + v[:, WIDE:] if v.shape[1] > WIDE else v


def cross_of(lhs, rhs):
    return (
        lhs[1] * rhs[2] - lhs[2] * rhs[1],
        lhs[2] * rhs[0] - lhs[0] * rhs[2],
        lhs[0] * rhs[1] - lhs[1] * rhs[0],
    )


def diff_x(v):
    return 0.5 * (v[2:] - v[:-2])


def diff_y(v):
    n = v.shape[1]
    return (0.5 * (pltpu.roll(v, n - 1, 1) - pltpu.roll(v, 1, 1)))[1:-1]


def diff_z(v):
    n = v.shape[2]
    return (0.5 * (pltpu.roll(v, n - 1, 2) - pltpu.roll(v, 1, 2)))[1:-1]


def curl_of(a, b, c):
    return (diff_y(c) - diff_z(b), diff_z(a) - diff_x(c), diff_x(b) - diff_y(a))


def rate_of(field, flow, resist):
    current = curl_of(*field)
    inner = tuple(v[1:-1] for v in field)
    drift = cross_of(cross_of(current, inner), inner)
    motion = cross_of(flow, inner)
    emf = tuple(m + resist * d for m, d in zip(motion, drift))
    return curl_of(*emf)


def step_kernel(
    pos_in, vel_in, accel_in, mass_in, active_in, density_in, flow_from, field_in,
    star_new, flow, field_out,
    pos, vel, accel, mass, active, brick, flow_in, res, own, zbuf, tiles, table, table_of,
    spots, homes, seen, targ, rb, sm, cm, tm, dz2, mom, kacc, pt, rows8, square, wa, wb, pa, pb,
    part, near, wind_near, r1, q1, r2, t2, r3, big,
    ins, zs, zr, ys, yr, xs, xr, hs, hr, fs, fr, zs2, zr2, ys2, yr2, xs2, xr2
):
    star, gas, y, zl, xc = place()
    loads = [
        pltpu.make_async_copy(src, dst, ins.at[n])
        for n, (src, dst) in enumerate((
            (pos_in, pos), (vel_in, vel), (accel_in, accel), (mass_in, mass), (active_in, active),
            (density_in, brick.at[3]), (field_in, brick.at[pl.ds(0, 3)]), (flow_from, flow_in),
        ))
    ]
    for load in loads:
        load.start()
    zi, zp = z_peers(y, zl, xc, gas)
    yp = y_peers(y, zl, xc, gas)
    xp = xc_peers(y, zl, xc, gas)
    sides = []
    for dx in (-1, 0, 1):
        for dy in (-1, 0, 1):
            if dx or dy:
                device = (lax.rem(star + dx + TILES, TILES), lax.rem(gas + dy + GAS, GAS))
                sides.append((dx, dy, device))
    arrived = meet(
        [p[-1] for p in zp] + [p[-1] for p in yp] + [p[-1] for p in xp] + [p[-1] for p in sides]
    )
    for load in loads[:5]:
        load.wait()
    old_acc, old_jerk = accel[0:3, :], accel[3:6, :]
    v = vel[...]
    res[0:3, :] = (
        pos[...] + time_step * v + time_step**2 / 2.0 * old_acc + time_step**3 / 6.0 * old_jerk
    )
    res[3:6, :] = v + time_step * old_acc + time_step**2 / 2.0 * old_jerk
    res[6:7, :] = mass[...]
    res[7:8, :] = jnp.zeros((1, STARS), f32)
    local, used = own_indices(active, star * GAS + gas, gas * SLOTS)
    block, lane = local >> 7, local & 127
    packed = jnp.zeros((8, 128), f32)
    for b in range(STARS // 128):
        packed = jnp.where(
            used & (block == b), take_lanes(res[:, b * 128 : (b + 1) * 128], lane), packed
        )
    own[...] = packed
    zbuf[zi] = packed
    arrived()
    zc = [
        send(own, zbuf.at[zi], zs.at[d], zr.at[d], device)
        for d, (other, ozl, device) in enumerate(zp)
    ]

    lane8 = lanes()
    edge0 = (lanes((128, 128)) * STARS).astype(f32)
    edge1 = edge0 + 128.0 * STARS
    count0 = jnp.zeros((8, 128), f32)
    count1 = jnp.zeros((8, 128), f32)
    for b in range(BLOCKS):
        row = jnp.broadcast_to(active[b : b + 1, :].astype(f32), (128, 128))
        col = jnp.transpose(row)
        less0 = jnp.where(col < edge0, 1.0, 0.0).reshape(16, 8, 128)
        less1 = jnp.where(col < edge1, 1.0, 0.0).reshape(16, 8, 128)
        count0 = count0 + jnp.sum(less0, 0)
        count1 = count1 + jnp.sum(less1, 0)
    begin0 = jnp.broadcast_to(jnp.sum(count0, 0, keepdims=True).astype(i32), (8, 128))
    begin1 = jnp.broadcast_to(jnp.sum(count1, 0, keepdims=True).astype(i32), (8, 128))
    steps = jnp.zeros((8, 128), f32)
    for half, begin in enumerate((begin0, begin1)):
        owner = lane8 + half * 128
        leaves = (owner >> 2) - 1 + (begin >> 7)
        leaves = jnp.where(((owner & 3) == 0) & (owner > 0), leaves, 1000).astype(f32)
        col = jnp.transpose(jnp.broadcast_to(leaves[0:1], (128, 128)))
        past = jnp.where(col < lanes((128, 128)).astype(f32), 1.0, 0.0).reshape(16, 8, 128)
        steps = steps + jnp.sum(past, 0)
    table[0:1, :] = begin0[0:1]
    table[1:2, :] = begin1[0:1]
    tile_of = jnp.sum(steps, 0, keepdims=True)
    table[2:3, :] = tile_of.astype(i32)
    in_block = lanes((1, 128)).astype(f32) - tile_of
    in_block = jnp.where(lanes((1, 128)) < PATH, in_block, 1000.0)
    col = jnp.transpose(jnp.broadcast_to(in_block, (128, 128)))
    past = jnp.where(col <= lanes((128, 128)).astype(f32), 1.0, 0.0).reshape(16, 8, 128)
    last = jnp.sum(jnp.sum(past, 0), 0, keepdims=True) - 1.0
    table[3:4, :] = last.astype(i32)
    table[4:8, :] = jnp.zeros((4, 128), i32)
    to_scalars = pltpu.make_async_copy(table, table_of, ins.at[8])
    to_scalars.start()
    for b in range(BLOCKS):
        act = jnp.broadcast_to(active[b : b + 1, :], (8, 128))
        owner = act >> 9
        begin = jnp.where(
            owner < 128, take_lanes(begin0, owner & 127), take_lanes(begin1, owner & 127)
        )
        spots[b] = ((owner & (GAS - 1)) * SLOTS + b * 128 + lane8 - begin) & 127
        homes[b] = owner >> 2
    to_scalars.wait()
    for copy in zc:
        copy.wait()
    for z in range(ZL):
        merged = zbuf[z * GAS]
        for g in range(1, GAS):
            merged = merged + zbuf[z * GAS + g]
        tiles[y, z, xc] = merged
    yc = [
        send(tiles.at[y, :, xc], tiles.at[y, :, xc], ys.at[d], yr.at[d], device)
        for d, (other, device) in enumerate(yp)
    ]
    square[...] = jnp.zeros((128, 128), f32)
    for q in range(STARS // 128):
        square[0:8, :] = res[:, q * 128 : (q + 1) * 128]
        turned = jnp.transpose(square[...])
        for f in range(6):
            rb[f, q * 128 : (q + 1) * 128, :] = jnp.broadcast_to(turned[:, f : f + 1], (128, 128))
    gm = res[6:7, :] * gravity
    rows8[0:1, :] = gm
    rows8[1:4, :] = gm * (res[0:3, :] - MIDDLE)
    rows8[4:7, :] = gm * res[3:6, :]
    rows8[7:8, :] = jnp.zeros((1, STARS), f32)
    sm[...] = both(rows8[...])

    for copy in yc:
        copy.wait()
    xcs = [
        send(tiles.at[:, :, xc], tiles.at[:, :, xc], xs.at[d], xr.at[d], device)
        for d, (other, device) in enumerate(xp)
    ]
    for load in loads[5:]:
        load.wait()
    x_mid = (star * NXL).astype(f32) + 0.5 * NXL
    y_mid = (gas * NYL).astype(f32) + 0.5 * NYL
    z_mid = 0.5 * NZ
    lane1 = lanes((1, 128))
    z_off = (lane1 & (NZ - 1)).astype(f32) + (0.5 - z_mid)
    rows8[4:8, :] = jnp.zeros((4, STARS), f32)
    for i in range(NXL):
        cells = twice(brick[3, i]) * gravity
        for h in range(NYL // 2):
            q, at = i * 2 + h // 2, (h % 2) * 128
            cell = jnp.where(lane1 < NZ, cells[2 * h : 2 * h + 1], cells[2 * h + 1 : 2 * h + 2])
            y_off = jnp.where(lane1 < NZ, 2 * h, 2 * h + 1).astype(f32) + (0.5 - 0.5 * NYL)
            rows8[0:1, at : at + 128] = cell
            rows8[1:2, at : at + 128] = cell * (i + 0.5 - 0.5 * NXL)
            rows8[2:3, at : at + 128] = cell * y_off
            rows8[3:4, at : at + 128] = cell * z_off
            if h % 2:
                cm[q] = both(rows8[:, 0:WIDE])

    for buffer in (wa, wb, pa, pb):
        buffer[...] = jnp.zeros((WIDE, 2 * WIDE), bf16)
    for q in range(CELL_TILES):
        kacc[q] = jnp.zeros((8, WIDE), f32)
    for copy in xcs:
        copy.wait()
    hcs = [
        send(brick, near.at[1 - dx, 1 - dy], hs.at[d], hr.at[d], device)
        for d, (dx, dy, device) in enumerate(sides)
    ]
    near[1, 1] = brick[...]

    def walk(n, now):
        for r in range(8):
            step = n * 8 + r
            tile = jnp.clip(table_of[2, step], 0, TILES - 1)
            at = jnp.clip(step - tile, 0, BLOCKS - 1)
            ty, tz, tx = tile_at(tile)
            values = take_lanes(tiles[ty, tz, tx], spots[at])
            now = jnp.where(homes[at] == tile, values, now)
            seen[step] = now
        return now

    lax.fori_loop(0, PATH // 8, walk, jnp.zeros((8, 128), f32))
    for b in range(BLOCKS):
        targ[b] = seen[jnp.clip(table_of[3, b], 0, PATH - 1)]

    def wide(p, f):
        two = jnp.concatenate([targ[2 * p, f : f + 1, :], targ[2 * p + 1, f : f + 1, :]], axis=1)
        return jnp.broadcast_to(two, (8, WIDE))

    height = lax.broadcasted_iota(i32, (NZ, WIDE), 0).astype(f32) + 0.5

    def moments(p, _):
        gm = wide(p, 6)[0:1] * gravity
        rows8[0:1, 0:WIDE] = gm
        rows8[1:2, 0:WIDE] = gm * (wide(p, 0)[0:1] - x_mid)
        rows8[2:3, 0:WIDE] = gm * (wide(p, 1)[0:1] - y_mid)
        rows8[3:4, 0:WIDE] = gm * (wide(p, 2)[0:1] - z_mid)
        tm[p] = twice(both(rows8[:, 0:WIDE]))
        depth = height - jnp.broadcast_to(wide(p, 2)[0:1], (NZ, WIDE))
        dz2[p] = depth * depth
        for f in range(3):
            mom[f, p] = jnp.zeros((8, WIDE), f32)
        return 0

    lax.fori_loop(0, WIDES, moments, 0)

    x_first, y_first = x_mid - 0.5 * NXL + 0.5, y_mid - 0.5 * NYL + 0.5

    def gas_weights(step, half, w_buf):
        p, i = lax.div(step, NXL), lax.rem(step, NXL)
        dx = (x_first + i.astype(f32)) - wide(p, 0)
        dx2 = dx * dx + soften
        ty = wide(p, 1)
        for j in range(4):
            dy = (y_first + (half * 4.0 + j)) - ty
            side = dx2 + dy * dy
            side = jnp.concatenate([side, side], axis=0)
            for g in range(NZ // 16):
                inv = lax.rsqrt(side + dz2[p, g * 16 : (g + 1) * 16, :])
                here = slice(j * NZ + g * 16, j * NZ + (g + 1) * 16)
                w_buf[here, 0:WIDE], w_buf[here, WIDE:] = split(inv * inv * inv)

    def gas_sums(step, half, w_buf):
        p, i = lax.div(step, NXL), lax.rem(step, NXL)
        q = i * 2 + half
        w = w_buf[...]
        mom[2, p] += fold(dot_nn(cm[q], w))
        kacc[q] += fold(dot_nt(tm[p], w))

    def gas_on(step, _):
        gas_sums(jnp.maximum(step - 1, 0), 1, wb)
        gas_weights(step, 0, wa)
        gas_sums(step, 0, wa)
        gas_weights(step, 1, wb)
        return 0

    lax.fori_loop(0, WIDES * NXL, gas_on, 0)
    gas_sums(jnp.int32(WIDES * NXL - 1), 1, wb)

    for q in range(CELL_TILES):
        i, half = q // 2, q % 2
        sums = kacc[q]
        for h in range(2):
            at = slice(h * 128, (h + 1) * 128)
            y_off = jnp.where(lane1 < NZ, 0, 1).astype(f32) + (half * 4 + h * 2 + 0.5 - 0.5 * NYL)
            none = sums[0:1, at]
            kick = (
                sums[1:2, at] - (i + 0.5 - 0.5 * NXL) * none,
                sums[2:3, at] - y_off * none,
                sums[3:4, at] - z_off * none,
            )
            for f in range(3):
                row = jnp.broadcast_to(kick[f], (8, 128))
                turned = pltpu.roll(row, NZ, 1)
                j = half * 4 + h * 2
                flow[f, i, j : j + 1, :] = (
                    flow_in[f, i, j : j + 1, :] + time_step * row[0:1, 0:NZ]
                )
                flow[f, i, j + 1 : j + 2, :] = (
                    flow_in[f, i, j + 1 : j + 2, :] + time_step * turned[0:1, 0:NZ]
                )

    wind_near[1, 1] = flow[...]
    fcs = [
        send(flow, wind_near.at[1 - dx, 1 - dy], fs.at[d], fr.at[d], device)
        for d, (dx, dy, device) in enumerate(sides)
    ]
    wb[...] = jnp.zeros((WIDE, 2 * WIDE), bf16)

    def star_weights(p, c, w_buf, p_buf):
        tx, ty, tz, tu, tv, tw = (jnp.concatenate([wide(p, f)] * 2, axis=0) for f in range(6))
        for g in range(WIDE // 16):
            at = pl.ds(c * WIDE + g * 16, 16)
            dx, dy, dz = twice(rb[0, at, :]) - tx, twice(rb[1, at, :]) - ty, twice(rb[2, at, :]) - tz
            ux, uy, uz = twice(rb[3, at, :]) - tu, twice(rb[4, at, :]) - tv, twice(rb[5, at, :]) - tw
            inv = lax.rsqrt(dx * dx + dy * dy + dz * dz + soften)
            inv2 = inv * inv
            w = inv2 * inv
            pull = (dx * ux + dy * uy + dz * uz) * (3.0 * inv2) * w
            here = slice(g * 16, (g + 1) * 16)
            w_buf[here, 0:WIDE], w_buf[here, WIDE:] = split(w)
            p_buf[here, 0:WIDE], p_buf[here, WIDE:] = split(pull)

    def star_sums(p, c, w_buf, p_buf):
        lhs = sm[:, c * WIDE : (c + 1) * WIDE]
        mom[0, p] += fold(dot_nn(lhs, w_buf[...]))
        mom[1, p] += fold(dot_nn(lhs, p_buf[...]))

    def stars_on(p, _):
        star_sums(jnp.maximum(p - 1, 0), 1, wb, pb)
        star_weights(p, 0, wa, pa)
        star_sums(p, 0, wa, pa)
        star_weights(p, 1, wb, pb)
        return 0

    lax.fori_loop(0, WIDES, stars_on, 0)
    star_sums(WIDES - 1, 1, wb, pb)
    def close(p, _):
        w, pull, g = mom[0, p], mom[1, p], mom[2, p]
        mids = (x_mid, y_mid, z_mid)
        for f in range(3):
            at = wide(p, f)[0:1]
            acc = (w[1 + f : 2 + f] - (at - MIDDLE) * w[0:1]) + (
                g[1 + f : 2 + f] - (at - mids[f]) * g[0:1]
            )
            jerk = (w[4 + f : 5 + f] - wide(p, 3 + f)[0:1] * w[0:1]) - (
                pull[1 + f : 2 + f] - (at - MIDDLE) * pull[0:1]
            )
            for h in range(2):
                pt[2 * p + h, f : f + 1, :] = acc[:, h * 128 : (h + 1) * 128]
                pt[2 * p + h, 3 + f : 4 + f, :] = jerk[:, h * 128 : (h + 1) * 128]
        for h in range(2):
            pt[2 * p + h, 6:8, :] = jnp.zeros((2, 128), f32)
        return 0

    lax.fori_loop(0, WIDES, close, 0)

    def expand(s, _):
        owner = s * GAS + (lane8 >> 5)
        begin = jnp.where(s < TILES // 2, take_lanes(begin0, owner & 127), take_lanes(begin1, owner & 127))
        t = jnp.minimum(begin + (lane8 & (SLOTS - 1)), ACTIVE - 1)
        block, lane = t >> 7, t & 127
        first = jnp.clip(table_of[s >> 5, (s << 2) & 127] >> 7, 0, BLOCKS - 1)
        second = jnp.minimum(first + 1, BLOCKS - 1)
        ty, tz, tx = tile_at(s)
        part[ty, tz, tx] = jnp.where(
            block == first, take_lanes(pt[first], lane), take_lanes(pt[second], lane)
        )
        return 0

    lax.fori_loop(0, TILES, expand, 0, unroll=4)

    xcs = [
        send(part.at[:, :, other], r1.at[xc], xs2.at[d], xr2.at[d], device)
        for d, (other, device) in enumerate(xp)
    ]
    r1[xc] = part[:, :, xc]

    for copy in hcs:
        copy.wait()
    for copy in fcs:
        copy.wait()
    for c in range(7):
        for dx in range(3):
            for dy in range(3):
                for i in range(NXL):
                    v = near[dx, dy, c, i] if c < 4 else wind_near[dx, dy, c - 4, i]
                    big[c, dx * NXL + i, dy * NYL : (dy + 1) * NYL, :] = twice(v)
    mag = tuple(big[c] for c in range(3))
    wind = tuple(big[4 + c] for c in range(3))
    inv = lax.rsqrt(big[3])
    resist = inv * inv * inv
    first = rate_of(mag, tuple(v[1:-1] for v in wind), resist[1:-1])
    one = tuple(m[2:-2] + field_step * r for m, r in zip(mag, first))
    second = rate_of(one, tuple(v[3:-3] for v in wind), resist[3:-3])
    for c in range(3):
        out = 0.5 * (mag[c][4:-4] + one[c][2:-2] + field_step * second[c])
        field_out[c] = out[:, NYL : 2 * NYL, 0:NZ]

    for copy in xcs:
        copy.wait()
    total = r1[0]
    for n in range(1, XC):
        total = total + r1[n]
    q1[...] = total
    ycs = [
        send(q1.at[other], r2.at[y], ys2.at[d], yr2.at[d], device)
        for d, (other, device) in enumerate(yp)
    ]
    r2[y] = q1[y]
    local, used = own_indices(active, star * GAS + gas, 0)
    for copy in ycs:
        copy.wait()
    total = r2[0]
    for n in range(1, YN):
        total = total + r2[n]
    t2[...] = total
    zcs = [
        send(t2.at[ozl], r3.at[zi], zs2.at[d], zr2.at[d], device)
        for d, (other, ozl, device) in enumerate(zp)
    ]
    r3[zi] = t2[zl]
    for copy in zcs:
        copy.wait()
    total = r3[0]
    for n in range(1, ZL * GAS):
        total = total + r3[n]
    mine = pltpu.roll(total, lax.rem(128 - gas * SLOTS, 128), 1)
    index = lanes((8, STARS))
    sums = jnp.zeros((8, STARS), f32)
    hit = jnp.zeros((8, STARS), f32)
    for s in range(MOST):
        here = index == local[:, s : s + 1]
        sums = jnp.where(here, mine[:, s : s + 1], sums)
        hit = jnp.where(here, 1.0, hit)
    is_active = hit[0:3] > 0.5
    new_acc, new_jerk = sums[0:3], sums[3:6]
    p, v = pos[...], vel[...]
    old_acc, old_jerk = accel[0:3, :], accel[3:6, :]
    vel_one = v + time_step * (old_acc + new_acc) / 2.0 + time_step**2 * (old_jerk - new_jerk) / 12.0
    pos_one = p + time_step * (v + vel_one) / 2.0 + time_step**2 * (old_acc - new_acc) / 12.0
    star_new[0:3, :] = jnp.where(is_active, pos_one, p)
    star_new[3:6, :] = jnp.where(is_active, vel_one, v)
    star_new[6:9, :] = jnp.where(is_active, new_acc, old_acc)
    star_new[9:12, :] = jnp.where(is_active, new_jerk, old_jerk)


VM = pl.BlockSpec(memory_space=pltpu.VMEM)
ANY = pl.BlockSpec(memory_space=pl.ANY)
DMA = pltpu.SemaphoreType.DMA


def body(star_pos, star_vel, star_accel, star_mass, active, density, flow_in, field_in):
    brick = (NXL, NYL, NZ)
    zn = ZL * GAS
    pairs = [DMA((n,)) for n in (zn - 1, zn - 1, YN - 1, YN - 1, XC - 1, XC - 1)]
    star_new, flow, field_out = pl.pallas_call(
        step_kernel,
        out_shape=(
            jax.ShapeDtypeStruct((12, STARS), f32),
            jax.ShapeDtypeStruct((3,) + brick, f32),
            jax.ShapeDtypeStruct((3,) + brick, f32),
        ),
        in_specs=[ANY] * 8,
        out_specs=(VM,) * 3,
        scratch_shapes=[
            pltpu.VMEM((3, STARS), f32),
            pltpu.VMEM((3, STARS), f32),
            pltpu.VMEM((6, STARS), f32),
            pltpu.VMEM((1, STARS), f32),
            pltpu.VMEM((BLOCKS, 128), i32),
            pltpu.VMEM((4,) + brick, f32),
            pltpu.VMEM((3,) + brick, f32),
            pltpu.VMEM((8, STARS), f32),
            pltpu.VMEM((8, 128), f32),
            pltpu.VMEM((zn, 8, 128), f32),
            pltpu.VMEM((YN, ZL, XC, 8, 128), f32),
            pltpu.VMEM((8, 128), i32),
            pltpu.SMEM((8, 128), i32),
            pltpu.VMEM((BLOCKS, 8, 128), i32),
            pltpu.VMEM((BLOCKS, 8, 128), i32),
            pltpu.VMEM((PATH, 8, 128), f32),
            pltpu.VMEM((BLOCKS, 8, 128), f32),
            pltpu.VMEM((6, STARS, 128), f32),
            pltpu.VMEM((16, STARS), bf16),
            pltpu.VMEM((CELL_TILES, 16, WIDE), bf16),
            pltpu.VMEM((WIDES, 16, 2 * WIDE), bf16),
            pltpu.VMEM((WIDES, NZ, WIDE), f32),
            pltpu.VMEM((3, WIDES, 8, WIDE), f32),
            pltpu.VMEM((CELL_TILES, 8, WIDE), f32),
            pltpu.VMEM((BLOCKS, 8, 128), f32),
            pltpu.VMEM((8, STARS), f32),
            pltpu.VMEM((128, 128), f32),
            pltpu.VMEM((WIDE, 2 * WIDE), bf16),
            pltpu.VMEM((WIDE, 2 * WIDE), bf16),
            pltpu.VMEM((WIDE, 2 * WIDE), bf16),
            pltpu.VMEM((WIDE, 2 * WIDE), bf16),
            pltpu.VMEM((YN, ZL, XC, 8, 128), f32),
            pltpu.VMEM((3, 3, 4) + brick, f32),
            pltpu.VMEM((3, 3, 3) + brick, f32),
            pltpu.VMEM((XC, YN, ZL, 8, 128), f32),
            pltpu.VMEM((YN, ZL, 8, 128), f32),
            pltpu.VMEM((YN, ZL, 8, 128), f32),
            pltpu.VMEM((ZL, 8, 128), f32),
            pltpu.VMEM((zn, 8, 128), f32),
            pltpu.VMEM((7, 3 * NXL, 3 * NYL, 128), f32),
            DMA((9,)), *pairs, DMA((8,)), DMA((8,)), DMA((8,)), DMA((8,)), *pairs,
        ],
        compiler_params=pltpu.CompilerParams(
            collective_id=0, has_side_effects=True, vmem_limit_bytes=63 << 20
        ),
        name="block_step",
    )(
        star_pos, star_vel, star_accel, star_mass.reshape(1, STARS),
        active.reshape(BLOCKS, 128), density, flow_in, field_in,
    )
    return (star_new, flow, field_out)


def solution(mesh):
    placed = (
        P(None, ("star", "gas")),
        P(None, ("star", "gas")),
        P(None, ("star", "gas")),
        P(("star", "gas")),
        P(),
        P("star", "gas", None),
        P(None, "star", "gas", None),
        P(None, "star", "gas", None),
    )
    return jax.shard_map(
        body,
        mesh=mesh,
        in_specs=placed,
        out_specs=(
            P(None, ("star", "gas")),
            P(None, "star", "gas", None),
            P(None, "star", "gas", None),
        ),
        check_vma=False,
    )
```

```python
import functools

import jax
import jax.numpy as jnp
from jax import lax
from jax.experimental import pallas as pl
from jax.experimental.pallas import tpu as pltpu
from jax.sharding import PartitionSpec as P

MESH = pl.DeviceIdType.MESH
gravity = 0.02
soften = 4.0
time_step = 1.5
field_step = 0.1

STARS = 512
ACTIVE = 2048
BLOCKS = ACTIVE // 128
XN, CORES, ZL, YN, GAS = 4, 2, 2, 4, 4
TILES = YN * ZL * XN * CORES
HALF = TILES // CORES
PATH = TILES + BLOCKS
SLOTS = 32
MOST = 24
NXL, NYL, NZ = 4, 8, 64
WIDE = 256
WIDES = ACTIVE // WIDE
CELL_TILES = NXL * NYL * NZ // WIDE
MIDDLE = 16.0
f32 = jnp.float32
bf16 = jnp.bfloat16
i32 = jnp.int32


def lanes(shape=(8, 128)):
    return lax.broadcasted_iota(i32, shape, len(shape) - 1)


def take_lanes(values, index):
    return jnp.take_along_axis(values, index, axis=1, mode="promise_in_bounds")


def place():
    star = lax.axis_index("star")
    gas = lax.axis_index("gas")
    core = lax.rem(star, CORES)
    x = lax.rem(lax.div(star, CORES), XN)
    zl = lax.rem(lax.div(star, CORES * XN), ZL)
    y = lax.div(star, CORES * XN * ZL)
    return star, gas, y, zl, x, core


def seat(star):
    return ((star & 1) << 5) | ((star >> 4) << 3) | (((star >> 1) & 3) << 1) | ((star >> 3) & 1)


def star_of(y, zl, x, core):
    return ((y * ZL + zl) * XN + x) * CORES + core


def z_peers(y, zl, x, core, gas):
    zi = zl * GAS + gas
    peers = []
    for d in range(1, ZL * GAS):
        other = lax.rem(zi + d, ZL * GAS)
        ozl, ogas = lax.div(other, GAS), lax.rem(other, GAS)
        peers.append((ozl, (star_of(y, ozl, x, core), ogas)))
    return zi, peers


def plane_peers(y, zl, x, core, gas):
    peers = []
    for dy in range(YN):
        for dx in range(XN):
            if dy or dx:
                oy, ox = lax.rem(y + dy, YN), lax.rem(x + dx, XN)
                peers.append((oy * XN + ox, (star_of(oy, zl, ox, core), gas)))
    return y * XN + x, peers


def meet(devices):
    barrier = pltpu.get_barrier_semaphore()
    for device in devices:
        pl.semaphore_signal(barrier, inc=1, device_id=device, device_id_type=MESH)
    return lambda: pl.semaphore_wait(barrier, len(devices))


def send(src, dst, send_sem, recv_sem, device):
    copy = pltpu.make_async_remote_copy(
        src_ref=src, dst_ref=dst, send_sem=send_sem, recv_sem=recv_sem,
        device_id=device, device_id_type=MESH,
    )
    copy.start()
    return copy


def own_indices(active_ref, rank, lane0):
    act = active_ref[...]
    base = rank * STARS
    begin = jnp.sum((act < base).astype(f32)).astype(i32)
    slot = lanes() - lane0
    t = begin + slot
    inside = (slot >= 0) & (slot < SLOTS) & (t < ACTIVE)
    t = jnp.where(inside, t, 0)
    block, lane = t >> 7, t & 127
    found = jnp.full((8, 128), -1, i32)
    for b in range(BLOCKS):
        row = jnp.broadcast_to(active_ref[b : b + 1, :], (8, 128))
        found = jnp.where(block == b, take_lanes(row, lane), found)
    local = found - base
    used = inside & (local >= 0) & (local < STARS)
    return jnp.where(used, local, -1), used


def split(v):
    hi = v.astype(bf16)
    return hi, (v - hi.astype(f32)).astype(bf16)


def twice(v):
    return jnp.concatenate([v, v], axis=1)


def both(v):
    hi = v.astype(bf16).astype(f32)
    return jnp.concatenate([hi, v - hi], axis=0).astype(bf16)


def dot_nn(lhs, rhs):
    return jnp.dot(lhs, rhs, preferred_element_type=f32)


def dot_nt(lhs, rhs):
    return lax.dot_general(lhs, rhs, (((1,), (1,)), ((), ())), preferred_element_type=f32)


def fold(v):
    v = v[0:8] + v[8:16]
    return v[:, 0:WIDE] + v[:, WIDE:] if v.shape[1] > WIDE else v


def cross_of(lhs, rhs):
    return (
        lhs[1] * rhs[2] - lhs[2] * rhs[1],
        lhs[2] * rhs[0] - lhs[0] * rhs[2],
        lhs[0] * rhs[1] - lhs[1] * rhs[0],
    )


def diff_x(v):
    return 0.5 * (v[2:] - v[:-2])


def diff_y(v):
    n = v.shape[1]
    return (0.5 * (pltpu.roll(v, n - 1, 1) - pltpu.roll(v, 1, 1)))[1:-1]


def diff_z(v):
    n = v.shape[2]
    return (0.5 * (pltpu.roll(v, n - 1, 2) - pltpu.roll(v, 1, 2)))[1:-1]


def curl_of(a, b, c):
    return (diff_y(c) - diff_z(b), diff_z(a) - diff_x(c), diff_x(b) - diff_y(a))


def rate_of(field, flow, resist):
    current = curl_of(*field)
    inner = tuple(v[1:-1] for v in field)
    drift = cross_of(cross_of(current, inner), inner)
    motion = cross_of(flow, inner)
    emf = tuple(m + resist * d for m, d in zip(motion, drift))
    return curl_of(*emf)


def step_kernel(
    pos_in, vel_in, accel_in, mass_in, active_in, density_in, flow_from, field_in,
    star_new, flow, field_out,
    pos, vel, accel, mass, active, brick, flow_in, res, own, zbuf, tiles, table, table_of,
    spots, homes, seen, targ, rb, sm, cm, tm, dz2, mom, kacc, pt, rows8, square, wa, wb, pa, pb,
    part, near, wind_near, r1, q1, r2, t2, r3, big,
    ins, zs, zr, ps, pr, cs, cr, hs, hr, fs, fr, zs2, zr2, ps2, pr2, cs2, cr2
):
    star, gas, y, zl, x, core = place()
    loads = [
        pltpu.make_async_copy(src, dst, ins.at[n])
        for n, (src, dst) in enumerate((
            (pos_in, pos), (vel_in, vel), (accel_in, accel), (mass_in, mass), (active_in, active),
            (density_in, brick.at[3]), (field_in, brick.at[pl.ds(0, 3)]), (flow_from, flow_in),
        ))
    ]
    for load in loads:
        load.start()
    zi, zp = z_peers(y, zl, x, core, gas)
    pi, pp = plane_peers(y, zl, x, core, gas)
    partner = (star_of(y, zl, x, 1 - core), gas)
    sides = []
    for dx in (-1, 0, 1):
        for dy in (-1, 0, 1):
            if dx or dy:
                device = (lax.rem(star + dx + TILES, TILES), lax.rem(gas + dy + GAS, GAS))
                sides.append((dx, dy, device))
    arrived = meet(
        [p[-1] for p in zp] + [p[-1] for p in pp] + [p[-1] for p in sides] + [partner]
    )
    for load in loads[:5]:
        load.wait()
    old_acc, old_jerk = accel[0:3, :], accel[3:6, :]
    v = vel[...]
    res[0:3, :] = (
        pos[...] + time_step * v + time_step**2 / 2.0 * old_acc + time_step**3 / 6.0 * old_jerk
    )
    res[3:6, :] = v + time_step * old_acc + time_step**2 / 2.0 * old_jerk
    res[6:7, :] = mass[...]
    res[7:8, :] = jnp.zeros((1, STARS), f32)
    local, used = own_indices(active, star * GAS + gas, gas * SLOTS)
    block, lane = local >> 7, local & 127
    packed = jnp.zeros((8, 128), f32)
    for b in range(STARS // 128):
        packed = jnp.where(
            used & (block == b), take_lanes(res[:, b * 128 : (b + 1) * 128], lane), packed
        )
    own[...] = packed
    zbuf[zi] = packed
    arrived()
    zc = [
        send(own, zbuf.at[zi], zs.at[d], zr.at[d], device)
        for d, (ozl, device) in enumerate(zp)
    ]

    lane8 = lanes()
    edge0 = (lanes((128, 128)) * STARS).astype(f32)
    edge1 = edge0 + 128.0 * STARS
    count0 = jnp.zeros((8, 128), f32)
    count1 = jnp.zeros((8, 128), f32)
    for b in range(BLOCKS):
        row = jnp.broadcast_to(active[b : b + 1, :].astype(f32), (128, 128))
        col = jnp.transpose(row)
        less0 = jnp.where(col < edge0, 1.0, 0.0).reshape(16, 8, 128)
        less1 = jnp.where(col < edge1, 1.0, 0.0).reshape(16, 8, 128)
        count0 = count0 + jnp.sum(less0, 0)
        count1 = count1 + jnp.sum(less1, 0)
    begin0 = jnp.broadcast_to(jnp.sum(count0, 0, keepdims=True).astype(i32), (8, 128))
    begin1 = jnp.broadcast_to(jnp.sum(count1, 0, keepdims=True).astype(i32), (8, 128))
    steps = jnp.zeros((8, 128), f32)
    for half, begin in enumerate((begin0, begin1)):
        owner = lane8 + half * 128
        leaves = (owner >> 2) - 1 + (begin >> 7)
        leaves = jnp.where(((owner & 3) == 0) & (owner > 0), leaves, 1000).astype(f32)
        col = jnp.transpose(jnp.broadcast_to(leaves[0:1], (128, 128)))
        past = jnp.where(col < lanes((128, 128)).astype(f32), 1.0, 0.0).reshape(16, 8, 128)
        steps = steps + jnp.sum(past, 0)
    tile_of = jnp.sum(steps, 0, keepdims=True)
    whole = jnp.clip(tile_of.astype(i32), 0, TILES - 1)
    table[0:1, :] = jnp.clip(begin0[0:1] >> 7, 0, BLOCKS - 1)
    table[1:2, :] = jnp.clip(begin1[0:1] >> 7, 0, BLOCKS - 1)
    table[2:3, :] = seat(whole)
    table[3:4, :] = jnp.clip(lanes((1, 128)) - whole, 0, BLOCKS - 1)
    in_block = lanes((1, 128)).astype(f32) - tile_of
    in_block = jnp.where(lanes((1, 128)) < PATH, in_block, 1000.0)
    col = jnp.transpose(jnp.broadcast_to(in_block, (128, 128)))
    past = jnp.where(col <= lanes((128, 128)).astype(f32), 1.0, 0.0).reshape(16, 8, 128)
    last = jnp.sum(jnp.sum(past, 0), 0, keepdims=True) - 1.0
    table[4:5, :] = jnp.clip(last.astype(i32), 0, PATH - 1)
    table[5:8, :] = jnp.zeros((3, 128), i32)
    to_scalars = pltpu.make_async_copy(table, table_of, ins.at[8])
    to_scalars.start()
    for b in range(BLOCKS):
        act = jnp.broadcast_to(active[b : b + 1, :], (8, 128))
        owner = act >> 9
        begin = jnp.where(
            owner < 128, take_lanes(begin0, owner & 127), take_lanes(begin1, owner & 127)
        )
        spots[b] = ((owner & (GAS - 1)) * SLOTS + b * 128 + lane8 - begin) & 127
        homes[b] = seat(owner >> 2)
    to_scalars.wait()
    for copy in zc:
        copy.wait()
    mine_at = core * HALF + pi * ZL
    for z in range(ZL):
        merged = zbuf[z * GAS]
        for g in range(1, GAS):
            merged = merged + zbuf[z * GAS + g]
        tiles[mine_at + z] = merged
    pair = pl.ds(mine_at, ZL)
    pcs = [
        send(tiles.at[pair], tiles.at[pair], ps.at[d], pr.at[d], device)
        for d, (other, device) in enumerate(pp)
    ]
    square[...] = jnp.zeros((128, 128), f32)
    for q in range(STARS // 128):
        square[0:8, :] = res[:, q * 128 : (q + 1) * 128]
        turned = jnp.transpose(square[...])
        for f in range(6):
            rb[f, q * 128 : (q + 1) * 128, :] = jnp.broadcast_to(turned[:, f : f + 1], (128, 128))
    gm = res[6:7, :] * gravity
    rows8[0:1, :] = gm
    rows8[1:4, :] = gm * (res[0:3, :] - MIDDLE)
    rows8[4:7, :] = gm * res[3:6, :]
    rows8[7:8, :] = jnp.zeros((1, STARS), f32)
    sm[...] = both(rows8[...])

    for copy in pcs:
        copy.wait()
    half = pl.ds(core * HALF, HALF)
    cc = send(tiles.at[half], tiles.at[half], cs.at[0], cr.at[0], partner)
    for load in loads[5:]:
        load.wait()
    x_mid = (star * NXL).astype(f32) + 0.5 * NXL
    y_mid = (gas * NYL).astype(f32) + 0.5 * NYL
    z_mid = 0.5 * NZ
    lane1 = lanes((1, 128))
    z_off = (lane1 & (NZ - 1)).astype(f32) + (0.5 - z_mid)
    rows8[4:8, :] = jnp.zeros((4, STARS), f32)
    for i in range(NXL):
        cells = twice(brick[3, i]) * gravity
        for h in range(NYL // 2):
            q, at = i * 2 + h // 2, (h % 2) * 128
            cell = jnp.where(lane1 < NZ, cells[2 * h : 2 * h + 1], cells[2 * h + 1 : 2 * h + 2])
            y_off = jnp.where(lane1 < NZ, 2 * h, 2 * h + 1).astype(f32) + (0.5 - 0.5 * NYL)
            rows8[0:1, at : at + 128] = cell
            rows8[1:2, at : at + 128] = cell * (i + 0.5 - 0.5 * NXL)
            rows8[2:3, at : at + 128] = cell * y_off
            rows8[3:4, at : at + 128] = cell * z_off
            if h % 2:
                cm[q] = both(rows8[:, 0:WIDE])

    for buffer in (wa, wb, pa, pb):
        buffer[...] = jnp.zeros((WIDE, 2 * WIDE), bf16)
    for q in range(CELL_TILES):
        kacc[q] = jnp.zeros((8, WIDE), f32)
    cc.wait()
    hcs = [
        send(brick, near.at[1 - dx, 1 - dy], hs.at[d], hr.at[d], device)
        for d, (dx, dy, device) in enumerate(sides)
    ]
    near[1, 1] = brick[...]

    now = jnp.zeros((8, 128), f32)
    for step in range(PATH - 1):
        tile = jnp.clip(table_of[2, step], 0, TILES - 1)
        at = jnp.clip(table_of[3, step], 0, BLOCKS - 1)
        now = jnp.where(homes[at] == tile, take_lanes(tiles[tile], spots[at]), now)
        seen[step] = now
    for b in range(BLOCKS):
        targ[b] = seen[jnp.clip(table_of[4, b], 0, PATH - 2)]

    def wide(p, f):
        two = jnp.concatenate([targ[2 * p, f : f + 1, :], targ[2 * p + 1, f : f + 1, :]], axis=1)
        return jnp.broadcast_to(two, (8, WIDE))

    height = lax.broadcasted_iota(i32, (NZ, WIDE), 0).astype(f32) + 0.5

    def moments(p, _):
        gm = wide(p, 6)[0:1] * gravity
        rows8[0:1, 0:WIDE] = gm
        rows8[1:2, 0:WIDE] = gm * (wide(p, 0)[0:1] - x_mid)
        rows8[2:3, 0:WIDE] = gm * (wide(p, 1)[0:1] - y_mid)
        rows8[3:4, 0:WIDE] = gm * (wide(p, 2)[0:1] - z_mid)
        tm[p] = twice(both(rows8[:, 0:WIDE]))
        depth = height - jnp.broadcast_to(wide(p, 2)[0:1], (NZ, WIDE))
        dz2[p] = depth * depth
        for f in range(3):
            mom[f, p] = jnp.zeros((8, WIDE), f32)
        return 0

    lax.fori_loop(0, WIDES, moments, 0)

    x_first, y_first = x_mid - 0.5 * NXL + 0.5, y_mid - 0.5 * NYL + 0.5

    def gas_weights(step, half, w_buf):
        p, i = lax.div(step, NXL), lax.rem(step, NXL)
        dx = (x_first + i.astype(f32)) - wide(p, 0)
        dx2 = dx * dx + soften
        ty = wide(p, 1)
        for j in range(4):
            dy = (y_first + (half * 4.0 + j)) - ty
            side = dx2 + dy * dy
            side = jnp.concatenate([side, side], axis=0)
            for g in range(NZ // 16):
                inv = lax.rsqrt(side + dz2[p, g * 16 : (g + 1) * 16, :])
                here = slice(j * NZ + g * 16, j * NZ + (g + 1) * 16)
                w_buf[here, 0:WIDE], w_buf[here, WIDE:] = split(inv * inv * inv)

    def gas_sums(step, half, w_buf):
        p, i = lax.div(step, NXL), lax.rem(step, NXL)
        q = i * 2 + half
        w = w_buf[...]
        mom[2, p] += fold(dot_nn(cm[q], w))
        kacc[q] += fold(dot_nt(tm[p], w))

    def gas_on(step, _):
        gas_sums(jnp.maximum(step - 1, 0), 1, wb)
        gas_weights(step, 0, wa)
        gas_sums(step, 0, wa)
        gas_weights(step, 1, wb)
        return 0

    lax.fori_loop(0, WIDES * NXL, gas_on, 0)
    gas_sums(jnp.int32(WIDES * NXL - 1), 1, wb)

    for q in range(CELL_TILES):
        i, half = q // 2, q % 2
        sums = kacc[q]
        for h in range(2):
            at = slice(h * 128, (h + 1) * 128)
            y_off = jnp.where(lane1 < NZ, 0, 1).astype(f32) + (half * 4 + h * 2 + 0.5 - 0.5 * NYL)
            none = sums[0:1, at]
            kick = (
                sums[1:2, at] - (i + 0.5 - 0.5 * NXL) * none,
                sums[2:3, at] - y_off * none,
                sums[3:4, at] - z_off * none,
            )
            for f in range(3):
                row = jnp.broadcast_to(kick[f], (8, 128))
                turned = pltpu.roll(row, NZ, 1)
                j = half * 4 + h * 2
                flow[f, i, j : j + 1, :] = (
                    flow_in[f, i, j : j + 1, :] + time_step * row[0:1, 0:NZ]
                )
                flow[f, i, j + 1 : j + 2, :] = (
                    flow_in[f, i, j + 1 : j + 2, :] + time_step * turned[0:1, 0:NZ]
                )

    wind_near[1, 1] = flow[...]
    fcs = [
        send(flow, wind_near.at[1 - dx, 1 - dy], fs.at[d], fr.at[d], device)
        for d, (dx, dy, device) in enumerate(sides)
    ]
    wb[...] = jnp.zeros((WIDE, 2 * WIDE), bf16)

    def star_weights(p, c, w_buf, p_buf):
        tx, ty, tz, tu, tv, tw = (jnp.concatenate([wide(p, f)] * 2, axis=0) for f in range(6))
        for g in range(WIDE // 16):
            at = pl.ds(c * WIDE + g * 16, 16)
            dx, dy, dz = twice(rb[0, at, :]) - tx, twice(rb[1, at, :]) - ty, twice(rb[2, at, :]) - tz
            ux, uy, uz = twice(rb[3, at, :]) - tu, twice(rb[4, at, :]) - tv, twice(rb[5, at, :]) - tw
            inv = lax.rsqrt(dx * dx + dy * dy + dz * dz + soften)
            inv2 = inv * inv
            w = inv2 * inv
            pull = (dx * ux + dy * uy + dz * uz) * (3.0 * inv2) * w
            here = slice(g * 16, (g + 1) * 16)
            w_buf[here, 0:WIDE], w_buf[here, WIDE:] = split(w)
            p_buf[here, 0:WIDE], p_buf[here, WIDE:] = split(pull)

    def star_sums(p, c, w_buf, p_buf):
        lhs = sm[:, c * WIDE : (c + 1) * WIDE]
        mom[0, p] += fold(dot_nn(lhs, w_buf[...]))
        mom[1, p] += fold(dot_nn(lhs, p_buf[...]))

    def stars_on(p, _):
        star_sums(jnp.maximum(p - 1, 0), 1, wb, pb)
        star_weights(p, 0, wa, pa)
        star_sums(p, 0, wa, pa)
        star_weights(p, 1, wb, pb)
        return 0

    lax.fori_loop(0, WIDES, stars_on, 0)
    star_sums(WIDES - 1, 1, wb, pb)
    def close(p, _):
        w, pull, g = mom[0, p], mom[1, p], mom[2, p]
        mids = (x_mid, y_mid, z_mid)
        for f in range(3):
            at = wide(p, f)[0:1]
            acc = (w[1 + f : 2 + f] - (at - MIDDLE) * w[0:1]) + (
                g[1 + f : 2 + f] - (at - mids[f]) * g[0:1]
            )
            jerk = (w[4 + f : 5 + f] - wide(p, 3 + f)[0:1] * w[0:1]) - (
                pull[1 + f : 2 + f] - (at - MIDDLE) * pull[0:1]
            )
            for h in range(2):
                pt[2 * p + h, f : f + 1, :] = acc[:, h * 128 : (h + 1) * 128]
                pt[2 * p + h, 3 + f : 4 + f, :] = jerk[:, h * 128 : (h + 1) * 128]
        for h in range(2):
            pt[2 * p + h, 6:8, :] = jnp.zeros((2, 128), f32)
        return 0

    lax.fori_loop(0, WIDES, close, 0)

    pt[BLOCKS] = jnp.zeros((8, 128), f32)
    for t in range(TILES):
        begin = take_lanes(begin0 if t < TILES // 2 else begin1, (lane8 >> 5) + ((t * GAS) & 127))
        slot = jnp.minimum(begin + (lane8 & (SLOTS - 1)), ACTIVE - 1)
        first = jnp.clip(table_of[t // 32, (t * GAS) & 127], 0, BLOCKS - 1)
        lane = slot & 127
        part[seat(t)] = jnp.where(
            (slot >> 7) == first, take_lanes(pt[first], lane), take_lanes(pt[first + 1], lane)
        )

    away = pl.ds((1 - core) * HALF, HALF)
    cc = send(part.at[away], r1, cs2.at[0], cr2.at[0], partner)

    cc.wait()
    q1[...] = part[pl.ds(core * HALF, HALF)] + r1[...]
    pcs = [
        send(q1.at[pl.ds(other * ZL, ZL)], r2.at[pi], ps2.at[d], pr2.at[d], device)
        for d, (other, device) in enumerate(pp)
    ]
    r2[pi] = q1[pl.ds(pi * ZL, ZL)]
    local, used = own_indices(active, star * GAS + gas, 0)

    for copy in hcs:
        copy.wait()
    for copy in fcs:
        copy.wait()
    for c in range(7):
        for dx in range(3):
            for dy in range(3):
                for i in range(NXL):
                    v = near[dx, dy, c, i] if c < 4 else wind_near[dx, dy, c - 4, i]
                    big[c, dx * NXL + i, dy * NYL : (dy + 1) * NYL, :] = twice(v)
    mag = tuple(big[c] for c in range(3))
    wind = tuple(big[4 + c] for c in range(3))
    inv = lax.rsqrt(big[3])
    resist = inv * inv * inv
    first = rate_of(mag, tuple(v[1:-1] for v in wind), resist[1:-1])
    one = tuple(m[2:-2] + field_step * r for m, r in zip(mag, first))
    second = rate_of(one, tuple(v[3:-3] for v in wind), resist[3:-3])
    for c in range(3):
        out = 0.5 * (mag[c][4:-4] + one[c][2:-2] + field_step * second[c])
        field_out[c] = out[:, NYL : 2 * NYL, 0:NZ]

    for copy in pcs:
        copy.wait()
    total = r2[0]
    for n in range(1, YN * XN):
        total = total + r2[n]
    t2[...] = total
    zcs = [
        send(t2.at[ozl], r3.at[zi], zs2.at[d], zr2.at[d], device)
        for d, (ozl, device) in enumerate(zp)
    ]
    r3[zi] = t2[zl]
    for copy in zcs:
        copy.wait()
    total = r3[0]
    for n in range(1, ZL * GAS):
        total = total + r3[n]
    mine = pltpu.roll(total, lax.rem(128 - gas * SLOTS, 128), 1)
    index = lanes((8, STARS))
    sums = jnp.zeros((8, STARS), f32)
    hit = jnp.zeros((8, STARS), f32)
    for s in range(MOST):
        here = index == local[:, s : s + 1]
        sums = jnp.where(here, mine[:, s : s + 1], sums)
        hit = jnp.where(here, 1.0, hit)
    is_active = hit[0:3] > 0.5
    new_acc, new_jerk = sums[0:3], sums[3:6]
    p, v = pos[...], vel[...]
    old_acc, old_jerk = accel[0:3, :], accel[3:6, :]
    vel_one = v + time_step * (old_acc + new_acc) / 2.0 + time_step**2 * (old_jerk - new_jerk) / 12.0
    pos_one = p + time_step * (v + vel_one) / 2.0 + time_step**2 * (old_acc - new_acc) / 12.0
    star_new[0:3, :] = jnp.where(is_active, pos_one, p)
    star_new[3:6, :] = jnp.where(is_active, vel_one, v)
    star_new[6:9, :] = jnp.where(is_active, new_acc, old_acc)
    star_new[9:12, :] = jnp.where(is_active, new_jerk, old_jerk)


VM = pl.BlockSpec(memory_space=pltpu.VMEM)
ANY = pl.BlockSpec(memory_space=pl.ANY)
DMA = pltpu.SemaphoreType.DMA


def body(star_pos, star_vel, star_accel, star_mass, active, density, flow_in, field_in):
    brick = (NXL, NYL, NZ)
    zn = ZL * GAS
    plane = YN * XN
    pairs = [DMA((n,)) for n in (zn - 1, zn - 1, plane - 1, plane - 1, 1, 1)]
    star_new, flow, field_out = pl.pallas_call(
        step_kernel,
        out_shape=(
            jax.ShapeDtypeStruct((12, STARS), f32),
            jax.ShapeDtypeStruct((3,) + brick, f32),
            jax.ShapeDtypeStruct((3,) + brick, f32),
        ),
        in_specs=[ANY] * 8,
        out_specs=(VM,) * 3,
        scratch_shapes=[
            pltpu.VMEM((3, STARS), f32),
            pltpu.VMEM((3, STARS), f32),
            pltpu.VMEM((6, STARS), f32),
            pltpu.VMEM((1, STARS), f32),
            pltpu.VMEM((BLOCKS, 128), i32),
            pltpu.VMEM((4,) + brick, f32),
            pltpu.VMEM((3,) + brick, f32),
            pltpu.VMEM((8, STARS), f32),
            pltpu.VMEM((8, 128), f32),
            pltpu.VMEM((zn, 8, 128), f32),
            pltpu.VMEM((TILES, 8, 128), f32),
            pltpu.VMEM((8, 128), i32),
            pltpu.SMEM((8, 128), i32),
            pltpu.VMEM((BLOCKS, 8, 128), i32),
            pltpu.VMEM((BLOCKS, 8, 128), i32),
            pltpu.VMEM((PATH, 8, 128), f32),
            pltpu.VMEM((BLOCKS, 8, 128), f32),
            pltpu.VMEM((6, STARS, 128), f32),
            pltpu.VMEM((16, STARS), bf16),
            pltpu.VMEM((CELL_TILES, 16, WIDE), bf16),
            pltpu.VMEM((WIDES, 16, 2 * WIDE), bf16),
            pltpu.VMEM((WIDES, NZ, WIDE), f32),
            pltpu.VMEM((3, WIDES, 8, WIDE), f32),
            pltpu.VMEM((CELL_TILES, 8, WIDE), f32),
            pltpu.VMEM((BLOCKS + 1, 8, 128), f32),
            pltpu.VMEM((8, STARS), f32),
            pltpu.VMEM((128, 128), f32),
            pltpu.VMEM((WIDE, 2 * WIDE), bf16),
            pltpu.VMEM((WIDE, 2 * WIDE), bf16),
            pltpu.VMEM((WIDE, 2 * WIDE), bf16),
            pltpu.VMEM((WIDE, 2 * WIDE), bf16),
            pltpu.VMEM((TILES, 8, 128), f32),
            pltpu.VMEM((3, 3, 4) + brick, f32),
            pltpu.VMEM((3, 3, 3) + brick, f32),
            pltpu.VMEM((HALF, 8, 128), f32),
            pltpu.VMEM((HALF, 8, 128), f32),
            pltpu.VMEM((plane, ZL, 8, 128), f32),
            pltpu.VMEM((ZL, 8, 128), f32),
            pltpu.VMEM((zn, 8, 128), f32),
            pltpu.VMEM((7, 3 * NXL, 3 * NYL, 128), f32),
            DMA((9,)), *pairs, DMA((8,)), DMA((8,)), DMA((8,)), DMA((8,)), *pairs,
        ],
        compiler_params=pltpu.CompilerParams(
            collective_id=0, has_side_effects=True, vmem_limit_bytes=63 << 20
        ),
        name="block_step",
    )(
        star_pos, star_vel, star_accel, star_mass.reshape(1, STARS),
        active.reshape(BLOCKS, 128), density, flow_in, field_in,
    )
    return (star_new, flow, field_out)


def solution(mesh):
    placed = (
        P(None, ("star", "gas")),
        P(None, ("star", "gas")),
        P(None, ("star", "gas")),
        P(("star", "gas")),
        P(),
        P("star", "gas", None),
        P(None, "star", "gas", None),
        P(None, "star", "gas", None),
    )
    return jax.shard_map(
        body,
        mesh=mesh,
        in_specs=placed,
        out_specs=(
            P(None, ("star", "gas")),
            P(None, "star", "gas", None),
            P(None, "star", "gas", None),
        ),
        check_vma=False,
    )
```

```python
import functools

import jax
import jax.numpy as jnp
from jax import lax
from jax.experimental import pallas as pl
from jax.experimental.pallas import tpu as pltpu
from jax.sharding import PartitionSpec as P

MESH = pl.DeviceIdType.MESH
gravity = 0.02
soften = 4.0
time_step = 1.5
field_step = 0.1

STARS = 512
ACTIVE = 2048
BLOCKS = ACTIVE // 128
XN, CORES, ZL, YN, GAS = 4, 2, 2, 4, 4
TILES = YN * ZL * XN * CORES
HALF = TILES // CORES
PATH = TILES + BLOCKS
SLOTS = 32
MOST = 24
NXL, NYL, NZ = 4, 8, 64
WIDE = 256
WIDES = ACTIVE // WIDE
CELL_TILES = NXL * NYL * NZ // WIDE
MIDDLE = 16.0
PART = 256
f32 = jnp.float32
bf16 = jnp.bfloat16
i32 = jnp.int32


def lanes(shape=(8, 128)):
    return lax.broadcasted_iota(i32, shape, len(shape) - 1)


def take_lanes(values, index):
    return jnp.take_along_axis(values, index, axis=1, mode="promise_in_bounds")


def place():
    star = lax.axis_index("star")
    gas = lax.axis_index("gas")
    core = lax.rem(star, CORES)
    x = lax.rem(lax.div(star, CORES), XN)
    zl = lax.rem(lax.div(star, CORES * XN), ZL)
    y = lax.div(star, CORES * XN * ZL)
    return star, gas, y, zl, x, core


def seat(star):
    return ((star & 1) << 5) | ((star >> 4) << 3) | (((star >> 1) & 3) << 1) | ((star >> 3) & 1)


def star_of(y, zl, x, core):
    return ((y * ZL + zl) * XN + x) * CORES + core


def z_peers(y, zl, x, core, gas):
    zi = zl * GAS + gas
    peers = []
    for d in range(1, ZL * GAS):
        other = lax.rem(zi + d, ZL * GAS)
        ozl, ogas = lax.div(other, GAS), lax.rem(other, GAS)
        peers.append((ozl, (star_of(y, ozl, x, core), ogas)))
    return zi, peers


def plane_peers(y, zl, x, core, gas):
    peers = []
    for dy in range(YN):
        for dx in range(XN):
            if dy or dx:
                oy, ox = lax.rem(y + dy, YN), lax.rem(x + dx, XN)
                peers.append((oy * XN + ox, (star_of(oy, zl, ox, core), gas)))
    return y * XN + x, peers


def meet(devices):
    barrier = pltpu.get_barrier_semaphore()
    for device in devices:
        pl.semaphore_signal(barrier, inc=1, device_id=device, device_id_type=MESH)
    return lambda: pl.semaphore_wait(barrier, len(devices))


def send(src, dst, send_sem, recv_sem, device):
    copy = pltpu.make_async_remote_copy(
        src_ref=src, dst_ref=dst, send_sem=send_sem, recv_sem=recv_sem,
        device_id=device, device_id_type=MESH,
    )
    copy.start()
    return copy


def own_indices(active_ref, rank, lane0):
    act = active_ref[...]
    base = rank * STARS
    begin = jnp.sum((act < base).astype(f32)).astype(i32)
    slot = lanes() - lane0
    t = begin + slot
    inside = (slot >= 0) & (slot < SLOTS) & (t < ACTIVE)
    t = jnp.where(inside, t, 0)
    block, lane = t >> 7, t & 127
    found = jnp.full((8, 128), -1, i32)
    for b in range(BLOCKS):
        row = jnp.broadcast_to(active_ref[b : b + 1, :], (8, 128))
        found = jnp.where(block == b, take_lanes(row, lane), found)
    local = found - base
    used = inside & (local >= 0) & (local < STARS)
    return jnp.where(used, local, -1), used


def split(v):
    hi = v.astype(bf16)
    return hi, (v - hi.astype(f32)).astype(bf16)


def twice(v):
    return jnp.concatenate([v, v], axis=1)


def thirds(v):
    high = v.astype(bf16).astype(f32)
    mid = (v - high).astype(bf16).astype(f32)
    return high, mid, (v - high - mid).astype(bf16).astype(f32)


def both(v):
    hi = v.astype(bf16).astype(f32)
    return jnp.concatenate([hi, v - hi], axis=0).astype(bf16)


def dot_nn(lhs, rhs):
    return jnp.dot(lhs, rhs, preferred_element_type=f32)


def dot_nt(lhs, rhs):
    return lax.dot_general(lhs, rhs, (((1,), (1,)), ((), ())), preferred_element_type=f32)


def fold(v):
    v = v[0:8] + v[8:16]
    return v[:, 0:WIDE] + v[:, WIDE:] if v.shape[1] > WIDE else v


def cross_of(lhs, rhs):
    return (
        lhs[1] * rhs[2] - lhs[2] * rhs[1],
        lhs[2] * rhs[0] - lhs[0] * rhs[2],
        lhs[0] * rhs[1] - lhs[1] * rhs[0],
    )


def diff_x(v):
    return 0.5 * (v[2:] - v[:-2])


def diff_y(v):
    n = v.shape[1]
    return (0.5 * (pltpu.roll(v, n - 1, 1) - pltpu.roll(v, 1, 1)))[1:-1]


def diff_z(v):
    n = v.shape[2]
    return (0.5 * (pltpu.roll(v, n - 1, 2) - pltpu.roll(v, 1, 2)))[1:-1]


def curl_of(a, b, c):
    return (diff_y(c) - diff_z(b), diff_z(a) - diff_x(c), diff_x(b) - diff_y(a))


def rate_of(field, flow, resist):
    current = curl_of(*field)
    inner = tuple(v[1:-1] for v in field)
    drift = cross_of(cross_of(current, inner), inner)
    motion = cross_of(flow, inner)
    emf = tuple(m + resist * d for m, d in zip(motion, drift))
    return curl_of(*emf)


def step_kernel(
    pos_in, vel_in, accel_in, mass_in, active_in, density_in, flow_from, field_in,
    star_new, flow, field_out,
    pos, vel, accel, mass, active, brick, flow_in, res, own, zbuf, tiles, table, table_of,
    spots, homes, seen, targ, ls, rt, sm, cm, tm, dz2, mom, kacc, pt, rows8, square, wa, wb, pa, pb,
    part, near, wind_near, r1, q1, r2, t2, r3, big,
    ins, zs, zr, ps, pr, cs, cr, hs, hr, fs, fr, zs2, zr2, ps2, pr2, cs2, cr2
):
    star, gas, y, zl, x, core = place()
    loads = [
        pltpu.make_async_copy(src, dst, ins.at[n])
        for n, (src, dst) in enumerate((
            (pos_in, pos), (vel_in, vel), (accel_in, accel), (mass_in, mass), (active_in, active),
            (density_in, brick.at[3]), (field_in, brick.at[pl.ds(0, 3)]), (flow_from, flow_in),
        ))
    ]
    for load in loads:
        load.start()
    zi, zp = z_peers(y, zl, x, core, gas)
    pi, pp = plane_peers(y, zl, x, core, gas)
    partner = (star_of(y, zl, x, 1 - core), gas)
    sides = []
    for dx in (-1, 0, 1):
        for dy in (-1, 0, 1):
            if dx or dy:
                device = (lax.rem(star + dx + TILES, TILES), lax.rem(gas + dy + GAS, GAS))
                sides.append((dx, dy, device))
    arrived = meet(
        [p[-1] for p in zp] + [p[-1] for p in pp] + [p[-1] for p in sides] + [partner]
    )
    for load in loads[:5]:
        load.wait()
    old_acc, old_jerk = accel[0:3, :], accel[3:6, :]
    v = vel[...]
    res[0:3, :] = (
        pos[...] + time_step * v + time_step**2 / 2.0 * old_acc + time_step**3 / 6.0 * old_jerk
    )
    res[3:6, :] = v + time_step * old_acc + time_step**2 / 2.0 * old_jerk
    res[6:7, :] = mass[...]
    res[7:8, :] = jnp.zeros((1, STARS), f32)
    local, used = own_indices(active, star * GAS + gas, gas * SLOTS)
    block, lane = local >> 7, local & 127
    packed = jnp.zeros((8, 128), f32)
    for b in range(STARS // 128):
        packed = jnp.where(
            used & (block == b), take_lanes(res[:, b * 128 : (b + 1) * 128], lane), packed
        )
    own[...] = packed
    zbuf[zi] = packed
    arrived()
    zc = [
        send(own, zbuf.at[zi], zs.at[d], zr.at[d], device)
        for d, (ozl, device) in enumerate(zp)
    ]

    lane8 = lanes()
    edge0 = (lanes((128, 128)) * STARS).astype(f32)
    edge1 = edge0 + 128.0 * STARS
    count0 = jnp.zeros((8, 128), f32)
    count1 = jnp.zeros((8, 128), f32)
    for b in range(BLOCKS):
        row = jnp.broadcast_to(active[b : b + 1, :].astype(f32), (128, 128))
        col = jnp.transpose(row)
        less0 = jnp.where(col < edge0, 1.0, 0.0).reshape(16, 8, 128)
        less1 = jnp.where(col < edge1, 1.0, 0.0).reshape(16, 8, 128)
        count0 = count0 + jnp.sum(less0, 0)
        count1 = count1 + jnp.sum(less1, 0)
    begin0 = jnp.broadcast_to(jnp.sum(count0, 0, keepdims=True).astype(i32), (8, 128))
    begin1 = jnp.broadcast_to(jnp.sum(count1, 0, keepdims=True).astype(i32), (8, 128))
    steps = jnp.zeros((8, 128), f32)
    for half, begin in enumerate((begin0, begin1)):
        owner = lane8 + half * 128
        leaves = (owner >> 2) - 1 + (begin >> 7)
        leaves = jnp.where(((owner & 3) == 0) & (owner > 0), leaves, 1000).astype(f32)
        col = jnp.transpose(jnp.broadcast_to(leaves[0:1], (128, 128)))
        past = jnp.where(col < lanes((128, 128)).astype(f32), 1.0, 0.0).reshape(16, 8, 128)
        steps = steps + jnp.sum(past, 0)
    tile_of = jnp.sum(steps, 0, keepdims=True)
    whole = jnp.clip(tile_of.astype(i32), 0, TILES - 1)
    table[0:1, :] = jnp.clip(begin0[0:1] >> 7, 0, BLOCKS - 1)
    table[1:2, :] = jnp.clip(begin1[0:1] >> 7, 0, BLOCKS - 1)
    table[2:3, :] = seat(whole)
    table[3:4, :] = jnp.clip(lanes((1, 128)) - whole, 0, BLOCKS - 1)
    in_block = lanes((1, 128)).astype(f32) - tile_of
    in_block = jnp.where(lanes((1, 128)) < PATH, in_block, 1000.0)
    col = jnp.transpose(jnp.broadcast_to(in_block, (128, 128)))
    past = jnp.where(col <= lanes((128, 128)).astype(f32), 1.0, 0.0).reshape(16, 8, 128)
    last = jnp.sum(jnp.sum(past, 0), 0, keepdims=True) - 1.0
    table[4:5, :] = jnp.clip(last.astype(i32), 0, PATH - 1)
    table[5:8, :] = jnp.zeros((3, 128), i32)
    to_scalars = pltpu.make_async_copy(table, table_of, ins.at[8])
    to_scalars.start()
    for b in range(BLOCKS):
        act = jnp.broadcast_to(active[b : b + 1, :], (8, 128))
        owner = act >> 9
        begin = jnp.where(
            owner < 128, take_lanes(begin0, owner & 127), take_lanes(begin1, owner & 127)
        )
        spots[b] = ((owner & (GAS - 1)) * SLOTS + b * 128 + lane8 - begin) & 127
        homes[b] = seat(owner >> 2)
    to_scalars.wait()
    for copy in zc:
        copy.wait()
    mine_at = core * HALF + pi * ZL
    for z in range(ZL):
        merged = zbuf[z * GAS]
        for g in range(1, GAS):
            merged = merged + zbuf[z * GAS + g]
        tiles[mine_at + z] = merged
    pair = pl.ds(mine_at, ZL)
    pcs = [
        send(tiles.at[pair], tiles.at[pair], ps.at[d], pr.at[d], device)
        for d, (other, device) in enumerate(pp)
    ]
    away_x = res[0:3, :] - MIDDLE
    rows8[0:3, :] = away_x
    rows8[3:6, :] = res[3:6, :]
    rows8[6:7, :] = jnp.sum(away_x * res[3:6, :], 0, keepdims=True)
    rows8[7:8, :] = jnp.sum(away_x * away_x, 0, keepdims=True)
    high, mid, low = thirds(rows8[...])
    ones = jnp.where(lax.broadcasted_iota(i32, (8, 128), 0) < 3, 1.0, 0.0)
    square[...] = jnp.zeros((128, 128), f32)
    for q in range(STARS // 128):
        at = slice(q * 128, (q + 1) * 128)
        for n, part_of in enumerate((high, high, high, mid, mid, low)):
            square[n * 8 : (n + 1) * 8, :] = part_of[:, at]
        square[48:56, :] = ones
        ls[at, :] = jnp.transpose(square[...]).astype(bf16)
    square[...] = jnp.zeros((128, 128), f32)
    gm = res[6:7, :] * gravity
    rows8[0:1, :] = gm
    rows8[1:4, :] = gm * (res[0:3, :] - MIDDLE)
    rows8[4:7, :] = gm * res[3:6, :]
    rows8[7:8, :] = jnp.zeros((1, STARS), f32)
    sm[...] = both(rows8[...])

    for copy in pcs:
        copy.wait()
    half = pl.ds(core * HALF, HALF)
    cc = send(tiles.at[half], tiles.at[half], cs.at[0], cr.at[0], partner)
    for load in loads[5:]:
        load.wait()
    x_mid = (star * NXL).astype(f32) + 0.5 * NXL
    y_mid = (gas * NYL).astype(f32) + 0.5 * NYL
    z_mid = 0.5 * NZ
    lane1 = lanes((1, 128))
    z_off = (lane1 & (NZ - 1)).astype(f32) + (0.5 - z_mid)
    rows8[4:8, :] = jnp.zeros((4, STARS), f32)
    for i in range(NXL):
        cells = twice(brick[3, i]) * gravity
        for h in range(NYL // 2):
            q, at = i * 2 + h // 2, (h % 2) * 128
            cell = jnp.where(lane1 < NZ, cells[2 * h : 2 * h + 1], cells[2 * h + 1 : 2 * h + 2])
            y_off = jnp.where(lane1 < NZ, 2 * h, 2 * h + 1).astype(f32) + (0.5 - 0.5 * NYL)
            rows8[0:1, at : at + 128] = cell
            rows8[1:2, at : at + 128] = cell * (i + 0.5 - 0.5 * NXL)
            rows8[2:3, at : at + 128] = cell * y_off
            rows8[3:4, at : at + 128] = cell * z_off
            if h % 2:
                cm[q] = both(rows8[:, 0:WIDE])

    for buffer in (wa, wb, pa, pb):
        buffer[...] = jnp.zeros((WIDE, 2 * WIDE), bf16)
    for q in range(CELL_TILES):
        kacc[q] = jnp.zeros((8, WIDE), f32)
    cc.wait()
    hcs = [
        send(brick, near.at[1 - dx, 1 - dy], hs.at[d], hr.at[d], device)
        for d, (dx, dy, device) in enumerate(sides)
    ]
    near[1, 1] = brick[...]

    now = jnp.zeros((8, 128), f32)
    for step in range(PATH - 1):
        tile = jnp.clip(table_of[2, step], 0, TILES - 1)
        at = jnp.clip(table_of[3, step], 0, BLOCKS - 1)
        now = jnp.where(homes[at] == tile, take_lanes(tiles[tile], spots[at]), now)
        seen[step] = now
    for b in range(BLOCKS):
        targ[b] = seen[jnp.clip(table_of[4, b], 0, PATH - 2)]

    def wide(p, f):
        two = jnp.concatenate([targ[2 * p, f : f + 1, :], targ[2 * p + 1, f : f + 1, :]], axis=1)
        return jnp.broadcast_to(two, (8, WIDE))

    height = lax.broadcasted_iota(i32, (NZ, WIDE), 0).astype(f32) + 0.5

    row_of = lax.broadcasted_iota(i32, (8, WIDE), 0)

    def moments(p, _):
        gm = wide(p, 6)[0:1] * gravity
        rows8[0:1, 0:WIDE] = gm
        rows8[1:2, 0:WIDE] = gm * (wide(p, 0)[0:1] - x_mid)
        rows8[2:3, 0:WIDE] = gm * (wide(p, 1)[0:1] - y_mid)
        rows8[3:4, 0:WIDE] = gm * (wide(p, 2)[0:1] - z_mid)
        tm[p] = twice(both(rows8[:, 0:WIDE]))
        block = jnp.concatenate([targ[2 * p], targ[2 * p + 1]], axis=1)
        away = jnp.where(row_of < 3, block - MIDDLE, block)
        swap = jnp.where(row_of < 3, pltpu.roll(away, 5, 0), pltpu.roll(away, 3, 0))
        apart = jnp.where(row_of < 6, -swap, jnp.where(row_of == 6, 1.0, 0.0))
        near_by = jnp.where(row_of < 3, -2.0 * away, jnp.where(row_of == 7, 1.0, 0.0))
        factors = thirds(jnp.concatenate([apart, near_by], axis=1))
        for n, k in enumerate((0, 1, 2, 0, 1, 0)):
            if n % 2 == 0:
                m = (0, 1, 2, 0, 1, 0)[n + 1]
                rt[p, n * 8 : (n + 2) * 8, :] = jnp.concatenate(
                    [factors[k], factors[m]], axis=0
                ).astype(bf16)
        first3 = row_of < 3
        self_u = jnp.sum(jnp.where(first3, away * swap, 0.0), 0, keepdims=True)
        self_d = jnp.sum(jnp.where(first3, away * away, 0.0), 0, keepdims=True) + soften
        tail = thirds(jnp.broadcast_to(jnp.concatenate([self_u, self_d], axis=1), (8, 2 * WIDE)))
        row2 = jnp.concatenate([row_of, row_of], axis=1)
        tail = jnp.where(
            row2 == 0, tail[0], jnp.where(row2 == 1, tail[1], jnp.where(row2 == 2, tail[2], 0.0))
        )
        rt[p, 48:64, :] = jnp.concatenate([tail, jnp.zeros_like(tail)], axis=0).astype(bf16)
        depth = height - jnp.broadcast_to(wide(p, 2)[0:1], (NZ, WIDE))
        dz2[p] = depth * depth
        for f in range(3):
            mom[f, p] = jnp.zeros((8, WIDE), f32)
        return 0

    lax.fori_loop(0, WIDES, moments, 0)

    x_first, y_first = x_mid - 0.5 * NXL + 0.5, y_mid - 0.5 * NYL + 0.5

    def gas_weights(step, half, w_buf):
        p, i = lax.div(step, NXL), lax.rem(step, NXL)
        dx = (x_first + i.astype(f32)) - wide(p, 0)
        dx2 = dx * dx + soften
        ty = wide(p, 1)
        for j in range(4):
            dy = (y_first + (half * 4.0 + j)) - ty
            side = dx2 + dy * dy
            side = jnp.concatenate([side, side], axis=0)
            for g in range(NZ // 16):
                inv = lax.rsqrt(side + dz2[p, g * 16 : (g + 1) * 16, :])
                here = slice(j * NZ + g * 16, j * NZ + (g + 1) * 16)
                w_buf[here, 0:WIDE], w_buf[here, WIDE:] = split(inv * inv * inv)

    def gas_sums(step, half, w_buf):
        p, i = lax.div(step, NXL), lax.rem(step, NXL)
        q = i * 2 + half
        w = w_buf[...]
        mom[2, p] += fold(dot_nn(cm[q], w[:, 0:WIDE]))
        kacc[q] += fold(dot_nt(tm[p], w))

    def gas_on(step, _):
        gas_sums(jnp.maximum(step - 1, 0), 1, wb)
        gas_weights(step, 0, wa)
        gas_sums(step, 0, wa)
        gas_weights(step, 1, wb)
        return 0

    lax.fori_loop(0, WIDES * NXL, gas_on, 0)
    gas_sums(jnp.int32(WIDES * NXL - 1), 1, wb)

    for q in range(CELL_TILES):
        i, half = q // 2, q % 2
        sums = kacc[q]
        for h in range(2):
            at = slice(h * 128, (h + 1) * 128)
            y_off = jnp.where(lane1 < NZ, 0, 1).astype(f32) + (half * 4 + h * 2 + 0.5 - 0.5 * NYL)
            none = sums[0:1, at]
            kick = (
                sums[1:2, at] - (i + 0.5 - 0.5 * NXL) * none,
                sums[2:3, at] - y_off * none,
                sums[3:4, at] - z_off * none,
            )
            for f in range(3):
                row = jnp.broadcast_to(kick[f], (8, 128))
                turned = pltpu.roll(row, NZ, 1)
                j = half * 4 + h * 2
                flow[f, i, j : j + 1, :] = (
                    flow_in[f, i, j : j + 1, :] + time_step * row[0:1, 0:NZ]
                )
                flow[f, i, j + 1 : j + 2, :] = (
                    flow_in[f, i, j + 1 : j + 2, :] + time_step * turned[0:1, 0:NZ]
                )

    wind_near[1, 1] = flow[...]
    fcs = [
        send(flow, wind_near.at[1 - dx, 1 - dy], fs.at[d], fr.at[d], device)
        for d, (dx, dy, device) in enumerate(sides)
    ]
    wb[...] = jnp.zeros((WIDE, 2 * WIDE), bf16)

    def star_weights(p, c, w_buf, p_buf):
        for m in range(WIDE // PART):
            rows = slice(c * WIDE + m * PART, c * WIDE + (m + 1) * PART)
            products = dot_nn(ls[rows, 0:64], rt[p])
            for g in range(PART // 16):
                at = slice(g * 16, (g + 1) * 16)
                inv = lax.rsqrt(products[at, WIDE:])
                inv2 = inv * inv
                w = inv2 * inv
                pull = products[at, 0:WIDE] * inv2 * w
                here = slice(m * PART + g * 16, m * PART + (g + 1) * 16)
                w_buf[here, 0:WIDE], w_buf[here, WIDE:] = split(w)
                p_buf[here, 0:WIDE], p_buf[here, WIDE:] = split(pull)

    def star_sums(p, c, w_buf, p_buf):
        lhs = sm[:, c * WIDE : (c + 1) * WIDE]
        mom[0, p] += fold(dot_nn(lhs, w_buf[...]))
        mom[1, p] += fold(dot_nn(lhs, p_buf[...]))

    def stars_on(p, _):
        star_sums(jnp.maximum(p - 1, 0), 1, wb, pb)
        star_weights(p, 0, wa, pa)
        star_sums(p, 0, wa, pa)
        star_weights(p, 1, wb, pb)
        return 0

    lax.fori_loop(0, WIDES, stars_on, 0)
    star_sums(WIDES - 1, 1, wb, pb)
    def close(p, _):
        w, pull, g = mom[0, p], 3.0 * mom[1, p], mom[2, p]
        mids = (x_mid, y_mid, z_mid)
        for f in range(3):
            at = wide(p, f)[0:1]
            acc = (w[1 + f : 2 + f] - (at - MIDDLE) * w[0:1]) + (
                g[1 + f : 2 + f] - (at - mids[f]) * g[0:1]
            )
            jerk = (w[4 + f : 5 + f] - wide(p, 3 + f)[0:1] * w[0:1]) - (
                pull[1 + f : 2 + f] - (at - MIDDLE) * pull[0:1]
            )
            for h in range(2):
                pt[2 * p + h, f : f + 1, :] = acc[:, h * 128 : (h + 1) * 128]
                pt[2 * p + h, 3 + f : 4 + f, :] = jerk[:, h * 128 : (h + 1) * 128]
        for h in range(2):
            pt[2 * p + h, 6:8, :] = jnp.zeros((2, 128), f32)
        return 0

    lax.fori_loop(0, WIDES, close, 0)

    pt[BLOCKS] = jnp.zeros((8, 128), f32)
    for t in range(TILES):
        begin = take_lanes(begin0 if t < TILES // 2 else begin1, (lane8 >> 5) + ((t * GAS) & 127))
        slot = jnp.minimum(begin + (lane8 & (SLOTS - 1)), ACTIVE - 1)
        first = jnp.clip(table_of[t // 32, (t * GAS) & 127], 0, BLOCKS - 1)
        lane = slot & 127
        part[seat(t)] = jnp.where(
            (slot >> 7) == first, take_lanes(pt[first], lane), take_lanes(pt[first + 1], lane)
        )

    away = pl.ds((1 - core) * HALF, HALF)
    cc = send(part.at[away], r1, cs2.at[0], cr2.at[0], partner)

    cc.wait()
    q1[...] = part[pl.ds(core * HALF, HALF)] + r1[...]
    pcs = [
        send(q1.at[pl.ds(other * ZL, ZL)], r2.at[pi], ps2.at[d], pr2.at[d], device)
        for d, (other, device) in enumerate(pp)
    ]
    r2[pi] = q1[pl.ds(pi * ZL, ZL)]
    local, used = own_indices(active, star * GAS + gas, 0)

    for copy in hcs:
        copy.wait()
    for copy in fcs:
        copy.wait()
    for c in range(7):
        for dx in range(3):
            for dy in range(3):
                for i in range(NXL):
                    v = near[dx, dy, c, i] if c < 4 else wind_near[dx, dy, c - 4, i]
                    big[c, dx * NXL + i, dy * NYL : (dy + 1) * NYL, :] = twice(v)
    mag = tuple(big[c] for c in range(3))
    wind = tuple(big[4 + c] for c in range(3))
    inv = lax.rsqrt(big[3])
    resist = inv * inv * inv
    first = rate_of(mag, tuple(v[1:-1] for v in wind), resist[1:-1])
    one = tuple(m[2:-2] + field_step * r for m, r in zip(mag, first))
    second = rate_of(one, tuple(v[3:-3] for v in wind), resist[3:-3])
    for c in range(3):
        out = 0.5 * (mag[c][4:-4] + one[c][2:-2] + field_step * second[c])
        field_out[c] = out[:, NYL : 2 * NYL, 0:NZ]

    for copy in pcs:
        copy.wait()
    total = r2[0]
    for n in range(1, YN * XN):
        total = total + r2[n]
    t2[...] = total
    zcs = [
        send(t2.at[ozl], r3.at[zi], zs2.at[d], zr2.at[d], device)
        for d, (ozl, device) in enumerate(zp)
    ]
    r3[zi] = t2[zl]
    for copy in zcs:
        copy.wait()
    total = r3[0]
    for n in range(1, ZL * GAS):
        total = total + r3[n]
    mine = pltpu.roll(total, lax.rem(128 - gas * SLOTS, 128), 1)
    index = lanes((8, STARS))
    sums = jnp.zeros((8, STARS), f32)
    hit = jnp.zeros((8, STARS), f32)
    for s in range(MOST):
        here = index == local[:, s : s + 1]
        sums = jnp.where(here, mine[:, s : s + 1], sums)
        hit = jnp.where(here, 1.0, hit)
    is_active = hit[0:3] > 0.5
    new_acc, new_jerk = sums[0:3], sums[3:6]
    p, v = pos[...], vel[...]
    old_acc, old_jerk = accel[0:3, :], accel[3:6, :]
    vel_one = v + time_step * (old_acc + new_acc) / 2.0 + time_step**2 * (old_jerk - new_jerk) / 12.0
    pos_one = p + time_step * (v + vel_one) / 2.0 + time_step**2 * (old_acc - new_acc) / 12.0
    star_new[0:3, :] = jnp.where(is_active, pos_one, p)
    star_new[3:6, :] = jnp.where(is_active, vel_one, v)
    star_new[6:9, :] = jnp.where(is_active, new_acc, old_acc)
    star_new[9:12, :] = jnp.where(is_active, new_jerk, old_jerk)


VM = pl.BlockSpec(memory_space=pltpu.VMEM)
ANY = pl.BlockSpec(memory_space=pl.ANY)
DMA = pltpu.SemaphoreType.DMA


def body(star_pos, star_vel, star_accel, star_mass, active, density, flow_in, field_in):
    brick = (NXL, NYL, NZ)
    zn = ZL * GAS
    plane = YN * XN
    pairs = [DMA((n,)) for n in (zn - 1, zn - 1, plane - 1, plane - 1, 1, 1)]
    star_new, flow, field_out = pl.pallas_call(
        step_kernel,
        out_shape=(
            jax.ShapeDtypeStruct((12, STARS), f32),
            jax.ShapeDtypeStruct((3,) + brick, f32),
            jax.ShapeDtypeStruct((3,) + brick, f32),
        ),
        in_specs=[ANY] * 8,
        out_specs=(VM,) * 3,
        scratch_shapes=[
            pltpu.VMEM((3, STARS), f32),
            pltpu.VMEM((3, STARS), f32),
            pltpu.VMEM((6, STARS), f32),
            pltpu.VMEM((1, STARS), f32),
            pltpu.VMEM((BLOCKS, 128), i32),
            pltpu.VMEM((4,) + brick, f32),
            pltpu.VMEM((3,) + brick, f32),
            pltpu.VMEM((8, STARS), f32),
            pltpu.VMEM((8, 128), f32),
            pltpu.VMEM((zn, 8, 128), f32),
            pltpu.VMEM((TILES, 8, 128), f32),
            pltpu.VMEM((8, 128), i32),
            pltpu.SMEM((8, 128), i32),
            pltpu.VMEM((BLOCKS, 8, 128), i32),
            pltpu.VMEM((BLOCKS, 8, 128), i32),
            pltpu.VMEM((PATH, 8, 128), f32),
            pltpu.VMEM((BLOCKS, 8, 128), f32),
            pltpu.VMEM((STARS, 128), bf16),
            pltpu.VMEM((WIDES, 64, 2 * WIDE), bf16),
            pltpu.VMEM((16, STARS), bf16),
            pltpu.VMEM((CELL_TILES, 16, WIDE), bf16),
            pltpu.VMEM((WIDES, 16, 2 * WIDE), bf16),
            pltpu.VMEM((WIDES, NZ, WIDE), f32),
            pltpu.VMEM((3, WIDES, 8, WIDE), f32),
            pltpu.VMEM((CELL_TILES, 8, WIDE), f32),
            pltpu.VMEM((BLOCKS + 1, 8, 128), f32),
            pltpu.VMEM((8, STARS), f32),
            pltpu.VMEM((128, 128), f32),
            pltpu.VMEM((WIDE, 2 * WIDE), bf16),
            pltpu.VMEM((WIDE, 2 * WIDE), bf16),
            pltpu.VMEM((WIDE, 2 * WIDE), bf16),
            pltpu.VMEM((WIDE, 2 * WIDE), bf16),
            pltpu.VMEM((TILES, 8, 128), f32),
            pltpu.VMEM((3, 3, 4) + brick, f32),
            pltpu.VMEM((3, 3, 3) + brick, f32),
            pltpu.VMEM((HALF, 8, 128), f32),
            pltpu.VMEM((HALF, 8, 128), f32),
            pltpu.VMEM((plane, ZL, 8, 128), f32),
            pltpu.VMEM((ZL, 8, 128), f32),
            pltpu.VMEM((zn, 8, 128), f32),
            pltpu.VMEM((7, 3 * NXL, 3 * NYL, 128), f32),
            DMA((9,)), *pairs, DMA((8,)), DMA((8,)), DMA((8,)), DMA((8,)), *pairs,
        ],
        compiler_params=pltpu.CompilerParams(
            collective_id=0, has_side_effects=True, vmem_limit_bytes=63 << 20
        ),
        name="block_step",
    )(
        star_pos, star_vel, star_accel, star_mass.reshape(1, STARS),
        active.reshape(BLOCKS, 128), density, flow_in, field_in,
    )
    return (star_new, flow, field_out)


def solution(mesh):
    placed = (
        P(None, ("star", "gas")),
        P(None, ("star", "gas")),
        P(None, ("star", "gas")),
        P(("star", "gas")),
        P(),
        P("star", "gas", None),
        P(None, "star", "gas", None),
        P(None, "star", "gas", None),
    )
    return jax.shard_map(
        body,
        mesh=mesh,
        in_specs=placed,
        out_specs=(
            P(None, ("star", "gas")),
            P(None, "star", "gas", None),
            P(None, "star", "gas", None),
        ),
        check_vma=False,
    )
```

```python
import functools

import jax
import jax.numpy as jnp
from jax import lax
from jax.experimental import pallas as pl
from jax.experimental.pallas import tpu as pltpu
from jax.sharding import PartitionSpec as P

MESH = pl.DeviceIdType.MESH
gravity = 0.02
soften = 4.0
time_step = 1.5
field_step = 0.1

STARS = 512
ACTIVE = 2048
BLOCKS = ACTIVE // 128
XN, CORES, ZL, YN, GAS = 4, 2, 2, 4, 4
TILES = YN * ZL * XN * CORES
HALF = TILES // CORES
PATH = TILES + BLOCKS
SLOTS = 32
MOST = 24
NXL, NYL, NZ = 4, 8, 64
WIDE = 256
WIDES = ACTIVE // WIDE
CELL_TILES = NXL * NYL * NZ // WIDE
MIDDLE = 16.0
PART = 256
f32 = jnp.float32
bf16 = jnp.bfloat16
i32 = jnp.int32


def lanes(shape=(8, 128)):
    return lax.broadcasted_iota(i32, shape, len(shape) - 1)


def take_lanes(values, index):
    return jnp.take_along_axis(values, index, axis=1, mode="promise_in_bounds")


def place():
    star = lax.axis_index("star")
    gas = lax.axis_index("gas")
    core = lax.rem(star, CORES)
    x = lax.rem(lax.div(star, CORES), XN)
    zl = lax.rem(lax.div(star, CORES * XN), ZL)
    y = lax.div(star, CORES * XN * ZL)
    return star, gas, y, zl, x, core


def seat(star):
    return ((star & 1) << 5) | ((star >> 4) << 3) | (((star >> 1) & 3) << 1) | ((star >> 3) & 1)


def star_of(y, zl, x, core):
    return ((y * ZL + zl) * XN + x) * CORES + core


def z_peers(y, zl, x, core, gas):
    zi = zl * GAS + gas
    peers = []
    for d in range(1, ZL * GAS):
        other = lax.rem(zi + d, ZL * GAS)
        ozl, ogas = lax.div(other, GAS), lax.rem(other, GAS)
        peers.append((ozl, (star_of(y, ozl, x, core), ogas)))
    return zi, peers


def plane_peers(y, zl, x, core, gas):
    peers = []
    for dy in range(YN):
        for dx in range(XN):
            if dy or dx:
                oy, ox = lax.rem(y + dy, YN), lax.rem(x + dx, XN)
                peers.append((oy * XN + ox, (star_of(oy, zl, ox, core), gas)))
    return y * XN + x, peers


def meet(devices):
    barrier = pltpu.get_barrier_semaphore()
    for device in devices:
        pl.semaphore_signal(barrier, inc=1, device_id=device, device_id_type=MESH)
    return lambda: pl.semaphore_wait(barrier, len(devices))


def send(src, dst, send_sem, recv_sem, device):
    copy = pltpu.make_async_remote_copy(
        src_ref=src, dst_ref=dst, send_sem=send_sem, recv_sem=recv_sem,
        device_id=device, device_id_type=MESH,
    )
    copy.start()
    return copy


def own_indices(active_ref, rank, lane0):
    act = active_ref[...]
    base = rank * STARS
    begin = jnp.sum((act < base).astype(f32)).astype(i32)
    slot = lanes() - lane0
    t = begin + slot
    inside = (slot >= 0) & (slot < SLOTS) & (t < ACTIVE)
    t = jnp.where(inside, t, 0)
    block, lane = t >> 7, t & 127
    found = jnp.full((8, 128), -1, i32)
    for b in range(BLOCKS):
        row = jnp.broadcast_to(active_ref[b : b + 1, :], (8, 128))
        found = jnp.where(block == b, take_lanes(row, lane), found)
    local = found - base
    used = inside & (local >= 0) & (local < STARS)
    return jnp.where(used, local, -1), used


def split(v):
    hi = v.astype(bf16)
    return hi, (v - hi.astype(f32)).astype(bf16)


def twice(v):
    return jnp.concatenate([v, v], axis=1)


def thirds(v):
    high = v.astype(bf16).astype(f32)
    mid = (v - high).astype(bf16).astype(f32)
    return high, mid, (v - high - mid).astype(bf16).astype(f32)


def both(v):
    hi = v.astype(bf16).astype(f32)
    return jnp.concatenate([hi, v - hi], axis=0).astype(bf16)


def dot_nn(lhs, rhs):
    return jnp.dot(lhs, rhs, preferred_element_type=f32)


def dot_nt(lhs, rhs):
    return lax.dot_general(lhs, rhs, (((1,), (1,)), ((), ())), preferred_element_type=f32)


def fold(v):
    v = v[0:8] + v[8:16]
    return v[:, 0:WIDE] + v[:, WIDE:] if v.shape[1] > WIDE else v


def cross_of(lhs, rhs):
    return (
        lhs[1] * rhs[2] - lhs[2] * rhs[1],
        lhs[2] * rhs[0] - lhs[0] * rhs[2],
        lhs[0] * rhs[1] - lhs[1] * rhs[0],
    )


def diff_x(v):
    return 0.5 * (v[2:] - v[:-2])


def diff_y(v):
    n = v.shape[1]
    return (0.5 * (pltpu.roll(v, n - 1, 1) - pltpu.roll(v, 1, 1)))[1:-1]


def diff_z(v):
    n = v.shape[2]
    return (0.5 * (pltpu.roll(v, n - 1, 2) - pltpu.roll(v, 1, 2)))[1:-1]


def curl_of(a, b, c):
    return (diff_y(c) - diff_z(b), diff_z(a) - diff_x(c), diff_x(b) - diff_y(a))


def rate_of(field, flow, resist):
    current = curl_of(*field)
    inner = tuple(v[1:-1] for v in field)
    drift = cross_of(cross_of(current, inner), inner)
    motion = cross_of(flow, inner)
    emf = tuple(m + resist * d for m, d in zip(motion, drift))
    return curl_of(*emf)


def step_kernel(
    pos_in, vel_in, accel_in, mass_in, active_in, density_in, flow_from, field_in,
    star_new, flow, field_out,
    pos, vel, accel, mass, active, brick, flow_in, res, own, zbuf, tiles, table, table_of,
    spots, homes, seen, targ, ls, rt, sm, cm, tm, dz2, mom, kacc, pt, rows8, square, wa, wb, pa, pb,
    part, near, wind_near, r1, q1, r2, t2, r3, big,
    ins, zs, zr, ps, pr, cs, cr, hs, hr, fs, fr, zs2, zr2, ps2, pr2, cs2, cr2
):
    star, gas, y, zl, x, core = place()
    loads = [
        pltpu.make_async_copy(src, dst, ins.at[n])
        for n, (src, dst) in enumerate((
            (pos_in, pos), (vel_in, vel), (accel_in, accel), (mass_in, mass), (active_in, active),
            (density_in, brick.at[3]), (field_in, brick.at[pl.ds(0, 3)]), (flow_from, flow_in),
        ))
    ]
    for load in loads:
        load.start()
    zi, zp = z_peers(y, zl, x, core, gas)
    pi, pp = plane_peers(y, zl, x, core, gas)
    partner = (star_of(y, zl, x, 1 - core), gas)
    sides = []
    for dx in (-1, 0, 1):
        for dy in (-1, 0, 1):
            if dx or dy:
                device = (lax.rem(star + dx + TILES, TILES), lax.rem(gas + dy + GAS, GAS))
                sides.append((dx, dy, device))
    arrived = meet(
        [p[-1] for p in zp] + [p[-1] for p in pp] + [p[-1] for p in sides] + [partner]
    )
    for load in loads[:5]:
        load.wait()
    old_acc, old_jerk = accel[0:3, :], accel[3:6, :]
    v = vel[...]
    res[0:3, :] = (
        pos[...] + time_step * v + time_step**2 / 2.0 * old_acc + time_step**3 / 6.0 * old_jerk
    )
    res[3:6, :] = v + time_step * old_acc + time_step**2 / 2.0 * old_jerk
    res[6:7, :] = mass[...]
    res[7:8, :] = jnp.zeros((1, STARS), f32)
    local, used = own_indices(active, star * GAS + gas, gas * SLOTS)
    block, lane = local >> 7, local & 127
    packed = jnp.zeros((8, 128), f32)
    for b in range(STARS // 128):
        packed = jnp.where(
            used & (block == b), take_lanes(res[:, b * 128 : (b + 1) * 128], lane), packed
        )
    own[...] = packed
    zbuf[zi] = packed
    arrived()
    zc = [
        send(own, zbuf.at[zi], zs.at[d], zr.at[d], device)
        for d, (ozl, device) in enumerate(zp)
    ]

    lane8 = lanes()
    edge0 = (lanes((128, 128)) * STARS).astype(f32)
    edge1 = edge0 + 128.0 * STARS
    count0 = jnp.zeros((8, 128), f32)
    count1 = jnp.zeros((8, 128), f32)
    for b in range(BLOCKS):
        row = jnp.broadcast_to(active[b : b + 1, :].astype(f32), (128, 128))
        col = jnp.transpose(row)
        less0 = jnp.where(col < edge0, 1.0, 0.0).reshape(16, 8, 128)
        less1 = jnp.where(col < edge1, 1.0, 0.0).reshape(16, 8, 128)
        count0 = count0 + jnp.sum(less0, 0)
        count1 = count1 + jnp.sum(less1, 0)
    begin0 = jnp.broadcast_to(jnp.sum(count0, 0, keepdims=True).astype(i32), (8, 128))
    begin1 = jnp.broadcast_to(jnp.sum(count1, 0, keepdims=True).astype(i32), (8, 128))
    steps = jnp.zeros((8, 128), f32)
    for half, begin in enumerate((begin0, begin1)):
        owner = lane8 + half * 128
        leaves = (owner >> 2) - 1 + (begin >> 7)
        leaves = jnp.where(((owner & 3) == 0) & (owner > 0), leaves, 1000).astype(f32)
        col = jnp.transpose(jnp.broadcast_to(leaves[0:1], (128, 128)))
        past = jnp.where(col < lanes((128, 128)).astype(f32), 1.0, 0.0).reshape(16, 8, 128)
        steps = steps + jnp.sum(past, 0)
    tile_of = jnp.sum(steps, 0, keepdims=True)
    whole = jnp.clip(tile_of.astype(i32), 0, TILES - 1)
    table[0:1, :] = jnp.clip(begin0[0:1] >> 7, 0, BLOCKS - 1)
    table[1:2, :] = jnp.clip(begin1[0:1] >> 7, 0, BLOCKS - 1)
    table[2:3, :] = seat(whole)
    table[3:4, :] = jnp.clip(lanes((1, 128)) - whole, 0, BLOCKS - 1)
    in_block = lanes((1, 128)).astype(f32) - tile_of
    in_block = jnp.where(lanes((1, 128)) < PATH, in_block, 1000.0)
    col = jnp.transpose(jnp.broadcast_to(in_block, (128, 128)))
    past = jnp.where(col <= lanes((128, 128)).astype(f32), 1.0, 0.0).reshape(16, 8, 128)
    last = jnp.sum(jnp.sum(past, 0), 0, keepdims=True) - 1.0
    table[4:5, :] = jnp.clip(last.astype(i32), 0, PATH - 1)
    table[5:8, :] = jnp.zeros((3, 128), i32)
    to_scalars = pltpu.make_async_copy(table, table_of, ins.at[8])
    to_scalars.start()
    for b in range(BLOCKS):
        act = jnp.broadcast_to(active[b : b + 1, :], (8, 128))
        owner = act >> 9
        begin = jnp.where(
            owner < 128, take_lanes(begin0, owner & 127), take_lanes(begin1, owner & 127)
        )
        spots[b] = ((owner & (GAS - 1)) * SLOTS + b * 128 + lane8 - begin) & 127
        homes[b] = seat(owner >> 2)
    to_scalars.wait()
    for copy in zc:
        copy.wait()
    mine_at = core * HALF + pi * ZL
    for z in range(ZL):
        merged = zbuf[z * GAS]
        for g in range(1, GAS):
            merged = merged + zbuf[z * GAS + g]
        tiles[mine_at + z] = merged
    pair = pl.ds(mine_at, ZL)
    pcs = [
        send(tiles.at[pair], tiles.at[pair], ps.at[d], pr.at[d], device)
        for d, (other, device) in enumerate(pp)
    ]
    away_x = res[0:3, :] - MIDDLE
    rows8[0:3, :] = away_x
    rows8[3:6, :] = res[3:6, :]
    rows8[6:7, :] = jnp.sum(away_x * res[3:6, :], 0, keepdims=True)
    rows8[7:8, :] = jnp.sum(away_x * away_x, 0, keepdims=True)
    high, mid, low = thirds(rows8[...])
    ones = jnp.where(lax.broadcasted_iota(i32, (8, 128), 0) < 3, 1.0, 0.0)
    square[...] = jnp.zeros((128, 128), f32)
    for q in range(STARS // 128):
        at = slice(q * 128, (q + 1) * 128)
        for n, part_of in enumerate((high, high, high, mid, mid, low)):
            square[n * 8 : (n + 1) * 8, :] = part_of[:, at]
        square[48:56, :] = ones
        ls[at, :] = jnp.transpose(square[...]).astype(bf16)
    square[...] = jnp.zeros((128, 128), f32)
    gm = res[6:7, :] * gravity
    rows8[0:1, :] = gm
    rows8[1:4, :] = gm * (res[0:3, :] - MIDDLE)
    rows8[4:7, :] = gm * res[3:6, :]
    rows8[7:8, :] = jnp.zeros((1, STARS), f32)
    sm[...] = both(rows8[...])

    for copy in pcs:
        copy.wait()
    half = pl.ds(core * HALF, HALF)
    cc = send(tiles.at[half], tiles.at[half], cs.at[0], cr.at[0], partner)
    for load in loads[5:]:
        load.wait()
    x_mid = (star * NXL).astype(f32) + 0.5 * NXL
    y_mid = (gas * NYL).astype(f32) + 0.5 * NYL
    z_mid = 0.5 * NZ
    lane1 = lanes((1, 128))
    z_off = (lane1 & (NZ - 1)).astype(f32) + (0.5 - z_mid)
    rows8[4:8, :] = jnp.zeros((4, STARS), f32)
    for i in range(NXL):
        cells = twice(brick[3, i]) * gravity
        for h in range(NYL // 2):
            q, at = i * 2 + h // 2, (h % 2) * 128
            cell = jnp.where(lane1 < NZ, cells[2 * h : 2 * h + 1], cells[2 * h + 1 : 2 * h + 2])
            y_off = jnp.where(lane1 < NZ, 2 * h, 2 * h + 1).astype(f32) + (0.5 - 0.5 * NYL)
            rows8[0:1, at : at + 128] = cell
            rows8[1:2, at : at + 128] = cell * (i + 0.5 - 0.5 * NXL)
            rows8[2:3, at : at + 128] = cell * y_off
            rows8[3:4, at : at + 128] = cell * z_off
            if h % 2:
                cm[q] = both(rows8[:, 0:WIDE])

    for buffer in (wa, wb, pa, pb):
        buffer[...] = jnp.zeros((WIDE, 2 * WIDE), bf16)
    for q in range(CELL_TILES):
        kacc[q] = jnp.zeros((8, WIDE), f32)
    cc.wait()
    hcs = [
        send(brick, near.at[1 - dx, 1 - dy], hs.at[d], hr.at[d], device)
        for d, (dx, dy, device) in enumerate(sides)
    ]
    near[1, 1] = brick[...]

    now = jnp.zeros((8, 128), f32)
    for step in range(PATH - 1):
        tile = jnp.clip(table_of[2, step], 0, TILES - 1)
        at = jnp.clip(table_of[3, step], 0, BLOCKS - 1)
        now = jnp.where(homes[at] == tile, take_lanes(tiles[tile], spots[at]), now)
        seen[step] = now
    for b in range(BLOCKS):
        targ[b] = seen[jnp.clip(table_of[4, b], 0, PATH - 2)]

    def wide(p, f):
        two = jnp.concatenate([targ[2 * p, f : f + 1, :], targ[2 * p + 1, f : f + 1, :]], axis=1)
        return jnp.broadcast_to(two, (8, WIDE))

    height = lax.broadcasted_iota(i32, (NZ, WIDE), 0).astype(f32) + 0.5

    row_of = lax.broadcasted_iota(i32, (8, WIDE), 0)

    def moments(p, _):
        gm = wide(p, 6)[0:1] * gravity
        rows8[0:1, 0:WIDE] = gm
        rows8[1:2, 0:WIDE] = gm * (wide(p, 0)[0:1] - x_mid)
        rows8[2:3, 0:WIDE] = gm * (wide(p, 1)[0:1] - y_mid)
        rows8[3:4, 0:WIDE] = gm * (wide(p, 2)[0:1] - z_mid)
        tm[p] = twice(both(rows8[:, 0:WIDE]))
        block = jnp.concatenate([targ[2 * p], targ[2 * p + 1]], axis=1)
        away = jnp.where(row_of < 3, block - MIDDLE, block)
        swap = jnp.where(row_of < 3, pltpu.roll(away, 5, 0), pltpu.roll(away, 3, 0))
        apart = jnp.where(row_of < 6, -swap, jnp.where(row_of == 6, 1.0, 0.0))
        near_by = jnp.where(row_of < 3, -2.0 * away, jnp.where(row_of == 7, 1.0, 0.0))
        factors = thirds(jnp.concatenate([apart, near_by], axis=1))
        for n, k in enumerate((0, 1, 2, 0, 1, 0)):
            if n % 2 == 0:
                m = (0, 1, 2, 0, 1, 0)[n + 1]
                rt[p, n * 8 : (n + 2) * 8, :] = jnp.concatenate(
                    [factors[k], factors[m]], axis=0
                ).astype(bf16)
        first3 = row_of < 3
        self_u = jnp.sum(jnp.where(first3, away * swap, 0.0), 0, keepdims=True)
        self_d = jnp.sum(jnp.where(first3, away * away, 0.0), 0, keepdims=True) + soften
        tail = thirds(jnp.broadcast_to(jnp.concatenate([self_u, self_d], axis=1), (8, 2 * WIDE)))
        row2 = jnp.concatenate([row_of, row_of], axis=1)
        tail = jnp.where(
            row2 == 0, tail[0], jnp.where(row2 == 1, tail[1], jnp.where(row2 == 2, tail[2], 0.0))
        )
        rt[p, 48:64, :] = jnp.concatenate([tail, jnp.zeros_like(tail)], axis=0).astype(bf16)
        depth = height - jnp.broadcast_to(wide(p, 2)[0:1], (NZ, WIDE))
        dz2[p] = depth * depth
        for f in range(3):
            mom[f, p] = jnp.zeros((8, WIDE), f32)
        return 0

    lax.fori_loop(0, WIDES, moments, 0)

    x_first, y_first = x_mid - 0.5 * NXL + 0.5, y_mid - 0.5 * NYL + 0.5

    def gas_weights(step, half, w_buf):
        p, i = lax.div(step, NXL), lax.rem(step, NXL)
        dx = (x_first + i.astype(f32)) - wide(p, 0)
        dx2 = dx * dx + soften
        ty = wide(p, 1)
        for j in range(4):
            dy = (y_first + (half * 4.0 + j)) - ty
            side = dx2 + dy * dy
            side = jnp.concatenate([side, side], axis=0)
            for g in range(NZ // 16):
                inv = lax.rsqrt(side + dz2[p, g * 16 : (g + 1) * 16, :])
                here = slice(j * NZ + g * 16, j * NZ + (g + 1) * 16)
                w_buf[here, 0:WIDE], w_buf[here, WIDE:] = split(inv * inv * inv)

    def gas_sums(step, half, w_buf):
        p, i = lax.div(step, NXL), lax.rem(step, NXL)
        q = i * 2 + half
        w = w_buf[...]
        mom[2, p] += fold(dot_nn(cm[q], w[:, 0:WIDE]))
        kacc[q] += fold(dot_nt(tm[p], w))

    def gas_on(step, _):
        gas_sums(jnp.maximum(step - 1, 0), 1, wb)
        gas_weights(step, 0, wa)
        gas_sums(step, 0, wa)
        gas_weights(step, 1, wb)
        return 0

    lax.fori_loop(0, WIDES * NXL, gas_on, 0)
    gas_sums(jnp.int32(WIDES * NXL - 1), 1, wb)

    for q in range(CELL_TILES):
        i, half = q // 2, q % 2
        sums = kacc[q]
        for h in range(2):
            at = slice(h * 128, (h + 1) * 128)
            y_off = jnp.where(lane1 < NZ, 0, 1).astype(f32) + (half * 4 + h * 2 + 0.5 - 0.5 * NYL)
            none = sums[0:1, at]
            kick = (
                sums[1:2, at] - (i + 0.5 - 0.5 * NXL) * none,
                sums[2:3, at] - y_off * none,
                sums[3:4, at] - z_off * none,
            )
            for f in range(3):
                row = jnp.broadcast_to(kick[f], (8, 128))
                turned = pltpu.roll(row, NZ, 1)
                j = half * 4 + h * 2
                flow[f, i, j : j + 1, :] = (
                    flow_in[f, i, j : j + 1, :] + time_step * row[0:1, 0:NZ]
                )
                flow[f, i, j + 1 : j + 2, :] = (
                    flow_in[f, i, j + 1 : j + 2, :] + time_step * turned[0:1, 0:NZ]
                )

    wind_near[1, 1] = flow[...]
    fcs = [
        send(flow, wind_near.at[1 - dx, 1 - dy], fs.at[d], fr.at[d], device)
        for d, (dx, dy, device) in enumerate(sides)
    ]
    wb[...] = jnp.zeros((WIDE, 2 * WIDE), bf16)

    def star_weights(p, c, w_buf, p_buf):
        for m in range(WIDE // PART):
            rows = slice(c * WIDE + m * PART, c * WIDE + (m + 1) * PART)
            products = dot_nn(ls[rows, 0:64], rt[p])
            for g in range(PART // 16):
                at = slice(g * 16, (g + 1) * 16)
                inv = lax.rsqrt(products[at, WIDE:])
                inv2 = inv * inv
                w = inv2 * inv
                pull = products[at, 0:WIDE] * inv2 * w
                here = slice(m * PART + g * 16, m * PART + (g + 1) * 16)
                w_buf[here, 0:WIDE], w_buf[here, WIDE:] = split(w)
                p_buf[here, 0:WIDE], p_buf[here, WIDE:] = split(pull)

    def star_sums(p, c, w_buf, p_buf):
        lhs = sm[:, c * WIDE : (c + 1) * WIDE]
        mom[0, p] += fold(dot_nn(lhs, w_buf[...]))
        mom[1, p] += fold(dot_nn(lhs, p_buf[...]))

    def stars_on(p, _):
        star_sums(jnp.maximum(p - 1, 0), 1, wb, pb)
        star_weights(p, 0, wa, pa)
        star_sums(p, 0, wa, pa)
        star_weights(p, 1, wb, pb)
        return 0

    lax.fori_loop(0, WIDES, stars_on, 0)
    star_sums(WIDES - 1, 1, wb, pb)
    def close(p, _):
        w, pull, g = mom[0, p], 3.0 * mom[1, p], mom[2, p]
        mids = (x_mid, y_mid, z_mid)
        for f in range(3):
            at = wide(p, f)[0:1]
            acc = (w[1 + f : 2 + f] - (at - MIDDLE) * w[0:1]) + (
                g[1 + f : 2 + f] - (at - mids[f]) * g[0:1]
            )
            jerk = (w[4 + f : 5 + f] - wide(p, 3 + f)[0:1] * w[0:1]) - (
                pull[1 + f : 2 + f] - (at - MIDDLE) * pull[0:1]
            )
            for h in range(2):
                pt[2 * p + h, f : f + 1, :] = acc[:, h * 128 : (h + 1) * 128]
                pt[2 * p + h, 3 + f : 4 + f, :] = jerk[:, h * 128 : (h + 1) * 128]
        for h in range(2):
            pt[2 * p + h, 6:8, :] = jnp.zeros((2, 128), f32)
        return 0

    lax.fori_loop(0, WIDES, close, 0)

    pt[BLOCKS] = jnp.zeros((8, 128), f32)
    for t in range(TILES):
        begin = take_lanes(begin0 if t < TILES // 2 else begin1, (lane8 >> 5) + ((t * GAS) & 127))
        slot = jnp.minimum(begin + (lane8 & (SLOTS - 1)), ACTIVE - 1)
        first = jnp.clip(table_of[t // 32, (t * GAS) & 127], 0, BLOCKS - 1)
        lane = slot & 127
        part[seat(t)] = jnp.where(
            (slot >> 7) == first, take_lanes(pt[first], lane), take_lanes(pt[first + 1], lane)
        )

    away = pl.ds((1 - core) * HALF, HALF)
    cc = send(part.at[away], r1, cs2.at[0], cr2.at[0], partner)

    cc.wait()
    q1[...] = part[pl.ds(core * HALF, HALF)] + r1[...]
    pcs = [
        send(q1.at[pl.ds(other * ZL, ZL)], r2.at[pi], ps2.at[d], pr2.at[d], device)
        for d, (other, device) in enumerate(pp)
    ]
    r2[pi] = q1[pl.ds(pi * ZL, ZL)]
    local, used = own_indices(active, star * GAS + gas, 0)

    for copy in hcs:
        copy.wait()
    for copy in fcs:
        copy.wait()
    for c in range(7):
        for dx in range(3):
            for dy in range(3):
                for i in range(NXL):
                    v = near[dx, dy, c, i] if c < 4 else wind_near[dx, dy, c - 4, i]
                    big[c, dx * NXL + i, dy * NYL : (dy + 1) * NYL, :] = twice(v)
    mag = tuple(big[c] for c in range(3))
    wind = tuple(big[4 + c] for c in range(3))
    inv = lax.rsqrt(big[3])
    resist = inv * inv * inv
    first = rate_of(mag, tuple(v[1:-1] for v in wind), resist[1:-1])
    one = tuple(m[2:-2] + field_step * r for m, r in zip(mag, first))
    second = rate_of(one, tuple(v[3:-3] for v in wind), resist[3:-3])
    for c in range(3):
        out = 0.5 * (mag[c][4:-4] + one[c][2:-2] + field_step * second[c])
        field_out[c] = out[:, NYL : 2 * NYL, 0:NZ]

    for copy in pcs:
        copy.wait()
    total = r2[0]
    for n in range(1, YN * XN):
        total = total + r2[n]
    t2[...] = total
    zcs = [
        send(t2.at[ozl], r3.at[zi], zs2.at[d], zr2.at[d], device)
        for d, (ozl, device) in enumerate(zp)
    ]
    r3[zi] = t2[zl]
    for copy in zcs:
        copy.wait()
    total = r3[0]
    for n in range(1, ZL * GAS):
        total = total + r3[n]
    mine = pltpu.roll(total, lax.rem(128 - gas * SLOTS, 128), 1)
    index = lanes((8, STARS))
    sums = jnp.zeros((8, STARS), f32)
    hit = jnp.zeros((8, STARS), f32)
    for s in range(MOST):
        here = index == local[:, s : s + 1]
        sums = jnp.where(here, mine[:, s : s + 1], sums)
        hit = jnp.where(here, 1.0, hit)
    is_active = hit[0:3] > 0.5
    new_acc, new_jerk = sums[0:3], sums[3:6]
    p, v = pos[...], vel[...]
    old_acc, old_jerk = accel[0:3, :], accel[3:6, :]
    vel_one = v + time_step * (old_acc + new_acc) / 2.0 + time_step**2 * (old_jerk - new_jerk) / 12.0
    pos_one = p + time_step * (v + vel_one) / 2.0 + time_step**2 * (old_acc - new_acc) / 12.0
    star_new[0:3, :] = jnp.where(is_active, pos_one, p)
    star_new[3:6, :] = jnp.where(is_active, vel_one, v)
    star_new[6:9, :] = jnp.where(is_active, new_acc, old_acc)
    star_new[9:12, :] = jnp.where(is_active, new_jerk, old_jerk)


VM = pl.BlockSpec(memory_space=pltpu.VMEM)
ANY = pl.BlockSpec(memory_space=pltpu.HBM)
DMA = pltpu.SemaphoreType.DMA


def hand_out(star_new, flow, field_out, a, b, c):
    a[...] = star_new[...]
    b[...] = flow[...]
    c[...] = field_out[...]


def body(star_pos, star_vel, star_accel, star_mass, active, density, flow_in, field_in):
    brick = (NXL, NYL, NZ)
    zn = ZL * GAS
    plane = YN * XN
    pairs = [DMA((n,)) for n in (zn - 1, zn - 1, plane - 1, plane - 1, 1, 1)]
    star_pos, star_vel, star_accel, star_mass, active, density, flow_in, field_in = (
        pltpu.with_memory_space_constraint(v, pltpu.HBM)
        for v in (star_pos, star_vel, star_accel, star_mass.reshape(1, STARS), active.reshape(BLOCKS, 128), density, flow_in, field_in)
    )
    star_new, flow, field_out = pl.pallas_call(
        step_kernel,
        out_shape=(
            jax.ShapeDtypeStruct((12, STARS), f32),
            jax.ShapeDtypeStruct((3,) + brick, f32),
            jax.ShapeDtypeStruct((3,) + brick, f32),
        ),
        in_specs=[ANY] * 8,
        out_specs=(VM,) * 3,
        scratch_shapes=[
            pltpu.VMEM((3, STARS), f32),
            pltpu.VMEM((3, STARS), f32),
            pltpu.VMEM((6, STARS), f32),
            pltpu.VMEM((1, STARS), f32),
            pltpu.VMEM((BLOCKS, 128), i32),
            pltpu.VMEM((4,) + brick, f32),
            pltpu.VMEM((3,) + brick, f32),
            pltpu.VMEM((8, STARS), f32),
            pltpu.VMEM((8, 128), f32),
            pltpu.VMEM((zn, 8, 128), f32),
            pltpu.VMEM((TILES, 8, 128), f32),
            pltpu.VMEM((8, 128), i32),
            pltpu.SMEM((8, 128), i32),
            pltpu.VMEM((BLOCKS, 8, 128), i32),
            pltpu.VMEM((BLOCKS, 8, 128), i32),
            pltpu.VMEM((PATH, 8, 128), f32),
            pltpu.VMEM((BLOCKS, 8, 128), f32),
            pltpu.VMEM((STARS, 128), bf16),
            pltpu.VMEM((WIDES, 64, 2 * WIDE), bf16),
            pltpu.VMEM((16, STARS), bf16),
            pltpu.VMEM((CELL_TILES, 16, WIDE), bf16),
            pltpu.VMEM((WIDES, 16, 2 * WIDE), bf16),
            pltpu.VMEM((WIDES, NZ, WIDE), f32),
            pltpu.VMEM((3, WIDES, 8, WIDE), f32),
            pltpu.VMEM((CELL_TILES, 8, WIDE), f32),
            pltpu.VMEM((BLOCKS + 1, 8, 128), f32),
            pltpu.VMEM((8, STARS), f32),
            pltpu.VMEM((128, 128), f32),
            pltpu.VMEM((WIDE, 2 * WIDE), bf16),
            pltpu.VMEM((WIDE, 2 * WIDE), bf16),
            pltpu.VMEM((WIDE, 2 * WIDE), bf16),
            pltpu.VMEM((WIDE, 2 * WIDE), bf16),
            pltpu.VMEM((TILES, 8, 128), f32),
            pltpu.VMEM((3, 3, 4) + brick, f32),
            pltpu.VMEM((3, 3, 3) + brick, f32),
            pltpu.VMEM((HALF, 8, 128), f32),
            pltpu.VMEM((HALF, 8, 128), f32),
            pltpu.VMEM((plane, ZL, 8, 128), f32),
            pltpu.VMEM((ZL, 8, 128), f32),
            pltpu.VMEM((zn, 8, 128), f32),
            pltpu.VMEM((7, 3 * NXL, 3 * NYL, 128), f32),
            DMA((9,)), *pairs, DMA((8,)), DMA((8,)), DMA((8,)), DMA((8,)), *pairs,
        ],
        compiler_params=pltpu.CompilerParams(
            collective_id=0, has_side_effects=True, vmem_limit_bytes=24 << 20
        ),
        name="block_step",
    )(
        star_pos, star_vel, star_accel, star_mass,
        active, density, flow_in, field_in,
    )
    return pl.pallas_call(
        hand_out,
        out_shape=tuple(jax.ShapeDtypeStruct(v.shape, f32) for v in (star_new, flow, field_out)),
        in_specs=[VM] * 3,
        out_specs=(VM,) * 3,
        compiler_params=pltpu.CompilerParams(vmem_limit_bytes=24 << 20),
        name="hand_out",
    )(star_new, flow, field_out)


def solution(mesh):
    placed = (
        P(None, ("star", "gas")),
        P(None, ("star", "gas")),
        P(None, ("star", "gas")),
        P(("star", "gas")),
        P(),
        P("star", "gas", None),
        P(None, "star", "gas", None),
        P(None, "star", "gas", None),
    )
    return jax.shard_map(
        body,
        mesh=mesh,
        in_specs=placed,
        out_specs=(
            P(None, ("star", "gas")),
            P(None, "star", "gas", None),
            P(None, "star", "gas", None),
        ),
        check_vma=False,
    )
```

```python
import functools

import jax
import jax.numpy as jnp
from jax import lax
from jax.experimental import pallas as pl
from jax.experimental.pallas import tpu as pltpu
from jax.sharding import PartitionSpec as P

MESH = pl.DeviceIdType.MESH
gravity = 0.02
soften = 4.0
time_step = 1.5
field_step = 0.1

STARS = 512
ACTIVE = 2048
BLOCKS = ACTIVE // 128
XN, CORES, ZL, YN, GAS = 4, 2, 2, 4, 4
TILES = YN * ZL * XN * CORES
HALF = TILES // CORES
PATH = TILES + BLOCKS
SLOTS = 32
MOST = 24
NXL, NYL, NZ = 4, 8, 64
WIDE = 256
WIDES = ACTIVE // WIDE
CELL_TILES = NXL * NYL * NZ // WIDE
MIDDLE = 16.0
PART = 256
f32 = jnp.float32
bf16 = jnp.bfloat16
i32 = jnp.int32


def lanes(shape=(8, 128)):
    return lax.broadcasted_iota(i32, shape, len(shape) - 1)


def take_lanes(values, index):
    return jnp.take_along_axis(values, index, axis=1, mode="promise_in_bounds")


def place():
    star = lax.axis_index("star")
    gas = lax.axis_index("gas")
    core = lax.rem(star, CORES)
    x = lax.rem(lax.div(star, CORES), XN)
    zl = lax.rem(lax.div(star, CORES * XN), ZL)
    y = lax.div(star, CORES * XN * ZL)
    return star, gas, y, zl, x, core


def seat(star):
    return ((star & 1) << 5) | ((star >> 4) << 3) | (((star >> 1) & 3) << 1) | ((star >> 3) & 1)


def star_of(y, zl, x, core):
    return ((y * ZL + zl) * XN + x) * CORES + core


def z_peers(y, zl, x, core, gas):
    zi = zl * GAS + gas
    peers = []
    for d in range(1, ZL * GAS):
        other = lax.rem(zi + d, ZL * GAS)
        ozl, ogas = lax.div(other, GAS), lax.rem(other, GAS)
        peers.append((ozl, (star_of(y, ozl, x, core), ogas)))
    return zi, peers


def plane_peers(y, zl, x, core, gas):
    peers = []
    for dy in range(YN):
        for dx in range(XN):
            if dy or dx:
                oy, ox = lax.rem(y + dy, YN), lax.rem(x + dx, XN)
                peers.append((oy * XN + ox, (star_of(oy, zl, ox, core), gas)))
    return y * XN + x, peers


def meet(devices):
    barrier = pltpu.get_barrier_semaphore()
    for device in devices:
        pl.semaphore_signal(barrier, inc=1, device_id=device, device_id_type=MESH)
    return lambda: pl.semaphore_wait(barrier, len(devices))


def send(src, dst, send_sem, recv_sem, device):
    copy = pltpu.make_async_remote_copy(
        src_ref=src, dst_ref=dst, send_sem=send_sem, recv_sem=recv_sem,
        device_id=device, device_id_type=MESH,
    )
    copy.start()
    return copy


def own_indices(active_ref, rank, lane0):
    act = active_ref[...]
    base = rank * STARS
    begin = jnp.sum((act < base).astype(f32)).astype(i32)
    slot = lanes() - lane0
    t = begin + slot
    inside = (slot >= 0) & (slot < SLOTS) & (t < ACTIVE)
    t = jnp.where(inside, t, 0)
    block, lane = t >> 7, t & 127
    found = jnp.full((8, 128), -1, i32)
    for b in range(BLOCKS):
        row = jnp.broadcast_to(active_ref[b : b + 1, :], (8, 128))
        found = jnp.where(block == b, take_lanes(row, lane), found)
    local = found - base
    used = inside & (local >= 0) & (local < STARS)
    return jnp.where(used, local, -1), used


def split(v):
    hi = v.astype(bf16)
    return hi, (v - hi.astype(f32)).astype(bf16)


def twice(v):
    return jnp.concatenate([v, v], axis=1)


def thirds(v):
    high = v.astype(bf16).astype(f32)
    mid = (v - high).astype(bf16).astype(f32)
    return high, mid, (v - high - mid).astype(bf16).astype(f32)


def both(v):
    hi = v.astype(bf16).astype(f32)
    return jnp.concatenate([hi, v - hi], axis=0).astype(bf16)


def dot_nn(lhs, rhs):
    return jnp.dot(lhs, rhs, preferred_element_type=f32)


def dot_nt(lhs, rhs):
    return lax.dot_general(lhs, rhs, (((1,), (1,)), ((), ())), preferred_element_type=f32)


def fold(v):
    v = v[0:8] + v[8:16]
    return v[:, 0:WIDE] + v[:, WIDE:] if v.shape[1] > WIDE else v


def cross_of(lhs, rhs):
    return (
        lhs[1] * rhs[2] - lhs[2] * rhs[1],
        lhs[2] * rhs[0] - lhs[0] * rhs[2],
        lhs[0] * rhs[1] - lhs[1] * rhs[0],
    )


def diff_x(v):
    return 0.5 * (v[2:] - v[:-2])


def diff_y(v):
    n = v.shape[1]
    return (0.5 * (pltpu.roll(v, n - 1, 1) - pltpu.roll(v, 1, 1)))[1:-1]


def diff_z(v):
    n = v.shape[2]
    return (0.5 * (pltpu.roll(v, n - 1, 2) - pltpu.roll(v, 1, 2)))[1:-1]


def curl_of(a, b, c):
    return (diff_y(c) - diff_z(b), diff_z(a) - diff_x(c), diff_x(b) - diff_y(a))


def rate_of(field, flow, resist):
    current = curl_of(*field)
    inner = tuple(v[1:-1] for v in field)
    drift = cross_of(cross_of(current, inner), inner)
    motion = cross_of(flow, inner)
    emf = tuple(m + resist * d for m, d in zip(motion, drift))
    return curl_of(*emf)


def step_kernel(
    pos_in, vel_in, accel_in, mass_in, active_in, density_in, flow_from, field_in,
    star_new, flow, field_out,
    pos, vel, accel, mass, active, brick, flow_in, res, own, zbuf, tiles, table, table_of,
    spots, homes, seen, targ, ls, rt, sm, cm, tm, dz2, mom, kacc, pt, rows8, square, wa, wb, pa, pb,
    part, near, wind_near, r1, q1, r2, t2, r3, big,
    ins, zs, zr, ps, pr, cs, cr, hs, hr, fs, fr, zs2, zr2, ps2, pr2, cs2, cr2
):
    star, gas, y, zl, x, core = place()
    loads = [
        pltpu.make_async_copy(src, dst, ins.at[n])
        for n, (src, dst) in enumerate((
            (pos_in, pos), (vel_in, vel), (accel_in, accel), (mass_in, mass), (active_in, active),
            (density_in, brick.at[3]), (field_in, brick.at[pl.ds(0, 3)]), (flow_from, flow_in),
        ))
    ]
    for load in loads:
        load.start()
    zi, zp = z_peers(y, zl, x, core, gas)
    pi, pp = plane_peers(y, zl, x, core, gas)
    partner = (star_of(y, zl, x, 1 - core), gas)
    sides = []
    for dx in (-1, 0, 1):
        for dy in (-1, 0, 1):
            if dx or dy:
                device = (lax.rem(star + dx + TILES, TILES), lax.rem(gas + dy + GAS, GAS))
                sides.append((dx, dy, device))
    arrived = meet(
        [p[-1] for p in zp] + [p[-1] for p in pp] + [p[-1] for p in sides] + [partner]
    )
    for load in loads[:5]:
        load.wait()
    old_acc, old_jerk = accel[0:3, :], accel[3:6, :]
    v = vel[...]
    res[0:3, :] = (
        pos[...] + time_step * v + time_step**2 / 2.0 * old_acc + time_step**3 / 6.0 * old_jerk
    )
    res[3:6, :] = v + time_step * old_acc + time_step**2 / 2.0 * old_jerk
    res[6:7, :] = mass[...]
    res[7:8, :] = jnp.zeros((1, STARS), f32)
    local, used = own_indices(active, star * GAS + gas, gas * SLOTS)
    block, lane = local >> 7, local & 127
    packed = jnp.zeros((8, 128), f32)
    for b in range(STARS // 128):
        packed = jnp.where(
            used & (block == b), take_lanes(res[:, b * 128 : (b + 1) * 128], lane), packed
        )
    own[...] = packed
    zbuf[zi] = packed
    arrived()
    zc = [
        send(own, zbuf.at[zi], zs.at[d], zr.at[d], device)
        for d, (ozl, device) in enumerate(zp)
    ]

    lane8 = lanes()
    edge0 = (lanes((128, 128)) * STARS).astype(f32)
    edge1 = edge0 + 128.0 * STARS
    count0 = jnp.zeros((8, 128), f32)
    count1 = jnp.zeros((8, 128), f32)
    for b in range(BLOCKS):
        row = jnp.broadcast_to(active[b : b + 1, :].astype(f32), (128, 128))
        col = jnp.transpose(row)
        less0 = jnp.where(col < edge0, 1.0, 0.0).reshape(16, 8, 128)
        less1 = jnp.where(col < edge1, 1.0, 0.0).reshape(16, 8, 128)
        count0 = count0 + jnp.sum(less0, 0)
        count1 = count1 + jnp.sum(less1, 0)
    begin0 = jnp.broadcast_to(jnp.sum(count0, 0, keepdims=True).astype(i32), (8, 128))
    begin1 = jnp.broadcast_to(jnp.sum(count1, 0, keepdims=True).astype(i32), (8, 128))
    steps = jnp.zeros((8, 128), f32)
    for half, begin in enumerate((begin0, begin1)):
        owner = lane8 + half * 128
        leaves = (owner >> 2) - 1 + (begin >> 7)
        leaves = jnp.where(((owner & 3) == 0) & (owner > 0), leaves, 1000).astype(f32)
        col = jnp.transpose(jnp.broadcast_to(leaves[0:1], (128, 128)))
        past = jnp.where(col < lanes((128, 128)).astype(f32), 1.0, 0.0).reshape(16, 8, 128)
        steps = steps + jnp.sum(past, 0)
    tile_of = jnp.sum(steps, 0, keepdims=True)
    whole = jnp.clip(tile_of.astype(i32), 0, TILES - 1)
    table[0:1, :] = jnp.clip(begin0[0:1] >> 7, 0, BLOCKS - 1)
    table[1:2, :] = jnp.clip(begin1[0:1] >> 7, 0, BLOCKS - 1)
    table[2:3, :] = seat(whole)
    table[3:4, :] = jnp.clip(lanes((1, 128)) - whole, 0, BLOCKS - 1)
    in_block = lanes((1, 128)).astype(f32) - tile_of
    in_block = jnp.where(lanes((1, 128)) < PATH, in_block, 1000.0)
    col = jnp.transpose(jnp.broadcast_to(in_block, (128, 128)))
    past = jnp.where(col <= lanes((128, 128)).astype(f32), 1.0, 0.0).reshape(16, 8, 128)
    last = jnp.sum(jnp.sum(past, 0), 0, keepdims=True) - 1.0
    table[4:5, :] = jnp.clip(last.astype(i32), 0, PATH - 1)
    table[5:8, :] = jnp.zeros((3, 128), i32)
    to_scalars = pltpu.make_async_copy(table, table_of, ins.at[8])
    to_scalars.start()
    for b in range(BLOCKS):
        act = jnp.broadcast_to(active[b : b + 1, :], (8, 128))
        owner = act >> 9
        begin = jnp.where(
            owner < 128, take_lanes(begin0, owner & 127), take_lanes(begin1, owner & 127)
        )
        spots[b] = ((owner & (GAS - 1)) * SLOTS + b * 128 + lane8 - begin) & 127
        homes[b] = seat(owner >> 2)
    to_scalars.wait()
    for copy in zc:
        copy.wait()
    mine_at = core * HALF + pi * ZL
    for z in range(ZL):
        merged = zbuf[z * GAS]
        for g in range(1, GAS):
            merged = merged + zbuf[z * GAS + g]
        tiles[mine_at + z] = merged
    pair = pl.ds(mine_at, ZL)
    pcs = [
        send(tiles.at[pair], tiles.at[pair], ps.at[d], pr.at[d], device)
        for d, (other, device) in enumerate(pp)
    ]
    away_x = res[0:3, :] - MIDDLE
    rows8[0:3, :] = away_x
    rows8[3:6, :] = res[3:6, :]
    rows8[6:7, :] = jnp.sum(away_x * res[3:6, :], 0, keepdims=True)
    rows8[7:8, :] = jnp.sum(away_x * away_x, 0, keepdims=True)
    high, mid, low = thirds(rows8[...])
    ones = jnp.where(lax.broadcasted_iota(i32, (8, 128), 0) < 3, 1.0, 0.0)
    square[...] = jnp.zeros((128, 128), f32)
    for q in range(STARS // 128):
        at = slice(q * 128, (q + 1) * 128)
        for n, part_of in enumerate((high, high, high, mid, mid, low)):
            square[n * 8 : (n + 1) * 8, :] = part_of[:, at]
        square[48:56, :] = ones
        ls[at, :] = jnp.transpose(square[...]).astype(bf16)
    square[...] = jnp.zeros((128, 128), f32)
    gm = res[6:7, :] * gravity
    rows8[0:1, :] = gm
    rows8[1:4, :] = gm * (res[0:3, :] - MIDDLE)
    rows8[4:7, :] = gm * res[3:6, :]
    rows8[7:8, :] = jnp.zeros((1, STARS), f32)
    sm[...] = both(rows8[...])

    for copy in pcs:
        copy.wait()
    half = pl.ds(core * HALF, HALF)
    cc = send(tiles.at[half], tiles.at[half], cs.at[0], cr.at[0], partner)
    for load in loads[5:]:
        load.wait()
    x_mid = (star * NXL).astype(f32) + 0.5 * NXL
    y_mid = (gas * NYL).astype(f32) + 0.5 * NYL
    z_mid = 0.5 * NZ
    lane1 = lanes((1, 128))
    z_off = (lane1 & (NZ - 1)).astype(f32) + (0.5 - z_mid)
    rows8[4:8, :] = jnp.zeros((4, STARS), f32)
    for i in range(NXL):
        cells = twice(brick[3, i]) * gravity
        for h in range(NYL // 2):
            q, at = i * 2 + h // 2, (h % 2) * 128
            cell = jnp.where(lane1 < NZ, cells[2 * h : 2 * h + 1], cells[2 * h + 1 : 2 * h + 2])
            y_off = jnp.where(lane1 < NZ, 2 * h, 2 * h + 1).astype(f32) + (0.5 - 0.5 * NYL)
            rows8[0:1, at : at + 128] = cell
            rows8[1:2, at : at + 128] = cell * (i + 0.5 - 0.5 * NXL)
            rows8[2:3, at : at + 128] = cell * y_off
            rows8[3:4, at : at + 128] = cell * z_off
            if h % 2:
                cm[q] = both(rows8[:, 0:WIDE])

    for buffer in (wa, wb, pa, pb):
        buffer[...] = jnp.zeros((WIDE, 2 * WIDE), bf16)
    for q in range(CELL_TILES):
        kacc[q] = jnp.zeros((8, WIDE), f32)
    cc.wait()
    hcs = [
        send(brick, near.at[1 - dx, 1 - dy], hs.at[d], hr.at[d], device)
        for d, (dx, dy, device) in enumerate(sides)
    ]
    near[1, 1] = brick[...]

    now = jnp.zeros((8, 128), f32)
    for step in range(PATH - 1):
        tile = jnp.clip(table_of[2, step], 0, TILES - 1)
        at = jnp.clip(table_of[3, step], 0, BLOCKS - 1)
        now = jnp.where(homes[at] == tile, take_lanes(tiles[tile], spots[at]), now)
        seen[step] = now
    for b in range(BLOCKS):
        targ[b] = seen[jnp.clip(table_of[4, b], 0, PATH - 2)]

    def wide(p, f):
        two = jnp.concatenate([targ[2 * p, f : f + 1, :], targ[2 * p + 1, f : f + 1, :]], axis=1)
        return jnp.broadcast_to(two, (8, WIDE))

    height = lax.broadcasted_iota(i32, (NZ, WIDE), 0).astype(f32) + 0.5

    row_of = lax.broadcasted_iota(i32, (8, WIDE), 0)

    def moments(p, _):
        gm = wide(p, 6)[0:1] * gravity
        rows8[0:1, 0:WIDE] = gm
        rows8[1:2, 0:WIDE] = gm * (wide(p, 0)[0:1] - x_mid)
        rows8[2:3, 0:WIDE] = gm * (wide(p, 1)[0:1] - y_mid)
        rows8[3:4, 0:WIDE] = gm * (wide(p, 2)[0:1] - z_mid)
        tm[p] = twice(both(rows8[:, 0:WIDE]))
        block = jnp.concatenate([targ[2 * p], targ[2 * p + 1]], axis=1)
        away = jnp.where(row_of < 3, block - MIDDLE, block)
        swap = jnp.where(row_of < 3, pltpu.roll(away, 5, 0), pltpu.roll(away, 3, 0))
        apart = jnp.where(row_of < 6, -swap, jnp.where(row_of == 6, 1.0, 0.0))
        near_by = jnp.where(row_of < 3, -2.0 * away, jnp.where(row_of == 7, 1.0, 0.0))
        factors = thirds(jnp.concatenate([apart, near_by], axis=1))
        for n, k in enumerate((0, 1, 2, 0, 1, 0)):
            if n % 2 == 0:
                m = (0, 1, 2, 0, 1, 0)[n + 1]
                rt[p, n * 8 : (n + 2) * 8, :] = jnp.concatenate(
                    [factors[k], factors[m]], axis=0
                ).astype(bf16)
        first3 = row_of < 3
        self_u = jnp.sum(jnp.where(first3, away * swap, 0.0), 0, keepdims=True)
        self_d = jnp.sum(jnp.where(first3, away * away, 0.0), 0, keepdims=True) + soften
        tail = thirds(jnp.broadcast_to(jnp.concatenate([self_u, self_d], axis=1), (8, 2 * WIDE)))
        row2 = jnp.concatenate([row_of, row_of], axis=1)
        tail = jnp.where(
            row2 == 0, tail[0], jnp.where(row2 == 1, tail[1], jnp.where(row2 == 2, tail[2], 0.0))
        )
        rt[p, 48:64, :] = jnp.concatenate([tail, jnp.zeros_like(tail)], axis=0).astype(bf16)
        depth = height - jnp.broadcast_to(wide(p, 2)[0:1], (NZ, WIDE))
        dz2[p] = depth * depth
        for f in range(3):
            mom[f, p] = jnp.zeros((8, WIDE), f32)
        return 0

    lax.fori_loop(0, WIDES, moments, 0)

    x_first, y_first = x_mid - 0.5 * NXL + 0.5, y_mid - 0.5 * NYL + 0.5

    def gas_weights(step, half, w_buf):
        p, i = lax.div(step, NXL), lax.rem(step, NXL)
        dx = (x_first + i.astype(f32)) - wide(p, 0)
        dx2 = dx * dx + soften
        ty = wide(p, 1)
        for j in range(4):
            dy = (y_first + (half * 4.0 + j)) - ty
            side = dx2 + dy * dy
            side = jnp.concatenate([side, side], axis=0)
            for g in range(NZ // 16):
                inv = lax.rsqrt(side + dz2[p, g * 16 : (g + 1) * 16, :])
                here = slice(j * NZ + g * 16, j * NZ + (g + 1) * 16)
                w_buf[here, 0:WIDE], w_buf[here, WIDE:] = split(inv * inv * inv)

    def gas_sums(step, half, w_buf):
        p, i = lax.div(step, NXL), lax.rem(step, NXL)
        q = i * 2 + half
        w = w_buf[...]
        mom[2, p] += fold(dot_nn(cm[q], w[:, 0:WIDE]))
        kacc[q] += fold(dot_nt(tm[p], w))

    def gas_on(step, _):
        gas_sums(jnp.maximum(step - 1, 0), 1, wb)
        gas_weights(step, 0, wa)
        gas_sums(step, 0, wa)
        gas_weights(step, 1, wb)
        return 0

    lax.fori_loop(0, WIDES * NXL, gas_on, 0)
    gas_sums(jnp.int32(WIDES * NXL - 1), 1, wb)

    for q in range(CELL_TILES):
        i, half = q // 2, q % 2
        sums = kacc[q]
        for h in range(2):
            at = slice(h * 128, (h + 1) * 128)
            y_off = jnp.where(lane1 < NZ, 0, 1).astype(f32) + (half * 4 + h * 2 + 0.5 - 0.5 * NYL)
            none = sums[0:1, at]
            kick = (
                sums[1:2, at] - (i + 0.5 - 0.5 * NXL) * none,
                sums[2:3, at] - y_off * none,
                sums[3:4, at] - z_off * none,
            )
            for f in range(3):
                row = jnp.broadcast_to(kick[f], (8, 128))
                turned = pltpu.roll(row, NZ, 1)
                j = half * 4 + h * 2
                flow[f, i, j : j + 1, :] = (
                    flow_in[f, i, j : j + 1, :] + time_step * row[0:1, 0:NZ]
                )
                flow[f, i, j + 1 : j + 2, :] = (
                    flow_in[f, i, j + 1 : j + 2, :] + time_step * turned[0:1, 0:NZ]
                )

    wind_near[1, 1] = flow[...]
    fcs = [
        send(flow, wind_near.at[1 - dx, 1 - dy], fs.at[d], fr.at[d], device)
        for d, (dx, dy, device) in enumerate(sides)
    ]
    wb[...] = jnp.zeros((WIDE, 2 * WIDE), bf16)

    def star_weights(p, c, w_buf, p_buf):
        for m in range(WIDE // PART):
            rows = slice(c * WIDE + m * PART, c * WIDE + (m + 1) * PART)
            products = dot_nn(ls[rows, 0:64], rt[p])
            for g in range(PART // 16):
                at = slice(g * 16, (g + 1) * 16)
                inv = lax.rsqrt(products[at, WIDE:])
                inv2 = inv * inv
                w = inv2 * inv
                pull = products[at, 0:WIDE] * inv2 * w
                here = slice(m * PART + g * 16, m * PART + (g + 1) * 16)
                w_buf[here, 0:WIDE], w_buf[here, WIDE:] = split(w)
                p_buf[here, 0:WIDE], p_buf[here, WIDE:] = split(pull)

    def star_sums(p, c, w_buf, p_buf):
        lhs = sm[:, c * WIDE : (c + 1) * WIDE]
        mom[0, p] += fold(dot_nn(lhs, w_buf[...]))
        mom[1, p] += fold(dot_nn(lhs, p_buf[...]))

    def stars_on(p, _):
        star_sums(jnp.maximum(p - 1, 0), 1, wb, pb)
        star_weights(p, 0, wa, pa)
        star_sums(p, 0, wa, pa)
        star_weights(p, 1, wb, pb)
        return 0

    lax.fori_loop(0, WIDES, stars_on, 0)
    star_sums(WIDES - 1, 1, wb, pb)
    def close(p, _):
        w, pull, g = mom[0, p], 3.0 * mom[1, p], mom[2, p]
        mids = (x_mid, y_mid, z_mid)
        for f in range(3):
            at = wide(p, f)[0:1]
            acc = (w[1 + f : 2 + f] - (at - MIDDLE) * w[0:1]) + (
                g[1 + f : 2 + f] - (at - mids[f]) * g[0:1]
            )
            jerk = (w[4 + f : 5 + f] - wide(p, 3 + f)[0:1] * w[0:1]) - (
                pull[1 + f : 2 + f] - (at - MIDDLE) * pull[0:1]
            )
            for h in range(2):
                pt[2 * p + h, f : f + 1, :] = acc[:, h * 128 : (h + 1) * 128]
                pt[2 * p + h, 3 + f : 4 + f, :] = jerk[:, h * 128 : (h + 1) * 128]
        for h in range(2):
            pt[2 * p + h, 6:8, :] = jnp.zeros((2, 128), f32)
        return 0

    lax.fori_loop(0, WIDES, close, 0)

    pt[BLOCKS] = jnp.zeros((8, 128), f32)

    def expand(bit):
        for k in range(HALF):
            owner = (k * CORES * GAS) % 128 + bit * GAS
            half = k * CORES * GAS // 128
            begin = take_lanes(begin1 if half else begin0, (lane8 >> 5) + owner)
            slot = jnp.minimum(begin + (lane8 & (SLOTS - 1)), ACTIVE - 1)
            first = jnp.clip(table_of[half, owner], 0, BLOCKS - 1)
            lane = slot & 127
            part[bit * HALF + seat(k * CORES)] = jnp.where(
                (slot >> 7) == first, take_lanes(pt[first], lane), take_lanes(pt[first + 1], lane)
            )

    expand(1 - core)

    away = pl.ds((1 - core) * HALF, HALF)
    cc = send(part.at[away], r1, cs2.at[0], cr2.at[0], partner)
    expand(core)

    cc.wait()
    q1[...] = part[pl.ds(core * HALF, HALF)] + r1[...]
    pcs = [
        send(q1.at[pl.ds(other * ZL, ZL)], r2.at[pi], ps2.at[d], pr2.at[d], device)
        for d, (other, device) in enumerate(pp)
    ]
    r2[pi] = q1[pl.ds(pi * ZL, ZL)]
    local, used = own_indices(active, star * GAS + gas, 0)

    for copy in hcs:
        copy.wait()
    for copy in fcs:
        copy.wait()
    for c in range(7):
        for dx in range(3):
            for dy in range(3):
                for i in range(NXL):
                    v = near[dx, dy, c, i] if c < 4 else wind_near[dx, dy, c - 4, i]
                    big[c, dx * NXL + i, dy * NYL : (dy + 1) * NYL, :] = twice(v)
    mag = tuple(big[c] for c in range(3))
    wind = tuple(big[4 + c] for c in range(3))
    inv = lax.rsqrt(big[3])
    resist = inv * inv * inv
    first = rate_of(mag, tuple(v[1:-1] for v in wind), resist[1:-1])
    one = tuple(m[2:-2] + field_step * r for m, r in zip(mag, first))
    second = rate_of(one, tuple(v[3:-3] for v in wind), resist[3:-3])
    for c in range(3):
        out = 0.5 * (mag[c][4:-4] + one[c][2:-2] + field_step * second[c])
        field_out[c] = out[:, NYL : 2 * NYL, 0:NZ]

    index = lanes((8, STARS))
    source = jnp.full((8, STARS), -1, i32)
    for n in range(MOST):
        source = jnp.where(index == local[:, n : n + 1], n, source)
    is_active = source[0:3] >= 0
    source = jnp.where(source >= 0, source + gas * SLOTS, 0)
    for copy in pcs:
        copy.wait()
    total = r2[0]
    for n in range(1, YN * XN):
        total = total + r2[n]
    t2[...] = total
    zcs = [
        send(t2.at[ozl], r3.at[zi], zs2.at[d], zr2.at[d], device)
        for d, (ozl, device) in enumerate(zp)
    ]
    r3[zi] = t2[zl]
    for copy in zcs:
        copy.wait()
    total = r3[0]
    for n in range(1, ZL * GAS):
        total = total + r3[n]
    sums = jnp.concatenate(
        [take_lanes(total, source[:, b * 128 : (b + 1) * 128]) for b in range(STARS // 128)], axis=1
    )
    new_acc, new_jerk = sums[0:3], sums[3:6]
    p, v = pos[...], vel[...]
    old_acc, old_jerk = accel[0:3, :], accel[3:6, :]
    vel_one = v + time_step * (old_acc + new_acc) / 2.0 + time_step**2 * (old_jerk - new_jerk) / 12.0
    pos_one = p + time_step * (v + vel_one) / 2.0 + time_step**2 * (old_acc - new_acc) / 12.0
    star_new[0:3, :] = jnp.where(is_active, pos_one, p)
    star_new[3:6, :] = jnp.where(is_active, vel_one, v)
    star_new[6:9, :] = jnp.where(is_active, new_acc, old_acc)
    star_new[9:12, :] = jnp.where(is_active, new_jerk, old_jerk)


VM = pl.BlockSpec(memory_space=pltpu.VMEM)
ANY = pl.BlockSpec(memory_space=pltpu.HBM)
DMA = pltpu.SemaphoreType.DMA


def hand_out(star_new, flow, field_out, a, b, c):
    a[...] = star_new[...]
    b[...] = flow[...]
    c[...] = field_out[...]


def body(star_pos, star_vel, star_accel, star_mass, active, density, flow_in, field_in):
    brick = (NXL, NYL, NZ)
    zn = ZL * GAS
    plane = YN * XN
    pairs = [DMA((n,)) for n in (zn - 1, zn - 1, plane - 1, plane - 1, 1, 1)]
    star_pos, star_vel, star_accel, star_mass, active, density, flow_in, field_in = (
        pltpu.with_memory_space_constraint(v, pltpu.HBM)
        for v in (star_pos, star_vel, star_accel, star_mass.reshape(1, STARS), active.reshape(BLOCKS, 128), density, flow_in, field_in)
    )
    star_new, flow, field_out = pl.pallas_call(
        step_kernel,
        out_shape=(
            jax.ShapeDtypeStruct((12, STARS), f32),
            jax.ShapeDtypeStruct((3,) + brick, f32),
            jax.ShapeDtypeStruct((3,) + brick, f32),
        ),
        in_specs=[ANY] * 8,
        out_specs=(VM,) * 3,
        scratch_shapes=[
            pltpu.VMEM((3, STARS), f32),
            pltpu.VMEM((3, STARS), f32),
            pltpu.VMEM((6, STARS), f32),
            pltpu.VMEM((1, STARS), f32),
            pltpu.VMEM((BLOCKS, 128), i32),
            pltpu.VMEM((4,) + brick, f32),
            pltpu.VMEM((3,) + brick, f32),
            pltpu.VMEM((8, STARS), f32),
            pltpu.VMEM((8, 128), f32),
            pltpu.VMEM((zn, 8, 128), f32),
            pltpu.VMEM((TILES, 8, 128), f32),
            pltpu.VMEM((8, 128), i32),
            pltpu.SMEM((8, 128), i32),
            pltpu.VMEM((BLOCKS, 8, 128), i32),
            pltpu.VMEM((BLOCKS, 8, 128), i32),
            pltpu.VMEM((PATH, 8, 128), f32),
            pltpu.VMEM((BLOCKS, 8, 128), f32),
            pltpu.VMEM((STARS, 128), bf16),
            pltpu.VMEM((WIDES, 64, 2 * WIDE), bf16),
            pltpu.VMEM((16, STARS), bf16),
            pltpu.VMEM((CELL_TILES, 16, WIDE), bf16),
            pltpu.VMEM((WIDES, 16, 2 * WIDE), bf16),
            pltpu.VMEM((WIDES, NZ, WIDE), f32),
            pltpu.VMEM((3, WIDES, 8, WIDE), f32),
            pltpu.VMEM((CELL_TILES, 8, WIDE), f32),
            pltpu.VMEM((BLOCKS + 1, 8, 128), f32),
            pltpu.VMEM((8, STARS), f32),
            pltpu.VMEM((128, 128), f32),
            pltpu.VMEM((WIDE, 2 * WIDE), bf16),
            pltpu.VMEM((WIDE, 2 * WIDE), bf16),
            pltpu.VMEM((WIDE, 2 * WIDE), bf16),
            pltpu.VMEM((WIDE, 2 * WIDE), bf16),
            pltpu.VMEM((TILES, 8, 128), f32),
            pltpu.VMEM((3, 3, 4) + brick, f32),
            pltpu.VMEM((3, 3, 3) + brick, f32),
            pltpu.VMEM((HALF, 8, 128), f32),
            pltpu.VMEM((HALF, 8, 128), f32),
            pltpu.VMEM((plane, ZL, 8, 128), f32),
            pltpu.VMEM((ZL, 8, 128), f32),
            pltpu.VMEM((zn, 8, 128), f32),
            pltpu.VMEM((7, 3 * NXL, 3 * NYL, 128), f32),
            DMA((9,)), *pairs, DMA((8,)), DMA((8,)), DMA((8,)), DMA((8,)), *pairs,
        ],
        compiler_params=pltpu.CompilerParams(
            collective_id=0, has_side_effects=True, vmem_limit_bytes=24 << 20
        ),
        name="block_step",
    )(
        star_pos, star_vel, star_accel, star_mass,
        active, density, flow_in, field_in,
    )
    return pl.pallas_call(
        hand_out,
        out_shape=tuple(jax.ShapeDtypeStruct(v.shape, f32) for v in (star_new, flow, field_out)),
        in_specs=[VM] * 3,
        out_specs=(VM,) * 3,
        compiler_params=pltpu.CompilerParams(vmem_limit_bytes=24 << 20),
        name="hand_out",
    )(star_new, flow, field_out)


def solution(mesh):
    placed = (
        P(None, ("star", "gas")),
        P(None, ("star", "gas")),
        P(None, ("star", "gas")),
        P(("star", "gas")),
        P(),
        P("star", "gas", None),
        P(None, "star", "gas", None),
        P(None, "star", "gas", None),
    )
    return jax.shard_map(
        body,
        mesh=mesh,
        in_specs=placed,
        out_specs=(
            P(None, ("star", "gas")),
            P(None, "star", "gas", None),
            P(None, "star", "gas", None),
        ),
        check_vma=False,
    )
```

```python
import functools

import jax
import jax.numpy as jnp
from jax import lax
from jax.experimental import pallas as pl
from jax.experimental.pallas import tpu as pltpu
from jax.sharding import PartitionSpec as P

MESH = pl.DeviceIdType.MESH
gravity = 0.02
soften = 4.0
time_step = 1.5
field_step = 0.1

STARS = 512
ACTIVE = 2048
BLOCKS = ACTIVE // 128
XN, CORES, ZL, YN, GAS = 4, 2, 2, 4, 4
TILES = YN * ZL * XN * CORES
HALF = TILES // CORES
PATH = TILES + BLOCKS
SLOTS = 32
MOST = 24
NXL, NYL, NZ = 4, 8, 64
WIDE = 256
WIDES = ACTIVE // WIDE
CELL_TILES = NXL * NYL * NZ // WIDE
MIDDLE = 16.0
PART = 256
f32 = jnp.float32
bf16 = jnp.bfloat16
i32 = jnp.int32


def lanes(shape=(8, 128)):
    return lax.broadcasted_iota(i32, shape, len(shape) - 1)


def take_lanes(values, index):
    return jnp.take_along_axis(values, index, axis=1, mode="promise_in_bounds")


def place():
    star = lax.axis_index("star")
    gas = lax.axis_index("gas")
    core = lax.rem(star, CORES)
    x = lax.rem(lax.div(star, CORES), XN)
    zl = lax.rem(lax.div(star, CORES * XN), ZL)
    y = lax.div(star, CORES * XN * ZL)
    return star, gas, y, zl, x, core


def seat(star):
    return ((star & 1) << 5) | ((star >> 4) << 3) | (((star >> 1) & 3) << 1) | ((star >> 3) & 1)


def star_of(y, zl, x, core):
    return ((y * ZL + zl) * XN + x) * CORES + core


def z_peers(y, zl, x, core, gas):
    zi = zl * GAS + gas
    peers = []
    z, n = gas * ZL + zl, ZL * GAS
    for d in sorted(range(1, n), key=lambda d: -min(d, n - d)):
        other = lax.rem(z + d, n)
        ozl, ogas = lax.rem(other, ZL), lax.div(other, ZL)
        peers.append((ozl, (star_of(y, ozl, x, core), ogas)))
    return zi, peers


def plane_peers(y, zl, x, core, gas):
    peers = []
    steps = [(dy, dx) for dy in range(YN) for dx in range(XN) if dy or dx]
    steps.sort(key=lambda s: -min(s[0], YN - s[0]) - min(s[1], XN - s[1]))
    for dy, dx in steps:
        oy, ox = lax.rem(y + dy, YN), lax.rem(x + dx, XN)
        peers.append((oy * XN + ox, (star_of(oy, zl, ox, core), gas)))
    return y * XN + x, peers


def meet(devices):
    barrier = pltpu.get_barrier_semaphore()
    for device in devices:
        pl.semaphore_signal(barrier, inc=1, device_id=device, device_id_type=MESH)
    return lambda: pl.semaphore_wait(barrier, len(devices))


def send(src, dst, send_sem, recv_sem, device):
    copy = pltpu.make_async_remote_copy(
        src_ref=src, dst_ref=dst, send_sem=send_sem, recv_sem=recv_sem,
        device_id=device, device_id_type=MESH,
    )
    copy.start()
    return copy


def own_indices(active_ref, rank, lane0):
    act = active_ref[...]
    base = rank * STARS
    begin = jnp.sum((act < base).astype(f32)).astype(i32)
    slot = lanes() - lane0
    t = begin + slot
    inside = (slot >= 0) & (slot < SLOTS) & (t < ACTIVE)
    t = jnp.where(inside, t, 0)
    block, lane = t >> 7, t & 127
    found = jnp.full((8, 128), -1, i32)
    for b in range(BLOCKS):
        row = jnp.broadcast_to(active_ref[b : b + 1, :], (8, 128))
        found = jnp.where(block == b, take_lanes(row, lane), found)
    local = found - base
    used = inside & (local >= 0) & (local < STARS)
    return jnp.where(used, local, -1), used


def split(v):
    hi = v.astype(bf16)
    return hi, (v - hi.astype(f32)).astype(bf16)


def twice(v):
    return jnp.concatenate([v, v], axis=1)


def thirds(v):
    high = v.astype(bf16).astype(f32)
    mid = (v - high).astype(bf16).astype(f32)
    return high, mid, (v - high - mid).astype(bf16).astype(f32)


def both(v):
    hi = v.astype(bf16).astype(f32)
    return jnp.concatenate([hi, v - hi], axis=0).astype(bf16)


def dot_nn(lhs, rhs):
    return jnp.dot(lhs, rhs, preferred_element_type=f32)


def dot_nt(lhs, rhs):
    return lax.dot_general(lhs, rhs, (((1,), (1,)), ((), ())), preferred_element_type=f32)


def fold(v):
    v = v[0:8] + v[8:16]
    return v[:, 0:WIDE] + v[:, WIDE:] if v.shape[1] > WIDE else v


def cross_of(lhs, rhs):
    return (
        lhs[1] * rhs[2] - lhs[2] * rhs[1],
        lhs[2] * rhs[0] - lhs[0] * rhs[2],
        lhs[0] * rhs[1] - lhs[1] * rhs[0],
    )


def diff_x(v):
    return 0.5 * (v[2:] - v[:-2])


def diff_y(v):
    n = v.shape[1]
    return (0.5 * (pltpu.roll(v, n - 1, 1) - pltpu.roll(v, 1, 1)))[1:-1]


def diff_z(v):
    n = v.shape[2]
    return (0.5 * (pltpu.roll(v, n - 1, 2) - pltpu.roll(v, 1, 2)))[1:-1]


def curl_of(a, b, c):
    return (diff_y(c) - diff_z(b), diff_z(a) - diff_x(c), diff_x(b) - diff_y(a))


def rate_of(field, flow, resist):
    current = curl_of(*field)
    inner = tuple(v[1:-1] for v in field)
    drift = cross_of(cross_of(current, inner), inner)
    motion = cross_of(flow, inner)
    emf = tuple(m + resist * d for m, d in zip(motion, drift))
    return curl_of(*emf)


def step_kernel(
    pos_in, vel_in, accel_in, mass_in, active_in, density_in, flow_from, field_in,
    star_new, flow, field_out,
    pos, vel, accel, mass, active, brick, flow_in, res, own, zbuf, tiles, table, table_of,
    spots, homes, seen, targ, ls, rt, sm, cm, tm, dz2, mom, kacc, pt, rows8, square, wa, wb, pa, pb,
    part, near, wind_near, r1, q1, r2, t2, r3, big,
    ins, zs, zr, ps, pr, cs, cr, hs, hr, fs, fr, zs2, zr2, ps2, pr2, cs2, cr2
):
    star, gas, y, zl, x, core = place()
    loads = [
        pltpu.make_async_copy(src, dst, ins.at[n])
        for n, (src, dst) in enumerate((
            (pos_in, pos), (vel_in, vel), (accel_in, accel), (mass_in, mass), (active_in, active),
            (density_in, brick.at[3]), (field_in, brick.at[pl.ds(0, 3)]), (flow_from, flow_in),
        ))
    ]
    for load in loads:
        load.start()
    zi, zp = z_peers(y, zl, x, core, gas)
    pi, pp = plane_peers(y, zl, x, core, gas)
    partner = (star_of(y, zl, x, 1 - core), gas)
    sides = []
    for dx in (-1, 0, 1):
        for dy in (-1, 0, 1):
            if dx or dy:
                device = (lax.rem(star + dx + TILES, TILES), lax.rem(gas + dy + GAS, GAS))
                sides.append((dx, dy, device))
    arrived = meet(
        [p[-1] for p in zp] + [p[-1] for p in pp] + [p[-1] for p in sides] + [partner]
    )
    for load in loads[:5]:
        load.wait()
    old_acc, old_jerk = accel[0:3, :], accel[3:6, :]
    v = vel[...]
    res[0:3, :] = (
        pos[...] + time_step * v + time_step**2 / 2.0 * old_acc + time_step**3 / 6.0 * old_jerk
    )
    res[3:6, :] = v + time_step * old_acc + time_step**2 / 2.0 * old_jerk
    res[6:7, :] = mass[...]
    res[7:8, :] = jnp.zeros((1, STARS), f32)
    local, used = own_indices(active, star * GAS + gas, gas * SLOTS)
    block, lane = local >> 7, local & 127
    packed = jnp.zeros((8, 128), f32)
    for b in range(STARS // 128):
        packed = jnp.where(
            used & (block == b), take_lanes(res[:, b * 128 : (b + 1) * 128], lane), packed
        )
    own[...] = packed
    zbuf[zi] = packed
    arrived()
    zc = [
        send(own, zbuf.at[zi], zs.at[d], zr.at[d], device)
        for d, (ozl, device) in enumerate(zp)
    ]

    lane8 = lanes()
    edge0 = (lanes((128, 128)) * STARS).astype(f32)
    edge1 = edge0 + 128.0 * STARS
    count0 = jnp.zeros((8, 128), f32)
    count1 = jnp.zeros((8, 128), f32)
    for b in range(BLOCKS):
        row = jnp.broadcast_to(active[b : b + 1, :].astype(f32), (128, 128))
        col = jnp.transpose(row)
        less0 = jnp.where(col < edge0, 1.0, 0.0).reshape(16, 8, 128)
        less1 = jnp.where(col < edge1, 1.0, 0.0).reshape(16, 8, 128)
        count0 = count0 + jnp.sum(less0, 0)
        count1 = count1 + jnp.sum(less1, 0)
    begin0 = jnp.broadcast_to(jnp.sum(count0, 0, keepdims=True).astype(i32), (8, 128))
    begin1 = jnp.broadcast_to(jnp.sum(count1, 0, keepdims=True).astype(i32), (8, 128))
    steps = jnp.zeros((8, 128), f32)
    for half, begin in enumerate((begin0, begin1)):
        owner = lane8 + half * 128
        leaves = (owner >> 2) - 1 + (begin >> 7)
        leaves = jnp.where(((owner & 3) == 0) & (owner > 0), leaves, 1000).astype(f32)
        col = jnp.transpose(jnp.broadcast_to(leaves[0:1], (128, 128)))
        past = jnp.where(col < lanes((128, 128)).astype(f32), 1.0, 0.0).reshape(16, 8, 128)
        steps = steps + jnp.sum(past, 0)
    tile_of = jnp.sum(steps, 0, keepdims=True)
    whole = jnp.clip(tile_of.astype(i32), 0, TILES - 1)
    table[0:1, :] = jnp.clip(begin0[0:1] >> 7, 0, BLOCKS - 1)
    table[1:2, :] = jnp.clip(begin1[0:1] >> 7, 0, BLOCKS - 1)
    table[2:3, :] = seat(whole)
    table[3:4, :] = jnp.clip(lanes((1, 128)) - whole, 0, BLOCKS - 1)
    in_block = lanes((1, 128)).astype(f32) - tile_of
    in_block = jnp.where(lanes((1, 128)) < PATH, in_block, 1000.0)
    col = jnp.transpose(jnp.broadcast_to(in_block, (128, 128)))
    past = jnp.where(col <= lanes((128, 128)).astype(f32), 1.0, 0.0).reshape(16, 8, 128)
    last = jnp.sum(jnp.sum(past, 0), 0, keepdims=True) - 1.0
    table[4:5, :] = jnp.clip(last.astype(i32), 0, PATH - 1)
    table[5:8, :] = jnp.zeros((3, 128), i32)
    to_scalars = pltpu.make_async_copy(table, table_of, ins.at[8])
    to_scalars.start()
    for b in range(BLOCKS):
        act = jnp.broadcast_to(active[b : b + 1, :], (8, 128))
        owner = act >> 9
        begin = jnp.where(
            owner < 128, take_lanes(begin0, owner & 127), take_lanes(begin1, owner & 127)
        )
        spots[b] = ((owner & (GAS - 1)) * SLOTS + b * 128 + lane8 - begin) & 127
        homes[b] = seat(owner >> 2)
    to_scalars.wait()
    for copy in zc:
        copy.wait()
    mine_at = core * HALF + pi * ZL
    for z in range(ZL):
        merged = zbuf[z * GAS]
        for g in range(1, GAS):
            merged = merged + zbuf[z * GAS + g]
        tiles[mine_at + z] = merged
    pair = pl.ds(mine_at, ZL)
    pcs = [
        send(tiles.at[pair], tiles.at[pair], ps.at[d], pr.at[d], device)
        for d, (other, device) in enumerate(pp)
    ]
    away_x = res[0:3, :] - MIDDLE
    rows8[0:3, :] = away_x
    rows8[3:6, :] = res[3:6, :]
    rows8[6:7, :] = jnp.sum(away_x * res[3:6, :], 0, keepdims=True)
    rows8[7:8, :] = jnp.sum(away_x * away_x, 0, keepdims=True)
    high, mid, low = thirds(rows8[...])
    ones = jnp.where(lax.broadcasted_iota(i32, (8, 128), 0) < 3, 1.0, 0.0)
    square[...] = jnp.zeros((128, 128), f32)
    for q in range(STARS // 128):
        at = slice(q * 128, (q + 1) * 128)
        for n, part_of in enumerate((high, high, high, mid, mid, low)):
            square[n * 8 : (n + 1) * 8, :] = part_of[:, at]
        square[48:56, :] = ones
        ls[at, :] = jnp.transpose(square[...]).astype(bf16)
    square[...] = jnp.zeros((128, 128), f32)
    gm = res[6:7, :] * gravity
    rows8[0:1, :] = gm
    rows8[1:4, :] = gm * (res[0:3, :] - MIDDLE)
    rows8[4:7, :] = gm * res[3:6, :]
    rows8[7:8, :] = jnp.zeros((1, STARS), f32)
    sm[...] = both(rows8[...])

    for copy in pcs:
        copy.wait()
    half = pl.ds(core * HALF, HALF)
    cc = send(tiles.at[half], tiles.at[half], cs.at[0], cr.at[0], partner)
    for load in loads[5:]:
        load.wait()
    x_mid = (star * NXL).astype(f32) + 0.5 * NXL
    y_mid = (gas * NYL).astype(f32) + 0.5 * NYL
    z_mid = 0.5 * NZ
    lane1 = lanes((1, 128))
    z_off = (lane1 & (NZ - 1)).astype(f32) + (0.5 - z_mid)
    rows8[4:8, :] = jnp.zeros((4, STARS), f32)
    for i in range(NXL):
        cells = twice(brick[3, i]) * gravity
        for h in range(NYL // 2):
            q, at = i * 2 + h // 2, (h % 2) * 128
            cell = jnp.where(lane1 < NZ, cells[2 * h : 2 * h + 1], cells[2 * h + 1 : 2 * h + 2])
            y_off = jnp.where(lane1 < NZ, 2 * h, 2 * h + 1).astype(f32) + (0.5 - 0.5 * NYL)
            rows8[0:1, at : at + 128] = cell
            rows8[1:2, at : at + 128] = cell * (i + 0.5 - 0.5 * NXL)
            rows8[2:3, at : at + 128] = cell * y_off
            rows8[3:4, at : at + 128] = cell * z_off
            if h % 2:
                cm[q] = both(rows8[:, 0:WIDE])

    for buffer in (wa, wb, pa, pb):
        buffer[...] = jnp.zeros((WIDE, 2 * WIDE), bf16)
    for q in range(CELL_TILES):
        kacc[q] = jnp.zeros((8, WIDE), f32)
    cc.wait()
    hcs = [
        send(brick, near.at[1 - dx, 1 - dy], hs.at[d], hr.at[d], device)
        for d, (dx, dy, device) in enumerate(sides)
    ]
    near[1, 1] = brick[...]

    now = jnp.zeros((8, 128), f32)
    for step in range(PATH - 1):
        tile = jnp.clip(table_of[2, step], 0, TILES - 1)
        at = jnp.clip(table_of[3, step], 0, BLOCKS - 1)
        now = jnp.where(homes[at] == tile, take_lanes(tiles[tile], spots[at]), now)
        seen[step] = now
    for b in range(BLOCKS):
        targ[b] = seen[jnp.clip(table_of[4, b], 0, PATH - 2)]

    def wide(p, f):
        two = jnp.concatenate([targ[2 * p, f : f + 1, :], targ[2 * p + 1, f : f + 1, :]], axis=1)
        return jnp.broadcast_to(two, (8, WIDE))

    height = lax.broadcasted_iota(i32, (NZ, WIDE), 0).astype(f32) + 0.5

    row_of = lax.broadcasted_iota(i32, (8, WIDE), 0)

    def moments(p, _):
        gm = wide(p, 6)[0:1] * gravity
        rows8[0:1, 0:WIDE] = gm
        rows8[1:2, 0:WIDE] = gm * (wide(p, 0)[0:1] - x_mid)
        rows8[2:3, 0:WIDE] = gm * (wide(p, 1)[0:1] - y_mid)
        rows8[3:4, 0:WIDE] = gm * (wide(p, 2)[0:1] - z_mid)
        tm[p] = twice(both(rows8[:, 0:WIDE]))
        block = jnp.concatenate([targ[2 * p], targ[2 * p + 1]], axis=1)
        away = jnp.where(row_of < 3, block - MIDDLE, block)
        swap = jnp.where(row_of < 3, pltpu.roll(away, 5, 0), pltpu.roll(away, 3, 0))
        apart = jnp.where(row_of < 6, -swap, jnp.where(row_of == 6, 1.0, 0.0))
        near_by = jnp.where(row_of < 3, -2.0 * away, jnp.where(row_of == 7, 1.0, 0.0))
        factors = thirds(jnp.concatenate([apart, near_by], axis=1))
        for n, k in enumerate((0, 1, 2, 0, 1, 0)):
            if n % 2 == 0:
                m = (0, 1, 2, 0, 1, 0)[n + 1]
                rt[p, n * 8 : (n + 2) * 8, :] = jnp.concatenate(
                    [factors[k], factors[m]], axis=0
                ).astype(bf16)
        first3 = row_of < 3
        self_u = jnp.sum(jnp.where(first3, away * swap, 0.0), 0, keepdims=True)
        self_d = jnp.sum(jnp.where(first3, away * away, 0.0), 0, keepdims=True) + soften
        tail = thirds(jnp.broadcast_to(jnp.concatenate([self_u, self_d], axis=1), (8, 2 * WIDE)))
        row2 = jnp.concatenate([row_of, row_of], axis=1)
        tail = jnp.where(
            row2 == 0, tail[0], jnp.where(row2 == 1, tail[1], jnp.where(row2 == 2, tail[2], 0.0))
        )
        rt[p, 48:64, :] = jnp.concatenate([tail, jnp.zeros_like(tail)], axis=0).astype(bf16)
        depth = height - jnp.broadcast_to(wide(p, 2)[0:1], (NZ, WIDE))
        dz2[p] = depth * depth
        for f in range(3):
            mom[f, p] = jnp.zeros((8, WIDE), f32)
        return 0

    lax.fori_loop(0, WIDES, moments, 0)

    x_first, y_first = x_mid - 0.5 * NXL + 0.5, y_mid - 0.5 * NYL + 0.5

    def gas_weights(step, half, w_buf):
        p, i = lax.div(step, NXL), lax.rem(step, NXL)
        dx = (x_first + i.astype(f32)) - wide(p, 0)
        dx2 = dx * dx + soften
        ty = wide(p, 1)
        for j in range(4):
            dy = (y_first + (half * 4.0 + j)) - ty
            side = dx2 + dy * dy
            side = jnp.concatenate([side, side], axis=0)
            for g in range(NZ // 16):
                inv = lax.rsqrt(side + dz2[p, g * 16 : (g + 1) * 16, :])
                here = slice(j * NZ + g * 16, j * NZ + (g + 1) * 16)
                w_buf[here, 0:WIDE], w_buf[here, WIDE:] = split(inv * inv * inv)

    def gas_sums(step, half, w_buf):
        p, i = lax.div(step, NXL), lax.rem(step, NXL)
        q = i * 2 + half
        w = w_buf[...]
        mom[2, p] += fold(dot_nn(cm[q], w[:, 0:WIDE]))
        kacc[q] += fold(dot_nt(tm[p], w))

    def gas_on(step, _):
        gas_sums(jnp.maximum(step - 1, 0), 1, wb)
        gas_weights(step, 0, wa)
        gas_sums(step, 0, wa)
        gas_weights(step, 1, wb)
        return 0

    lax.fori_loop(0, WIDES * NXL, gas_on, 0)
    gas_sums(jnp.int32(WIDES * NXL - 1), 1, wb)

    for q in range(CELL_TILES):
        i, half = q // 2, q % 2
        sums = kacc[q]
        for h in range(2):
            at = slice(h * 128, (h + 1) * 128)
            y_off = jnp.where(lane1 < NZ, 0, 1).astype(f32) + (half * 4 + h * 2 + 0.5 - 0.5 * NYL)
            none = sums[0:1, at]
            kick = (
                sums[1:2, at] - (i + 0.5 - 0.5 * NXL) * none,
                sums[2:3, at] - y_off * none,
                sums[3:4, at] - z_off * none,
            )
            for f in range(3):
                row = jnp.broadcast_to(kick[f], (8, 128))
                turned = pltpu.roll(row, NZ, 1)
                j = half * 4 + h * 2
                flow[f, i, j : j + 1, :] = (
                    flow_in[f, i, j : j + 1, :] + time_step * row[0:1, 0:NZ]
                )
                flow[f, i, j + 1 : j + 2, :] = (
                    flow_in[f, i, j + 1 : j + 2, :] + time_step * turned[0:1, 0:NZ]
                )

    wind_near[1, 1] = flow[...]
    fcs = [
        send(flow, wind_near.at[1 - dx, 1 - dy], fs.at[d], fr.at[d], device)
        for d, (dx, dy, device) in enumerate(sides)
    ]
    wb[...] = jnp.zeros((WIDE, 2 * WIDE), bf16)

    def star_weights(p, c, w_buf, p_buf):
        for m in range(WIDE // PART):
            rows = slice(c * WIDE + m * PART, c * WIDE + (m + 1) * PART)
            products = dot_nn(ls[rows, 0:64], rt[p])
            for g in range(PART // 16):
                at = slice(g * 16, (g + 1) * 16)
                inv = lax.rsqrt(products[at, WIDE:])
                inv2 = inv * inv
                w = inv2 * inv
                pull = products[at, 0:WIDE] * inv2 * w
                here = slice(m * PART + g * 16, m * PART + (g + 1) * 16)
                w_buf[here, 0:WIDE], w_buf[here, WIDE:] = split(w)
                p_buf[here, 0:WIDE], p_buf[here, WIDE:] = split(pull)

    def star_sums(p, c, w_buf, p_buf):
        lhs = sm[:, c * WIDE : (c + 1) * WIDE]
        mom[0, p] += fold(dot_nn(lhs, w_buf[...]))
        mom[1, p] += fold(dot_nn(lhs, p_buf[...]))

    def stars_on(p, _):
        star_sums(jnp.maximum(p - 1, 0), 1, wb, pb)
        star_weights(p, 0, wa, pa)
        star_sums(p, 0, wa, pa)
        star_weights(p, 1, wb, pb)
        return 0

    lax.fori_loop(0, WIDES, stars_on, 0)
    star_sums(WIDES - 1, 1, wb, pb)
    def close(p, _):
        w, pull, g = mom[0, p], 3.0 * mom[1, p], mom[2, p]
        mids = (x_mid, y_mid, z_mid)
        for f in range(3):
            at = wide(p, f)[0:1]
            acc = (w[1 + f : 2 + f] - (at - MIDDLE) * w[0:1]) + (
                g[1 + f : 2 + f] - (at - mids[f]) * g[0:1]
            )
            jerk = (w[4 + f : 5 + f] - wide(p, 3 + f)[0:1] * w[0:1]) - (
                pull[1 + f : 2 + f] - (at - MIDDLE) * pull[0:1]
            )
            for h in range(2):
                pt[2 * p + h, f : f + 1, :] = acc[:, h * 128 : (h + 1) * 128]
                pt[2 * p + h, 3 + f : 4 + f, :] = jerk[:, h * 128 : (h + 1) * 128]
        for h in range(2):
            pt[2 * p + h, 6:8, :] = jnp.zeros((2, 128), f32)
        return 0

    lax.fori_loop(0, WIDES, close, 0)

    pt[BLOCKS] = jnp.zeros((8, 128), f32)

    def expand(bit):
        for k in range(HALF):
            owner = (k * CORES * GAS) % 128 + bit * GAS
            half = k * CORES * GAS // 128
            begin = take_lanes(begin1 if half else begin0, (lane8 >> 5) + owner)
            slot = jnp.minimum(begin + (lane8 & (SLOTS - 1)), ACTIVE - 1)
            first = jnp.clip(table_of[half, owner], 0, BLOCKS - 1)
            lane = slot & 127
            part[bit * HALF + seat(k * CORES)] = jnp.where(
                (slot >> 7) == first, take_lanes(pt[first], lane), take_lanes(pt[first + 1], lane)
            )

    expand(1 - core)

    away = pl.ds((1 - core) * HALF, HALF)
    cc = send(part.at[away], r1, cs2.at[0], cr2.at[0], partner)
    expand(core)

    cc.wait()
    q1[...] = part[pl.ds(core * HALF, HALF)] + r1[...]
    pcs = [
        send(q1.at[pl.ds(other * ZL, ZL)], r2.at[pi], ps2.at[d], pr2.at[d], device)
        for d, (other, device) in enumerate(pp)
    ]
    r2[pi] = q1[pl.ds(pi * ZL, ZL)]
    local, used = own_indices(active, star * GAS + gas, 0)

    for copy in hcs:
        copy.wait()
    for copy in fcs:
        copy.wait()
    for c in range(7):
        for dx in range(3):
            for dy in range(3):
                for i in range(NXL):
                    v = near[dx, dy, c, i] if c < 4 else wind_near[dx, dy, c - 4, i]
                    big[c, dx * NXL + i, dy * NYL : (dy + 1) * NYL, :] = twice(v)
    mag = tuple(big[c] for c in range(3))
    wind = tuple(big[4 + c] for c in range(3))
    inv = lax.rsqrt(big[3])
    resist = inv * inv * inv
    first = rate_of(mag, tuple(v[1:-1] for v in wind), resist[1:-1])
    one = tuple(m[2:-2] + field_step * r for m, r in zip(mag, first))
    second = rate_of(one, tuple(v[3:-3] for v in wind), resist[3:-3])
    for c in range(3):
        out = 0.5 * (mag[c][4:-4] + one[c][2:-2] + field_step * second[c])
        field_out[c] = out[:, NYL : 2 * NYL, 0:NZ]

    index = lanes((8, STARS))
    source = jnp.full((8, STARS), -1, i32)
    for n in range(MOST):
        source = jnp.where(index == local[:, n : n + 1], n, source)
    is_active = source[0:3] >= 0
    source = jnp.where(source >= 0, source + gas * SLOTS, 0)
    for copy in pcs:
        copy.wait()
    total = r2[0]
    for n in range(1, YN * XN):
        total = total + r2[n]
    t2[...] = total
    zcs = [
        send(t2.at[ozl], r3.at[zi], zs2.at[d], zr2.at[d], device)
        for d, (ozl, device) in enumerate(zp)
    ]
    r3[zi] = t2[zl]
    for copy in zcs:
        copy.wait()
    total = r3[0]
    for n in range(1, ZL * GAS):
        total = total + r3[n]
    sums = jnp.concatenate(
        [take_lanes(total, source[:, b * 128 : (b + 1) * 128]) for b in range(STARS // 128)], axis=1
    )
    new_acc, new_jerk = sums[0:3], sums[3:6]
    p, v = pos[...], vel[...]
    old_acc, old_jerk = accel[0:3, :], accel[3:6, :]
    vel_one = v + time_step * (old_acc + new_acc) / 2.0 + time_step**2 * (old_jerk - new_jerk) / 12.0
    pos_one = p + time_step * (v + vel_one) / 2.0 + time_step**2 * (old_acc - new_acc) / 12.0
    star_new[0:3, :] = jnp.where(is_active, pos_one, p)
    star_new[3:6, :] = jnp.where(is_active, vel_one, v)
    star_new[6:9, :] = jnp.where(is_active, new_acc, old_acc)
    star_new[9:12, :] = jnp.where(is_active, new_jerk, old_jerk)


VM = pl.BlockSpec(memory_space=pltpu.VMEM)
ANY = pl.BlockSpec(memory_space=pltpu.HBM)
DMA = pltpu.SemaphoreType.DMA


def hand_out(star_new, flow, field_out, a, b, c):
    a[...] = star_new[...]
    b[...] = flow[...]
    c[...] = field_out[...]


def body(star_pos, star_vel, star_accel, star_mass, active, density, flow_in, field_in):
    brick = (NXL, NYL, NZ)
    zn = ZL * GAS
    plane = YN * XN
    pairs = [DMA((n,)) for n in (zn - 1, zn - 1, plane - 1, plane - 1, 1, 1)]
    star_pos, star_vel, star_accel, star_mass, active, density, flow_in, field_in = (
        pltpu.with_memory_space_constraint(v, pltpu.HBM)
        for v in (star_pos, star_vel, star_accel, star_mass.reshape(1, STARS), active.reshape(BLOCKS, 128), density, flow_in, field_in)
    )
    star_new, flow, field_out = pl.pallas_call(
        step_kernel,
        out_shape=(
            jax.ShapeDtypeStruct((12, STARS), f32),
            jax.ShapeDtypeStruct((3,) + brick, f32),
            jax.ShapeDtypeStruct((3,) + brick, f32),
        ),
        in_specs=[ANY] * 8,
        out_specs=(VM,) * 3,
        scratch_shapes=[
            pltpu.VMEM((3, STARS), f32),
            pltpu.VMEM((3, STARS), f32),
            pltpu.VMEM((6, STARS), f32),
            pltpu.VMEM((1, STARS), f32),
            pltpu.VMEM((BLOCKS, 128), i32),
            pltpu.VMEM((4,) + brick, f32),
            pltpu.VMEM((3,) + brick, f32),
            pltpu.VMEM((8, STARS), f32),
            pltpu.VMEM((8, 128), f32),
            pltpu.VMEM((zn, 8, 128), f32),
            pltpu.VMEM((TILES, 8, 128), f32),
            pltpu.VMEM((8, 128), i32),
            pltpu.SMEM((8, 128), i32),
            pltpu.VMEM((BLOCKS, 8, 128), i32),
            pltpu.VMEM((BLOCKS, 8, 128), i32),
            pltpu.VMEM((PATH, 8, 128), f32),
            pltpu.VMEM((BLOCKS, 8, 128), f32),
            pltpu.VMEM((STARS, 128), bf16),
            pltpu.VMEM((WIDES, 64, 2 * WIDE), bf16),
            pltpu.VMEM((16, STARS), bf16),
            pltpu.VMEM((CELL_TILES, 16, WIDE), bf16),
            pltpu.VMEM((WIDES, 16, 2 * WIDE), bf16),
            pltpu.VMEM((WIDES, NZ, WIDE), f32),
            pltpu.VMEM((3, WIDES, 8, WIDE), f32),
            pltpu.VMEM((CELL_TILES, 8, WIDE), f32),
            pltpu.VMEM((BLOCKS + 1, 8, 128), f32),
            pltpu.VMEM((8, STARS), f32),
            pltpu.VMEM((128, 128), f32),
            pltpu.VMEM((WIDE, 2 * WIDE), bf16),
            pltpu.VMEM((WIDE, 2 * WIDE), bf16),
            pltpu.VMEM((WIDE, 2 * WIDE), bf16),
            pltpu.VMEM((WIDE, 2 * WIDE), bf16),
            pltpu.VMEM((TILES, 8, 128), f32),
            pltpu.VMEM((3, 3, 4) + brick, f32),
            pltpu.VMEM((3, 3, 3) + brick, f32),
            pltpu.VMEM((HALF, 8, 128), f32),
            pltpu.VMEM((HALF, 8, 128), f32),
            pltpu.VMEM((plane, ZL, 8, 128), f32),
            pltpu.VMEM((ZL, 8, 128), f32),
            pltpu.VMEM((zn, 8, 128), f32),
            pltpu.VMEM((7, 3 * NXL, 3 * NYL, 128), f32),
            DMA((9,)), *pairs, DMA((8,)), DMA((8,)), DMA((8,)), DMA((8,)), *pairs,
        ],
        compiler_params=pltpu.CompilerParams(
            collective_id=0, has_side_effects=True, vmem_limit_bytes=24 << 20
        ),
        name="block_step",
    )(
        star_pos, star_vel, star_accel, star_mass,
        active, density, flow_in, field_in,
    )
    return pl.pallas_call(
        hand_out,
        out_shape=tuple(jax.ShapeDtypeStruct(v.shape, f32) for v in (star_new, flow, field_out)),
        in_specs=[VM] * 3,
        out_specs=(VM,) * 3,
        compiler_params=pltpu.CompilerParams(vmem_limit_bytes=24 << 20),
        name="hand_out",
    )(star_new, flow, field_out)


def solution(mesh):
    placed = (
        P(None, ("star", "gas")),
        P(None, ("star", "gas")),
        P(None, ("star", "gas")),
        P(("star", "gas")),
        P(),
        P("star", "gas", None),
        P(None, "star", "gas", None),
        P(None, "star", "gas", None),
    )
    return jax.shard_map(
        body,
        mesh=mesh,
        in_specs=placed,
        out_specs=(
            P(None, ("star", "gas")),
            P(None, "star", "gas", None),
            P(None, "star", "gas", None),
        ),
        check_vma=False,
    )
```
